128 devices in a mesh: row: 8 (over x_hi, z), col: 16 (over y, x_lo, core).
Axes of the slice: x: 4 (x_hi: 2, x_lo: 2; x = x_hi * 2 + x_lo), y: 4, z: 4, core: 2. Of those that a mesh axis runs over, the one named last changes fastest.
Arguments:
- object_field: bfloat16 [2, 4096, 8192], P(None, 'row', 'col'), may hold values from -6 to 6
- probe_modes: float32 [2, 2, 256, 256], replicated, may hold values from -6 to 6
- measured_amp: bfloat16 [8, 16, 8, 256, 256], P('row', 'col'), may hold values from 0.25 to 8
- scan_positions: int32 [8, 16, 2, 8], P('row', 'col'), may hold values from 0 to 512
- frame_counts: int32 [8, 16], P('row', 'col'), may hold values from 1 to 8, as said below
Outputs:
- object_grad: float32 [2, 4096, 8192], P(None, 'row', 'col')
- probe_grad: float32 [2, 2, 256, 256], replicated
The draws below stay inside these ranges and needn't reach their ends.
Inputs may be any that keep to these rules, and one draw needn't show every extreme that they name: `frame_counts`: live frames of a tile; slots at or past it are ignored; some tile has exactly 8.
All inputs are finite; a program needn't handle non-finite values.
Results may differ from the reference program's by a relative error of at most 0.0059.
The reference program's roundings to bfloat16 on the way count: a program that leaves them out, or rounds other values in their place, can miss the bound.
Values may be sent and summed in bfloat16 or wider, within the bound.
No kernel may reach another device: no remote copies, remote signals or barrier semaphores. Data moves between devices by JAX's collectives and lax.ppermute only.
A program may use at most 64 MiB of HBM per device.

```python
import math
import jax
import jax.numpy as jnp
from jax import lax

FS = 256
MODES = 2
TILE = 512
HALO = 128
FR_MAX = 8
NR = 4096
NC = 8192
N_ROW = 8
N_COL = 16


def draw_frame_counts(key, part):
    first_key = jax.random.fold_in(key, 11)
    second_key = jax.random.fold_in(key, 12)
    third_key = jax.random.fold_in(key, 13)
    base_counts = jax.random.randint(first_key, (N_ROW * N_COL,), FR_MAX // 4 + 1, 3 * FR_MAX // 4 + 1)
    heavy = jax.random.randint(second_key, (N_ROW * N_COL,), 0, 4) == 0
    chosen = jax.random.randint(third_key, (), 0, N_ROW * N_COL)
    places = jnp.arange(N_ROW * N_COL, dtype=jnp.int32)
    counts_flat = jnp.where(heavy | (places == chosen), FR_MAX, base_counts)
    return counts_flat.reshape(N_ROW, N_COL).astype(jnp.int32)


def place_ends(drawn, rng, least, high):
    shape = drawn.shape
    place = [jax.random.randint(jax.random.fold_in(rng, axis), (), 0, shape[axis]) for axis in range(len(shape))]
    drawn = drawn.at[tuple(place)].set(least)
    longest = shape.index(max(shape))
    place[longest] = (place[longest] + 1) % shape[longest]
    return drawn.at[tuple(place)].set(high)


def block_levels(own_key, dims, split, least, top_value):
    gain, own = 1.0, jax.random.fold_in(own_key, 6)
    for dim, parts in split:
        heights = jnp.exp(jax.random.uniform(jax.random.fold_in(own, dim), (parts,), jnp.float32, least / len(split), top_value / len(split)))
        gain = gain * jnp.repeat(heights, dims[dim] // parts).reshape([-1 if axis == dim else 1 for axis in range(len(dims))])
    return gain


def scatter_about(key, shape, width, bound, cuts=(), held_as=jnp.bfloat16):
    gain = block_levels(key, shape, cuts, -0.22, 0.18) if cuts else 1.0
    entries = jax.random.normal(key, shape, jnp.float32) * width * gain
    return jnp.minimum(jnp.maximum(entries, -bound), bound).astype(held_as)


def setup_inputs(seed: int = 0) -> dict:
    seeds = jax.random.split(jax.random.key(seed), 6)
    object_field = scatter_about(seeds[0], (2, NR, NC), 1.0, 6.0, ((1, 8), (2, 16)))
    probe_modes = scatter_about(seeds[1], (2, MODES, FS, FS), 1.0, 6.0, (), jnp.float32)
    measured_amp = jnp.clip(jnp.exp(math.log(8.0) - 3.465736 * jax.random.uniform(seeds[2], (N_ROW, N_COL, FR_MAX, FS, FS), jnp.float32) ** block_levels(seeds[2], (N_ROW, N_COL, FR_MAX, FS, FS), ((0, 8), (1, 16)), -0.2, 0.2)), 0.25, 8.0).astype(jnp.bfloat16)
    scan_positions = place_ends(jax.random.randint(seeds[3], (N_ROW, N_COL, 2, FR_MAX), 0, TILE + 2 * HALO - FS + 1), jax.random.fold_in(seeds[3], 1), 0, TILE + 2 * HALO - FS).astype(jnp.int32)
    frame_counts = draw_frame_counts(jax.random.fold_in(seeds[5], 71), 0)
    return {"object_field": object_field, "probe_modes": probe_modes, "measured_amp": measured_amp, "scan_positions": scan_positions, "frame_counts": frame_counts}


def fourier_tables(frame_side):
    indices = jnp.arange(frame_side, dtype=jnp.int32)
    product = indices[:, None] * indices[None, :] % frame_side
    angles = 2.0 * math.pi / frame_side * product.astype(jnp.float32)
    norm_scale = 1.0 / math.sqrt(frame_side)
    return ((jnp.cos(angles) * norm_scale).astype(jnp.bfloat16), (-jnp.sin(angles) * norm_scale).astype(jnp.bfloat16))

def left_mul(table, data):
    return jnp.einsum('kn,mnj->mkj', table.astype(jnp.float32), data.astype(jnp.float32))

def right_mul(data, table):
    return jnp.einsum('mkn,nj->mkj', data.astype(jnp.float32), table.astype(jnp.float32))

def transform(real_part, imag_part, table_real, table_imag):
    first_real = (left_mul(table_real, real_part) - left_mul(table_imag, imag_part)).astype(jnp.bfloat16)
    first_imag = (left_mul(table_real, imag_part) + left_mul(table_imag, real_part)).astype(jnp.bfloat16)
    out_real = right_mul(first_real, table_real) - right_mul(first_imag, table_imag)
    out_imag = right_mul(first_real, table_imag) + right_mul(first_imag, table_real)
    return (out_real, out_imag)

def frame_terms(frame_patch, frame_amp, probe_modes, table_real, table_imag):
    probe_real = probe_modes[0]
    probe_imag = probe_modes[1]
    patch_real = frame_patch[0].astype(jnp.float32)
    patch_imag = frame_patch[1].astype(jnp.float32)
    exit_real = (probe_real * patch_real - probe_imag * patch_imag).astype(jnp.bfloat16)
    exit_imag = (probe_real * patch_imag + probe_imag * patch_real).astype(jnp.bfloat16)
    psi_real, psi_imag = transform(exit_real, exit_imag, table_real, table_imag)
    power = lax.optimization_barrier(jnp.sum(psi_real * psi_real + psi_imag * psi_imag, axis=0))
    factor = 1.0 - frame_amp.astype(jnp.float32) / jnp.maximum(jnp.sqrt(power), 0.5)
    chi_real = (psi_real * factor).astype(jnp.bfloat16)
    chi_imag = (psi_imag * factor).astype(jnp.bfloat16)
    back_real, back_imag = transform(chi_real, chi_imag, table_real, -table_imag)
    patch_grad = jnp.stack([lax.optimization_barrier(jnp.sum(probe_real * back_real + probe_imag * back_imag, axis=0)), lax.optimization_barrier(jnp.sum(probe_real * back_imag - probe_imag * back_real, axis=0))])
    probe_term = jnp.stack([patch_real * back_real + patch_imag * back_imag, patch_real * back_imag - patch_imag * back_real])
    return (patch_grad, probe_term)

def reference(object_field, probe_modes, measured_amp, scan_positions, frame_counts):
    table_real, table_imag = fourier_tables(FS)
    padded = jnp.pad(object_field, ((0, 0), (HALO, HALO), (HALO, HALO)))
    start_pair = (jnp.zeros(padded.shape, jnp.float32), jnp.zeros(probe_modes.shape, jnp.float32))

    def visit(position, state_pair):
        position = jnp.asarray(position).astype(jnp.int32)
        tile_row = position // (N_COL * FR_MAX)
        tile_col = position // FR_MAX % N_COL
        slot_at = position % FR_MAX

        def advance(inner_pair):
            gradient, probe_total = inner_pair
            row_at = (tile_row * TILE + scan_positions[tile_row, tile_col, 0, slot_at]).astype(jnp.int32)
            column_at = (tile_col * TILE + scan_positions[tile_row, tile_col, 1, slot_at]).astype(jnp.int32)
            zero_index = jnp.zeros((), jnp.int32)
            frame_patch = lax.dynamic_slice(padded, (zero_index, row_at, column_at), (2, FS, FS))
            patch_grad, probe_term = frame_terms(frame_patch, measured_amp[tile_row, tile_col, slot_at], probe_modes, table_real, table_imag)
            old_block = lax.dynamic_slice(gradient, (zero_index, row_at, column_at), (2, FS, FS))
            gradient = lax.dynamic_update_slice(gradient, old_block + patch_grad, (zero_index, row_at, column_at))
            return (gradient, probe_total + probe_term)
        return lax.cond(slot_at < frame_counts[tile_row, tile_col], advance, lambda unchanged: unchanged, state_pair)
    gradient, probe_total = lax.fori_loop(0, N_ROW * N_COL * FR_MAX, visit, start_pair)
    norm_scale = 1.0 / math.sqrt(N_ROW * N_COL * FR_MAX)
    return (gradient[:, HALO:HALO + N_ROW * TILE, HALO:HALO + N_COL * TILE], probe_total * norm_scale)
```

```python
import math

import jax
import jax.numpy as jnp
import numpy as np
from jax import lax
from jax.experimental import pallas as pl
from jax.experimental.pallas import tpu as pltpu
from jax.sharding import Mesh
from jax.sharding import PartitionSpec as P

HALO = 128
LANES = 128
CHUNK = 16
BF16 = jnp.bfloat16
F32 = jnp.float32
COL = ("colc", "core")
PEERS = ("row", "colc")
VM = pl.BlockSpec(memory_space=pltpu.VMEM)
SM = pl.BlockSpec(memory_space=pltpu.SMEM)


def fourier_tables(side):
    indices = np.arange(side)
    angles = 2.0 * math.pi / side * (indices[:, None] * indices[None, :] % side)
    real = jnp.asarray((np.cos(angles) / math.sqrt(side)).astype(np.float32)).astype(BF16)
    imag = jnp.asarray((-np.sin(angles) / math.sqrt(side)).astype(np.float32)).astype(BF16)
    return jnp.block([[real, -imag], [imag, real]]), jnp.block([[real, imag], [-imag, real]])


def matmul(a, b):
    return jnp.dot(a, b, preferred_element_type=F32)


def frames_kernel(
    meta_ref, pos_ref, mid_ref, row_a_ref, row_b_ref, col_a_ref, col_b_ref, probe_ref, amp_ref, lt_ref, rt_ref,
    main_ref, out_a_ref, out_b_ref, keep_ref, send_ref,
    ext, grad, pgrad, stage, firsts,
):
    side = probe_ref.shape[-1]
    modes = probe_ref.shape[1]
    tile = mid_ref.shape[1]
    nblk = tile // LANES
    count, row_odd, core = meta_ref[0], meta_ref[1], meta_ref[2]
    row_a = pl.multiple_of((1 - row_odd) * (HALO + tile), HALO)
    row_b = pl.multiple_of(row_odd * (HALO + tile), HALO)
    col_a = (1 - core) * (nblk + 1)
    col_b = core * (nblk + 1)
    for c in range(2):
        for b in range(nblk):
            cols = slice(b * LANES, (b + 1) * LANES)
            ext[c, b + 1, pl.ds(row_a, HALO), :] = row_a_ref[c, :, cols].astype(F32)
            ext[c, b + 1, HALO : HALO + tile, :] = mid_ref[c, :, cols].astype(F32)
            ext[c, b + 1, pl.ds(row_b, HALO), :] = row_b_ref[c, :, cols].astype(F32)
        ext[c, col_a] = col_a_ref[c].astype(F32)
        ext[c, col_b] = col_b_ref[c].astype(F32)
    grad[...] = jnp.zeros_like(grad)
    pgrad[...] = jnp.zeros_like(pgrad)
    lane = lax.broadcasted_iota(jnp.int32, (side, LANES), 1)

    def step(s, carry):
        row = pos_ref[0, s]
        col = pos_ref[1, s]
        cq = col // LANES
        cr = col % LANES
        back_shift = (LANES - cr) % LANES
        keep = lane < LANES - cr
        patch = []
        for c in range(2):
            rolled = [
                pltpu.roll(ext[c, jnp.minimum(cq + j, nblk + 1), pl.ds(row, side), :], back_shift, 1)
                for j in range(side // LANES + 1)
            ]
            patch.append([jnp.where(keep, rolled[j], rolled[j + 1]) for j in range(side // LANES)])
        patch_r = jnp.concatenate(patch[0], axis=1)
        patch_i = jnp.concatenate(patch[1], axis=1)
        for m in range(modes):
            pr = probe_ref[0, m]
            pi = probe_ref[1, m]
            stage[m, 0:side, :] = (pr * patch_r - pi * patch_i).astype(BF16)
            stage[m, side:, :] = (pr * patch_i + pi * patch_r).astype(BF16)
        for m in range(modes):
            f = matmul(lt_ref[...], stage[m]).astype(BF16)
            firsts[m * side : (m + 1) * side, 0:side] = f[:side]
            firsts[m * side : (m + 1) * side, side:] = f[side:]
        psi = matmul(firsts[...], rt_ref[...])
        psi_r = [psi[m * side : (m + 1) * side, :side] for m in range(modes)]
        psi_i = [psi[m * side : (m + 1) * side, side:] for m in range(modes)]
        power = sum(psi_r[m] * psi_r[m] + psi_i[m] * psi_i[m] for m in range(modes))
        factor = 1.0 - amp_ref[s].astype(F32) * lax.rsqrt(jnp.maximum(power, 0.25))
        for m in range(modes):
            stage[m, 0:side, :] = (psi_r[m] * factor).astype(BF16)
            stage[m, side:, :] = (psi_i[m] * factor).astype(BF16)
        for m in range(modes):
            f = matmul(rt_ref[...], stage[m]).astype(BF16)
            firsts[m * side : (m + 1) * side, 0:side] = f[:side]
            firsts[m * side : (m + 1) * side, side:] = f[side:]
        back = matmul(firsts[...], lt_ref[...])
        sum_r = jnp.zeros((side, side), F32)
        sum_i = jnp.zeros((side, side), F32)
        for m in range(modes):
            pr = probe_ref[0, m]
            pi = probe_ref[1, m]
            g_r = back[m * side : (m + 1) * side, :side]
            g_i = back[m * side : (m + 1) * side, side:]
            sum_r = sum_r + (pr * g_r + pi * g_i)
            sum_i = sum_i + (pr * g_i - pi * g_r)
            pgrad[0, m] += patch_r * g_r + patch_i * g_i
            pgrad[1, m] += patch_r * g_i - patch_i * g_r
        for c, v in enumerate((sum_r, sum_i)):
            parts = [pltpu.roll(v[:, j * LANES : (j + 1) * LANES], cr, 1) for j in range(side // LANES)]
            for j in range(side // LANES + 1):
                low = parts[j - 1] if j > 0 else jnp.zeros((side, LANES), F32)
                high = parts[j] if j < side // LANES else jnp.zeros((side, LANES), F32)
                grad[c, cq + j, pl.ds(row, side), :] += jnp.where(lane >= cr, high, low)
        return carry

    lax.fori_loop(0, count, step, 0)
    main_ref[...] = grad[:, 1 : nblk + 1]
    for c in range(2):
        out_a_ref[c] = grad[c, col_a].astype(BF16)
        out_b_ref[c] = grad[c, col_b].astype(BF16)
    for m in range(modes):
        for i in range(side // CHUNK):
            for j in range(side // LANES):
                k = (m * (side // CHUNK) + i) * (side // LANES) + j
                at = (slice(i * CHUNK, (i + 1) * CHUNK), slice(j * LANES, (j + 1) * LANES))
                keep_ref[k] = pgrad[core, m, at[0], at[1]]
                send_ref[k] = pgrad[1 - core, m, at[0], at[1]].astype(BF16)


def run_frames(meta, pos, mid, row_a, row_b, col_a, col_b, probe, amp, lt, rt):
    side = probe.shape[-1]
    modes = probe.shape[1]
    tile = mid.shape[1]
    nblk = tile // LANES
    rows = tile + 2 * HALO
    chunks = modes * side * side // (CHUNK * LANES)
    return pl.pallas_call(
        frames_kernel,
        out_shape=(
            jax.ShapeDtypeStruct((2, nblk, rows, LANES), F32),
            jax.ShapeDtypeStruct((2, rows, LANES), BF16),
            jax.ShapeDtypeStruct((2, rows, LANES), BF16),
            jax.ShapeDtypeStruct((chunks, CHUNK, LANES), F32),
            jax.ShapeDtypeStruct((chunks, CHUNK, LANES), BF16),
        ),
        in_specs=[SM, SM] + [VM] * 9,
        out_specs=(VM,) * 5,
        scratch_shapes=[
            pltpu.VMEM((2, nblk + 2, rows, LANES), F32),
            pltpu.VMEM((2, nblk + 3, rows, LANES), F32),
            pltpu.VMEM(probe.shape, F32),
            pltpu.VMEM((modes, 2 * side, side), BF16),
            pltpu.VMEM((modes * side, 2 * side), BF16),
        ],
        compiler_params=pltpu.CompilerParams(vmem_limit_bytes=56 * 1024 * 1024),
        name="frames",
    )(meta, pos, mid, row_a, row_b, col_a, col_b, probe, amp, lt, rt)


def row_margin_kernel(meta_ref, top_ref, bot_ref, got_a_ref, got_b_ref, out_a_ref, out_b_ref):
    nblk = top_ref.shape[1]
    row_odd, core = meta_ref[1], meta_ref[2]
    rows = got_a_ref.shape[1]

    def emit(out_ref, own_ref, start):
        for c in range(2):
            for b in range(nblk):
                out_ref[c, b] = own_ref[c, b].astype(BF16)
            for got_ref, blk in ((got_a_ref, (1 - core) * (nblk - 1)), (got_b_ref, core * (nblk - 1))):
                out_ref[c, blk] = (own_ref[c, blk] + got_ref[c, start : start + HALO, :].astype(F32)).astype(BF16)

    @pl.when(row_odd == 0)
    def _():
        emit(out_a_ref, bot_ref, rows - HALO)
        emit(out_b_ref, top_ref, 0)

    @pl.when(row_odd == 1)
    def _():
        emit(out_a_ref, top_ref, 0)
        emit(out_b_ref, bot_ref, rows - HALO)


def row_margins(meta, main, got_a, got_b):
    nblk, rows = main.shape[1], main.shape[2]
    whole = pl.BlockSpec((2, rows, LANES), lambda i: (0, 0, 0))
    shape = jax.ShapeDtypeStruct((2, nblk, HALO, LANES), BF16)
    edge = lambda at: pl.BlockSpec((2, nblk, HALO, LANES), lambda i: (0, 0, at, 0))
    out = pl.BlockSpec((2, nblk, HALO, LANES), lambda i: (0, 0, 0, 0))
    return pl.pallas_call(
        row_margin_kernel,
        grid=(1,),
        out_shape=(shape, shape),
        in_specs=[SM, edge(0), edge(rows // HALO - 1), whole, whole],
        out_specs=(out, out),
        name="row_margins",
    )(meta, main, main, got_a, got_b)


def pair_sum_kernel(keep_ref, got_ref, out_ref):
    out_ref[...] = (keep_ref[...] + got_ref[...].astype(F32)).astype(BF16)


def pair_sum(keep, got):
    return pl.pallas_call(
        pair_sum_kernel,
        out_shape=jax.ShapeDtypeStruct(keep.shape, BF16),
        in_specs=[VM, VM],
        out_specs=VM,
        name="pair_sum",
    )(keep, got)


def peer_sum_kernel(scale, got_ref, out_ref):
    total = jnp.sum(got_ref[...].astype(F32), axis=0) * scale
    out_ref[...] = jnp.broadcast_to(total.astype(BF16)[None], out_ref.shape)


def peer_sum(got, scale):
    return pl.pallas_call(
        lambda *refs: peer_sum_kernel(scale, *refs),
        out_shape=jax.ShapeDtypeStruct(got.shape, BF16),
        in_specs=[VM],
        out_specs=VM,
        name="peer_sum",
    )(got)


def object_kernel(meta_ref, main_ref, col_a_ref, col_b_ref, row_a_ref, row_b_ref, obj_ref, acc):
    nblk = main_ref.shape[1]
    tile = obj_ref.shape[1]
    row_odd, core = meta_ref[1], meta_ref[2]
    acc[...] = main_ref[:, :, HALO : HALO + tile, :]
    row_a = pl.multiple_of((1 - row_odd) * (tile - HALO), HALO)
    row_b = pl.multiple_of(row_odd * (tile - HALO), HALO)
    for c in range(2):
        acc[c, (1 - core) * (nblk - 1)] += col_a_ref[c, HALO : HALO + tile, :].astype(F32)
        acc[c, core * (nblk - 1)] += col_b_ref[c, HALO : HALO + tile, :].astype(F32)
        for b in range(nblk):
            acc[c, b, pl.ds(row_a, HALO), :] += row_a_ref[c, b].astype(F32)
            acc[c, b, pl.ds(row_b, HALO), :] += row_b_ref[c, b].astype(F32)
        for b in range(nblk):
            obj_ref[c, :, b * LANES : (b + 1) * LANES] = acc[c, b]


def finish_object(meta, main, col_a, col_b, row_a, row_b):
    nblk, rows = main.shape[1], main.shape[2]
    tile = rows - 2 * HALO
    return pl.pallas_call(
        object_kernel,
        out_shape=jax.ShapeDtypeStruct((2, tile, nblk * LANES), F32),
        in_specs=[SM] + [VM] * 5,
        out_specs=VM,
        scratch_shapes=[pltpu.VMEM((2, nblk, tile, LANES), F32)],
        compiler_params=pltpu.CompilerParams(vmem_limit_bytes=40 * 1024 * 1024),
        name="finish_object",
    )(meta, main, col_a, col_b, row_a, row_b)


def probe_kernel(meta_ref, mine_ref, theirs_ref, out_ref):
    core = meta_ref[2]
    modes, side = out_ref.shape[1], out_ref.shape[2]
    for part_ref, at in ((mine_ref, core), (theirs_ref, 1 - core)):
        for m in range(modes):
            for i in range(side // CHUNK):
                for j in range(side // LANES):
                    k = (m * (side // CHUNK) + i) * (side // LANES) + j
                    out_ref[at, m, i * CHUNK : (i + 1) * CHUNK, j * LANES : (j + 1) * LANES] = part_ref[k].astype(F32)


def finish_probe(meta, mine, theirs, shape):
    return pl.pallas_call(
        probe_kernel,
        out_shape=jax.ShapeDtypeStruct(shape, F32),
        in_specs=[SM, VM, VM],
        out_specs=VM,
        name="finish_probe",
    )(meta, mine, theirs)


def trade(value, axis, phase):
    n = lax.axis_size(axis)
    pairs = [(i, ((i + phase) ^ 1) - phase) for i in range(n)]
    return lax.ppermute(value, axis, [(i, j) for i, j in pairs if 0 <= j < n])


def shards(object_field, probe_modes, measured_amp, scan_positions, frame_counts):
    tile = object_field.shape[1]
    slots = measured_amp.shape[2]
    row_odd = lax.axis_index("row") % 2
    core = lax.axis_index("core")
    meta = jnp.stack([frame_counts[0, 0], row_odd, core]).astype(jnp.int32)
    bottom = object_field[:, tile - HALO :, :]
    top = object_field[:, :HALO, :]
    row_a = trade(jnp.where(row_odd == 0, bottom, top), "row", 0)
    row_b = trade(jnp.where(row_odd == 0, top, bottom), "row", 1)
    above = jnp.where(row_odd == 0, row_b, row_a)
    below = jnp.where(row_odd == 0, row_a, row_b)

    def column(lo):
        return jnp.concatenate([v[:, :, lo : lo + HALO] for v in (above, object_field, below)], axis=1)

    right, left = column(tile - HALO), column(0)
    col_a = trade(jnp.where(core == 0, right, left), COL, 0)
    col_b = trade(jnp.where(core == 0, left, right), COL, 1)
    lt, rt = fourier_tables(probe_modes.shape[-1])
    main, out_a, out_b, keep, send = run_frames(
        meta, scan_positions[0, 0], object_field, row_a, row_b, col_a, col_b, probe_modes, measured_amp[0, 0], lt, rt
    )
    scale = 1.0 / math.sqrt(lax.axis_size("row") * lax.axis_size(COL) * slots)
    pair = pair_sum(keep, trade(send, COL, 0))
    got_a = trade(out_a, COL, 0)
    got_b = trade(out_b, COL, 1)
    peers = lax.all_to_all(pair, PEERS, 0, 0, tiled=True)
    rows_a, rows_b = row_margins(meta, main, got_a, got_b)
    back_a = trade(rows_a, "row", 0)
    back_b = trade(rows_b, "row", 1)
    mine = lax.all_to_all(peer_sum(peers, scale), PEERS, 0, 0, tiled=True)
    theirs = trade(mine, COL, 0)
    obj = finish_object(meta, main, got_a, got_b, back_a, back_b)
    return obj, finish_probe(meta, mine, theirs, probe_modes.shape)


def solution(mesh):
    n_col = mesh.shape["col"]
    fine = Mesh(mesh.devices.reshape(mesh.shape["row"], n_col // 2, 2), ("row",) + COL)
    in_specs = (
        P(None, "row", COL),
        P(),
        P("row", COL, None, None, None),
        P("row", COL, None, None),
        P("row", COL),
    )
    out_specs = (P(None, "row", COL), P())
    return jax.shard_map(shards, mesh=fine, in_specs=in_specs, out_specs=out_specs, check_vma=False)
```

```python
import math

import jax
import jax.numpy as jnp
import numpy as np
from jax import lax
from jax.experimental import pallas as pl
from jax.experimental.pallas import tpu as pltpu
from jax.sharding import Mesh
from jax.sharding import PartitionSpec as P

HALO = 128
LANES = 128
CHUNK = 16
BF16 = jnp.bfloat16
F32 = jnp.float32
COL = ("colc", "core")
PEERS = ("row", "colc")
VM = pl.BlockSpec(memory_space=pltpu.VMEM)
SM = pl.BlockSpec(memory_space=pltpu.SMEM)


def fourier_tables(side):
    indices = np.arange(side)
    angles = 2.0 * math.pi / side * (indices[:, None] * indices[None, :] % side)
    real = jnp.asarray((np.cos(angles) / math.sqrt(side)).astype(np.float32)).astype(BF16)
    imag = jnp.asarray((-np.sin(angles) / math.sqrt(side)).astype(np.float32)).astype(BF16)
    return jnp.block([[real, -imag], [imag, real]]), jnp.block([[real, imag], [-imag, real]])


def matmul(a, b):
    return jnp.dot(a, b, preferred_element_type=F32)


def frames_kernel(
    meta_ref, pos_ref, mid_ref, row_a_ref, row_b_ref, col_a_ref, col_b_ref, cor_a_ref, cor_b_ref, probe_ref, amp_ref,
    lt_ref, rt_ref,
    obj_hbm, strip_a_hbm, strip_b_hbm, out_a_hbm, out_b_hbm, send_hbm,
    ext, grad, pgrad, stage, firsts, out_a, out_b, send, sems,
):
    side = probe_ref.shape[-1]
    modes = probe_ref.shape[1]
    tile = mid_ref.shape[1]
    nblk = tile // LANES
    count, row_odd, core = meta_ref[0], meta_ref[1], meta_ref[2]
    row_a = pl.multiple_of((1 - row_odd) * (HALO + tile), HALO)
    row_b = pl.multiple_of(row_odd * (HALO + tile), HALO)
    col_a = (1 - core) * (nblk + 1)
    col_b = core * (nblk + 1)
    for c in range(2):
        for b in range(nblk):
            cols = slice(b * LANES, (b + 1) * LANES)
            ext[c, b + 1, pl.ds(row_a, HALO), :] = row_a_ref[c, :, cols].astype(F32)
            ext[c, b + 1, HALO : HALO + tile, :] = mid_ref[c, :, cols].astype(F32)
            ext[c, b + 1, pl.ds(row_b, HALO), :] = row_b_ref[c, :, cols].astype(F32)
        for col, own_ref, cor_ref in ((col_a, col_a_ref, cor_a_ref), (col_b, col_b_ref, cor_b_ref)):
            ext[c, col, pl.ds(row_a, HALO), :] = cor_ref[c].astype(F32)
            ext[c, col, HALO : HALO + tile, :] = own_ref[c].astype(F32)
            ext[c, col, pl.ds(row_b, HALO), :] = cor_ref[2 + c].astype(F32)
    grad[...] = jnp.zeros_like(grad)
    pgrad[...] = jnp.zeros_like(pgrad)
    lane = lax.broadcasted_iota(jnp.int32, (side, LANES), 1)

    def step(s, carry):
        row = pos_ref[0, s]
        col = pos_ref[1, s]
        cq = col // LANES
        cr = col % LANES
        back_shift = (LANES - cr) % LANES
        keep = lane < LANES - cr
        patch = []
        for c in range(2):
            rolled = [
                pltpu.roll(ext[c, jnp.minimum(cq + j, nblk + 1), pl.ds(row, side), :], back_shift, 1)
                for j in range(side // LANES + 1)
            ]
            patch.append([jnp.where(keep, rolled[j], rolled[j + 1]) for j in range(side // LANES)])
        patch_r = jnp.concatenate(patch[0], axis=1)
        patch_i = jnp.concatenate(patch[1], axis=1)
        for m in range(modes):
            pr = probe_ref[0, m]
            pi = probe_ref[1, m]
            stage[m, 0:side, :] = (pr * patch_r - pi * patch_i).astype(BF16)
            stage[m, side:, :] = (pr * patch_i + pi * patch_r).astype(BF16)
        for m in range(modes):
            f = matmul(lt_ref[...], stage[m]).astype(BF16)
            firsts[m * side : (m + 1) * side, 0:side] = f[:side]
            firsts[m * side : (m + 1) * side, side:] = f[side:]
        psi = matmul(firsts[...], rt_ref[...])
        psi_r = [psi[m * side : (m + 1) * side, :side] for m in range(modes)]
        psi_i = [psi[m * side : (m + 1) * side, side:] for m in range(modes)]
        power = sum(psi_r[m] * psi_r[m] + psi_i[m] * psi_i[m] for m in range(modes))
        factor = 1.0 - amp_ref[s].astype(F32) * lax.rsqrt(jnp.maximum(power, 0.25))
        for m in range(modes):
            stage[m, 0:side, :] = (psi_r[m] * factor).astype(BF16)
            stage[m, side:, :] = (psi_i[m] * factor).astype(BF16)
        for m in range(modes):
            f = matmul(rt_ref[...], stage[m]).astype(BF16)
            firsts[m * side : (m + 1) * side, 0:side] = f[:side]
            firsts[m * side : (m + 1) * side, side:] = f[side:]
        back = matmul(firsts[...], lt_ref[...])
        sum_r = jnp.zeros((side, side), F32)
        sum_i = jnp.zeros((side, side), F32)
        for m in range(modes):
            pr = probe_ref[0, m]
            pi = probe_ref[1, m]
            g_r = back[m * side : (m + 1) * side, :side]
            g_i = back[m * side : (m + 1) * side, side:]
            sum_r = sum_r + (pr * g_r + pi * g_i)
            sum_i = sum_i + (pr * g_i - pi * g_r)
            pgrad[0, m] += patch_r * g_r + patch_i * g_i
            pgrad[1, m] += patch_r * g_i - patch_i * g_r
        for c, v in enumerate((sum_r, sum_i)):
            parts = [pltpu.roll(v[:, j * LANES : (j + 1) * LANES], cr, 1) for j in range(side // LANES)]
            for j in range(side // LANES + 1):
                low = parts[j - 1] if j > 0 else jnp.zeros((side, LANES), F32)
                high = parts[j] if j < side // LANES else jnp.zeros((side, LANES), F32)
                grad[c, cq + j, pl.ds(row, side), :] += jnp.where(lane >= cr, high, low)
        return carry

    lax.fori_loop(0, count, step, 0)
    copies = []

    def put(src, dst):
        copies.append(pltpu.make_async_copy(src, dst, sems.at[len(copies)]))
        copies[-1].start()

    for c in range(2):
        for b in range(nblk):
            put(grad.at[c, b + 1, HALO : HALO + tile, :], obj_hbm.at[c, :, b * LANES : (b + 1) * LANES])
        put(grad.at[c, 1 : nblk + 1, pl.ds(row_a, HALO), :], strip_a_hbm.at[c])
        put(grad.at[c, 1 : nblk + 1, pl.ds(row_b, HALO), :], strip_b_hbm.at[c])
    for c in range(2):
        for m in range(modes):
            for i in range(side // CHUNK):
                for j in range(side // LANES):
                    send[(c * modes + m) * (side // CHUNK) + i, j * CHUNK : (j + 1) * CHUNK, :] = pgrad[
                        c, m, i * CHUNK : (i + 1) * CHUNK, j * LANES : (j + 1) * LANES
                    ].astype(BF16)
    put(send, send_hbm)
    for c in range(2):
        out_a[c] = grad[c, col_a].astype(BF16)
        out_b[c] = grad[c, col_b].astype(BF16)
    put(out_a, out_a_hbm)
    put(out_b, out_b_hbm)
    for copy in copies:
        copy.wait()


def run_frames(meta, pos, mid, halo, probe, amp, lt, rt):
    side = probe.shape[-1]
    modes = probe.shape[1]
    tile = mid.shape[1]
    nblk = tile // LANES
    rows = tile + 2 * HALO
    per_peer = CHUNK * (side // LANES)
    peers = 2 * modes * side // CHUNK
    return pl.pallas_call(
        frames_kernel,
        out_shape=(
            pltpu.HBM((2, tile, tile), F32),
            pltpu.HBM((2, nblk, HALO, LANES), F32),
            pltpu.HBM((2, nblk, HALO, LANES), F32),
            pltpu.HBM((2, rows, LANES), BF16),
            pltpu.HBM((2, rows, LANES), BF16),
            pltpu.HBM((peers, per_peer, LANES), BF16),
        ),
        in_specs=[SM, SM] + [VM] * 11,
        out_specs=(pl.BlockSpec(memory_space=pltpu.HBM),) * 6,
        scratch_shapes=[
            pltpu.VMEM((2, nblk + 2, rows, LANES), F32),
            pltpu.VMEM((2, nblk + 3, rows, LANES), F32),
            pltpu.VMEM(probe.shape, F32),
            pltpu.VMEM((modes, 2 * side, side), BF16),
            pltpu.VMEM((modes * side, 2 * side), BF16),
            pltpu.VMEM((2, rows, LANES), BF16),
            pltpu.VMEM((2, rows, LANES), BF16),
            pltpu.VMEM((peers, per_peer, LANES), BF16),
            pltpu.SemaphoreType.DMA((2 * nblk + 7,)),
        ],
        compiler_params=pltpu.CompilerParams(vmem_limit_bytes=32 * 1024 * 1024),
        name="frames",
    )(meta, pos, mid, *halo, probe, amp, lt, rt)


def row_margin_kernel(meta_ref, strip_a_ref, strip_b_ref, got_a_ref, got_b_ref, out_a_ref, out_b_ref):
    nblk, rows = strip_a_ref.shape[1], got_a_ref.shape[1]
    row_odd, core = meta_ref[1], meta_ref[2]

    def emit(own_ref, out_ref, start):
        for c in range(2):
            for b in range(nblk):
                out_ref[c, b] = own_ref[c, b].astype(BF16)
            for got_ref, blk in ((got_a_ref, (1 - core) * (nblk - 1)), (got_b_ref, core * (nblk - 1))):
                out_ref[c, blk] = (own_ref[c, blk] + got_ref[c, start : start + HALO, :].astype(F32)).astype(BF16)

    @pl.when(row_odd == 0)
    def _():
        emit(strip_a_ref, out_a_ref, rows - HALO)
        emit(strip_b_ref, out_b_ref, 0)

    @pl.when(row_odd == 1)
    def _():
        emit(strip_a_ref, out_a_ref, 0)
        emit(strip_b_ref, out_b_ref, rows - HALO)


def row_margins(meta, strip_a, strip_b, got_a, got_b):
    shape = jax.ShapeDtypeStruct(strip_a.shape, BF16)
    return pl.pallas_call(
        row_margin_kernel,
        out_shape=(shape, shape),
        in_specs=[SM] + [VM] * 4,
        out_specs=(VM, VM),
        compiler_params=pltpu.CompilerParams(vmem_limit_bytes=16 * 1024 * 1024),
        cost_estimate=pl.CostEstimate(flops=5000000000, transcendentals=0, bytes_accessed=0),
        name="row_margins",
    )(meta, strip_a, strip_b, got_a, got_b)


def add_cols_kernel(meta_ref, part_ref, col_a_ref, col_b_ref, obj_ref):
    tile = part_ref.shape[1]
    inner = slice(HALO, HALO + tile)
    at_b = pl.program_id(0) == meta_ref[2]

    @pl.when(at_b)
    def _():
        obj_ref[...] = part_ref[...] + col_b_ref[:, inner, :].astype(F32)

    @pl.when(jnp.logical_not(at_b))
    def _():
        obj_ref[...] = part_ref[...] + col_a_ref[:, inner, :].astype(F32)


def add_cols(meta, part, col_a, col_b):
    tile, cols = part.shape[1:]
    edge = pl.BlockSpec((2, tile, LANES), lambda i: (0, 0, i * (cols // LANES - 1)))
    return pl.pallas_call(
        add_cols_kernel,
        grid=(2,),
        out_shape=jax.ShapeDtypeStruct(part.shape, F32),
        in_specs=[SM, edge, VM, VM],
        out_specs=edge,
        input_output_aliases={1: 0},
        cost_estimate=pl.CostEstimate(flops=5000000000, transcendentals=0, bytes_accessed=0),
        compiler_params=pltpu.CompilerParams(vmem_limit_bytes=16 * 1024 * 1024),
        name="add_cols",
    )(meta, part, col_a, col_b)


def add_rows_kernel(meta_ref, part_ref, row_a_ref, row_b_ref, obj_ref):
    nblk = row_a_ref.shape[1]
    at_b = pl.program_id(0) == meta_ref[1]

    def add(row_ref):
        for c in range(2):
            for b in range(nblk):
                cols = slice(b * LANES, (b + 1) * LANES)
                obj_ref[c, :, cols] = part_ref[c, :, cols] + row_ref[c, b].astype(F32)

    @pl.when(at_b)
    def _():
        add(row_b_ref)

    @pl.when(jnp.logical_not(at_b))
    def _():
        add(row_a_ref)


def add_rows(meta, part, row_a, row_b):
    tile, cols = part.shape[1:]
    edge = pl.BlockSpec((2, HALO, cols), lambda i: (0, i * (tile // HALO - 1), 0))
    return pl.pallas_call(
        add_rows_kernel,
        grid=(2,),
        out_shape=jax.ShapeDtypeStruct(part.shape, F32),
        in_specs=[SM, edge, VM, VM],
        out_specs=edge,
        input_output_aliases={1: 0},
        cost_estimate=pl.CostEstimate(flops=5000000000, transcendentals=0, bytes_accessed=0),
        compiler_params=pltpu.CompilerParams(vmem_limit_bytes=16 * 1024 * 1024),
        name="add_rows",
    )(meta, part, row_a, row_b)


def probe_kernel(got_ref, out_ref):
    modes, side = out_ref.shape[1], out_ref.shape[2]
    for c in range(2):
        for m in range(modes):
            for i in range(side // CHUNK):
                for j in range(side // LANES):
                    out_ref[c, m, i * CHUNK : (i + 1) * CHUNK, j * LANES : (j + 1) * LANES] = got_ref[
                        (c * modes + m) * (side // CHUNK) + i, j * CHUNK : (j + 1) * CHUNK, :
                    ].astype(F32)


def finish_probe(got, shape):
    return pl.pallas_call(
        probe_kernel,
        out_shape=jax.ShapeDtypeStruct(shape, F32),
        in_specs=[VM],
        out_specs=VM,
        compiler_params=pltpu.CompilerParams(vmem_limit_bytes=16 * 1024 * 1024),
        name="finish_probe",
    )(got)


def trade(value, axis, phase):
    n = lax.axis_size(axis)
    pairs = [(i, ((i + phase) ^ 1) - phase) for i in range(n)]
    return lax.ppermute(value, axis, [(i, j) for i, j in pairs if 0 <= j < n])


def shards(object_field, probe_modes, measured_amp, scan_positions, frame_counts):
    tile = object_field.shape[1]
    slots = measured_amp.shape[2]
    row_odd = lax.axis_index("row") % 2
    core = lax.axis_index("core")
    meta = jnp.stack([frame_counts[0, 0], row_odd, core]).astype(jnp.int32)
    even = row_odd == 0
    first = core == 0
    bottom = object_field[:, tile - HALO :, :]
    top = object_field[:, :HALO, :]
    row_a = trade(jnp.where(even, bottom, top), "row", 0)
    row_b = trade(jnp.where(even, top, bottom), "row", 1)
    right = object_field[:, :, tile - HALO :]
    left = object_field[:, :, :HALO]
    col_a = trade(jnp.where(first, right, left), COL, 0)
    col_b = trade(jnp.where(first, left, right), COL, 1)
    rights = jnp.concatenate([row_a[:, :, tile - HALO :], row_b[:, :, tile - HALO :]], axis=0)
    lefts = jnp.concatenate([row_a[:, :, :HALO], row_b[:, :, :HALO]], axis=0)
    cor_a = trade(jnp.where(first, rights, lefts), COL, 0)
    cor_b = trade(jnp.where(first, lefts, rights), COL, 1)
    lt, rt = fourier_tables(probe_modes.shape[-1])
    part, strip_a, strip_b, out_a, out_b, send = run_frames(
        meta, scan_positions[0, 0], object_field, (row_a, row_b, col_a, col_b, cor_a, cor_b),
        probe_modes, measured_amp[0, 0], lt, rt,
    )
    scale = 1.0 / math.sqrt(lax.axis_size("row") * lax.axis_size(COL) * slots)
    got_a = trade(out_a, COL, 0)
    got_b = trade(out_b, COL, 1)
    peers = lax.all_to_all(send, PEERS, 0, 0, tiled=True)
    rows_a, rows_b = row_margins(meta, strip_a, strip_b, got_a, got_b)
    peers, rows_a, rows_b = lax.optimization_barrier((peers, rows_a, rows_b))
    back_a = trade(rows_a, "row", 0)
    back_b = trade(rows_b, "row", 1)
    half = jnp.sum(peers.astype(F32), axis=0)
    total = ((half + trade(half, COL, 0)) * scale).astype(BF16)
    whole = lax.all_to_all(jnp.broadcast_to(total[None], send.shape), PEERS, 0, 0, tiled=True)
    part = add_cols(meta, part, got_a, got_b)
    obj = add_rows(meta, part, back_a, back_b)
    whole, obj = lax.optimization_barrier((whole, obj))
    return obj, finish_probe(whole, probe_modes.shape)


def solution(mesh):
    n_col = mesh.shape["col"]
    fine = Mesh(mesh.devices.reshape(mesh.shape["row"], n_col // 2, 2), ("row",) + COL)
    in_specs = (
        P(None, "row", COL),
        P(),
        P("row", COL, None, None, None),
        P("row", COL, None, None),
        P("row", COL),
    )
    out_specs = (P(None, "row", COL), P())
    return jax.shard_map(shards, mesh=fine, in_specs=in_specs, out_specs=out_specs, check_vma=False)
```

```python
import math

import jax
import jax.numpy as jnp
import numpy as np
from jax import lax
from jax.experimental import pallas as pl
from jax.experimental.pallas import tpu as pltpu
from jax.sharding import Mesh
from jax.sharding import PartitionSpec as P

HALO = 128
LANES = 128
CHUNK = 16
BF16 = jnp.bfloat16
F32 = jnp.float32
COL = ("colc", "core")
PEERS = ("row", "colc")
VM = pl.BlockSpec(memory_space=pltpu.VMEM)
SM = pl.BlockSpec(memory_space=pltpu.SMEM)


def fourier_tables(side):
    indices = np.arange(side)
    angles = 2.0 * math.pi / side * (indices[:, None] * indices[None, :] % side)
    real = jnp.asarray((np.cos(angles) / math.sqrt(side)).astype(np.float32)).astype(BF16)
    imag = jnp.asarray((-np.sin(angles) / math.sqrt(side)).astype(np.float32)).astype(BF16)
    return jnp.stack([jnp.block([[real, -imag], [imag, real]]), jnp.block([[real, imag], [-imag, real]])])


def place():
    return lax.axis_index("row") % 2, lax.axis_index("core")


def matmul(a, b):
    return jnp.dot(a, b, preferred_element_type=F32)


def margins_kernel(obj, edge_a, edge_b, row_a, row_b, col_a, col_b, sems):
    tile = obj.shape[1]
    row_odd, core = place()
    copies = []

    def put(src, dst):
        copies.append(pltpu.make_async_copy(src, dst, sems.at[len(copies)]))
        copies[-1].start()

    for edge, row, at in ((edge_b, row_b, row_odd), (edge_a, row_a, 1 - row_odd)):
        rows = pl.ds(pl.multiple_of(at * (tile - HALO), HALO), HALO)
        put(obj.at[:, rows, 0:HALO], edge.at[0:2])
        put(obj.at[:, rows, tile - HALO :], edge.at[2:4])
        put(obj.at[:, rows, HALO : tile - HALO], row)
    for col, at in ((col_b, core), (col_a, 1 - core)):
        put(obj.at[:, :, pl.ds(pl.multiple_of(at * (tile - HALO), HALO), HALO)], col)
    for copy in copies:
        copy.wait()


def margins(obj):
    tile = obj.shape[1]
    edge = jax.ShapeDtypeStruct((4, HALO, HALO), BF16)
    row = jax.ShapeDtypeStruct((2, HALO, tile - 2 * HALO), BF16)
    col = jax.ShapeDtypeStruct((2, tile, HALO), BF16)
    return pl.pallas_call(
        margins_kernel,
        out_shape=(edge, edge, row, row, col, col),
        in_specs=[pl.BlockSpec(memory_space=pltpu.HBM)],
        out_specs=(VM,) * 6,
        scratch_shapes=[pltpu.SemaphoreType.DMA((8,))],
        compiler_params=pltpu.CompilerParams(vmem_limit_bytes=8 * 1024 * 1024),
        name="margins",
    )(pltpu.with_memory_space_constraint(obj, pltpu.HBM))


def corners_kernel(edge_a, edge_b, cor_a, cor_b):
    core = lax.axis_index("core")
    for cor, at in ((cor_b, core), (cor_a, 1 - core)):
        cor[0:2] = edge_a[pl.ds(2 * at, 2)]
        cor[2:4] = edge_b[pl.ds(2 * at, 2)]


def corners(edge_a, edge_b):
    shape = jax.ShapeDtypeStruct(edge_a.shape, BF16)
    return pl.pallas_call(
        corners_kernel,
        out_shape=(shape, shape),
        in_specs=[VM, VM],
        out_specs=(VM, VM),
        compiler_params=pltpu.CompilerParams(vmem_limit_bytes=8 * 1024 * 1024),
        name="corners",
    )(edge_a, edge_b)


def frames_kernel(
    count_ref, pos_ref, edge_a_ref, edge_b_ref, row_a_ref, row_b_ref, col_a_ref, col_b_ref, cor_a_ref, cor_b_ref,
    ext_ref, grad_ref, pgrad_ref, probe_ref, amp_ref, tables_ref,
    ext, grad, pgrad, obj_hbm, strip_a_hbm, strip_b_hbm, out_a_hbm, out_b_hbm, keep_hbm, send_hbm,
    patch, waves, chi, firsts, backs, out_a, out_b, keep_out, send, sems,
):
    side = probe_ref.shape[-1]
    modes = probe_ref.shape[1]
    tile = col_a_ref.shape[1]
    nblk = tile // LANES
    count = count_ref[0, 0]
    row_odd, core = place()
    row_a = pl.multiple_of((1 - row_odd) * (HALO + tile), HALO)
    row_b = pl.multiple_of(row_odd * (HALO + tile), HALO)
    col_a = (1 - core) * (nblk + 1)
    col_b = core * (nblk + 1)
    lt_ref, rt_ref = tables_ref.at[0], tables_ref.at[1]
    for c in range(2):
        for b in range(nblk):
            outer = b in (0, nblk - 1)
            for at, edge_ref, row_ref in ((row_a, edge_a_ref, row_a_ref), (row_b, edge_b_ref, row_b_ref)):
                if outer:
                    ext[c, b + 1, pl.ds(at, HALO), :] = edge_ref[c + 2 * min(b, 1)].astype(F32)
                else:
                    ext[c, b + 1, pl.ds(at, HALO), :] = row_ref[c, :, (b - 1) * LANES : b * LANES].astype(F32)
        for col, own_ref, cor_ref in ((col_a, col_a_ref, cor_a_ref), (col_b, col_b_ref, cor_b_ref)):
            ext[c, col, pl.ds(row_a, HALO), :] = cor_ref[c].astype(F32)
            ext[c, col, HALO : HALO + tile, :] = own_ref[c].astype(F32)
            ext[c, col, pl.ds(row_b, HALO), :] = cor_ref[2 + c].astype(F32)
    lane = lax.broadcasted_iota(jnp.int32, (side, LANES), 1)

    def gather(s, slot):
        row = pos_ref[0, 0, 0, s]
        col = pos_ref[0, 0, 1, s]
        cq = col // LANES
        cr = col % LANES
        back_shift = (LANES - cr) % LANES
        keep = lane < LANES - cr
        for c in range(2):
            rolled = [
                pltpu.roll(ext[c, jnp.minimum(cq + j, nblk + 1), pl.ds(row, side), :], back_shift, 1)
                for j in range(side // LANES + 1)
            ]
            for j in range(side // LANES):
                patch[slot, c, :, j * LANES : (j + 1) * LANES] = jnp.where(keep, rolled[j], rolled[j + 1])

    def exits(slot):
        patch_r = patch[slot, 0]
        patch_i = patch[slot, 1]
        for m in range(modes):
            pr = probe_ref[0, m]
            pi = probe_ref[1, m]
            waves[m, 0:side, :] = (pr * patch_r - pi * patch_i).astype(BF16)
            waves[m, side:, :] = (pr * patch_i + pi * patch_r).astype(BF16)

    def left(table, src, dst):
        for m in range(modes):
            f = matmul(table, src[m]).astype(BF16)
            dst[m * side : (m + 1) * side, 0:side] = f[:side]
            dst[m * side : (m + 1) * side, side:] = f[side:]

    def make_chi(s):
        psi = matmul(firsts[...], rt_ref[...])
        psi_r = [psi[m * side : (m + 1) * side, :side] for m in range(modes)]
        psi_i = [psi[m * side : (m + 1) * side, side:] for m in range(modes)]
        power = sum(psi_r[m] * psi_r[m] + psi_i[m] * psi_i[m] for m in range(modes))
        factor = 1.0 - amp_ref[s].astype(F32) * lax.rsqrt(jnp.maximum(power, 0.25))
        for m in range(modes):
            chi[m, 0:side, :] = (psi_r[m] * factor).astype(BF16)
            chi[m, side:, :] = (psi_i[m] * factor).astype(BF16)

    def finish(s, slot, back):
        row = pos_ref[0, 0, 0, s]
        col = pos_ref[0, 0, 1, s]
        cq = col // LANES
        cr = col % LANES
        patch_r = patch[slot, 0]
        patch_i = patch[slot, 1]
        sum_r = jnp.zeros((side, side), F32)
        sum_i = jnp.zeros((side, side), F32)
        for m in range(modes):
            pr = probe_ref[0, m]
            pi = probe_ref[1, m]
            g_r = back[m * side : (m + 1) * side, :side]
            g_i = back[m * side : (m + 1) * side, side:]
            sum_r = sum_r + (pr * g_r + pi * g_i)
            sum_i = sum_i + (pr * g_i - pi * g_r)
            pgrad[0, m] += patch_r * g_r + patch_i * g_i
            pgrad[1, m] += patch_r * g_i - patch_i * g_r
        for c, v in enumerate((sum_r, sum_i)):
            parts = [pltpu.roll(v[:, j * LANES : (j + 1) * LANES], cr, 1) for j in range(side // LANES)]
            for j in range(side // LANES + 1):
                low = parts[j - 1] if j > 0 else jnp.zeros((side, LANES), F32)
                high = parts[j] if j < side // LANES else jnp.zeros((side, LANES), F32)
                grad[c, jnp.minimum(cq + j, nblk + 1), pl.ds(row, side), :] += jnp.where(lane >= cr, high, low)

    gather(0, 0)
    exits(0)
    left(lt_ref[...], waves, firsts)
    make_chi(0)

    def step(s, carry):
        slot = s % 2
        gather(s + 1, 1 - slot)
        left(rt_ref[...], chi, backs)
        exits(1 - slot)
        back = matmul(backs[...], lt_ref[...])
        left(lt_ref[...], waves, firsts)
        finish(s, slot, back)
        make_chi(s + 1)
        return carry

    lax.fori_loop(0, count - 1, step, 0)
    last = count - 1
    left(rt_ref[...], chi, backs)
    finish(last, last % 2, matmul(backs[...], lt_ref[...]))
    copies = []

    def put(src, dst):
        copies.append(pltpu.make_async_copy(src, dst, sems.at[len(copies)]))
        copies[-1].start()

    for c in range(2):
        for b in range(nblk):
            put(grad.at[c, b + 1, HALO : HALO + tile, :], obj_hbm.at[c, :, b * LANES : (b + 1) * LANES])
        put(grad.at[c, 1 : nblk + 1, pl.ds(row_a, HALO), :], strip_a_hbm.at[c])
        put(grad.at[c, 1 : nblk + 1, pl.ds(row_b, HALO), :], strip_b_hbm.at[c])
    for m in range(modes):
        for i in range(side // CHUNK):
            for j in range(side // LANES):
                k = (m * (side // CHUNK) + i) * (side // LANES) + j
                at = (m, slice(i * CHUNK, (i + 1) * CHUNK), slice(j * LANES, (j + 1) * LANES))
                send[k] = pgrad[(1 - core,) + at].astype(BF16)
                keep_out[k] = pgrad[(core,) + at]
    put(send, send_hbm)
    put(keep_out, keep_hbm)
    for c in range(2):
        out_a[c] = grad[c, col_a].astype(BF16)
        out_b[c] = grad[c, col_b].astype(BF16)
    put(out_a, out_a_hbm)
    put(out_b, out_b_hbm)
    for copy in copies:
        copy.wait()


def prepare_kernel(mid_hbm, probe_hbm, amp_hbm, tables_hbm, ext, grad, pgrad, probe, amp, tables, mid, sems):
    tile = mid.shape[1]
    copies = [
        pltpu.make_async_copy(src, dst, sems.at[i])
        for i, (src, dst) in enumerate(((mid_hbm, mid), (probe_hbm, probe), (amp_hbm, amp), (tables_hbm, tables)))
    ]
    for copy in copies:
        copy.start()
    grad[...] = jnp.zeros_like(grad)
    pgrad[...] = jnp.zeros_like(pgrad)
    copies[0].wait()
    for c in range(2):
        for b in range(tile // LANES):
            ext[c, b + 1, HALO : HALO + tile, :] = mid[c, :, b * LANES : (b + 1) * LANES].astype(F32)
    for copy in copies[1:]:
        copy.wait()


def prepare(mid, probe, amp, tables):
    tile = mid.shape[1]
    big = pltpu.VMEM((2, tile // LANES + 2, tile + 2 * HALO, LANES), F32)
    hbm = pl.BlockSpec(memory_space=pltpu.HBM)
    return pl.pallas_call(
        prepare_kernel,
        out_shape=(big, big, pltpu.VMEM(probe.shape, F32), pltpu.VMEM(probe.shape, F32), pltpu.VMEM(amp.shape, BF16),
                   pltpu.VMEM(tables.shape, BF16)),
        in_specs=[hbm] * 4,
        out_specs=(VM,) * 6,
        scratch_shapes=[pltpu.VMEM(mid.shape, BF16), pltpu.SemaphoreType.DMA((4,))],
        compiler_params=pltpu.CompilerParams(vmem_limit_bytes=16 * 1024 * 1024),
        cost_estimate=pl.CostEstimate(flops=5000000000, transcendentals=0, bytes_accessed=0),
        name="prepare",
    )(*[pltpu.with_memory_space_constraint(x, pltpu.HBM) for x in (mid, probe, amp, tables)])


def run_frames(count, pos, halo, prepared):
    ext, grad, pgrad, probe, amp, tables = prepared
    side = probe.shape[-1]
    modes = probe.shape[1]
    nblk = ext.shape[1] - 2
    rows = ext.shape[2]
    tile = rows - 2 * HALO
    chunks = modes * side * side // (CHUNK * LANES)
    first = 2 + len(halo)
    return pl.pallas_call(
        frames_kernel,
        out_shape=(
            pltpu.VMEM(ext.shape, F32),
            pltpu.VMEM(grad.shape, F32),
            pltpu.VMEM(pgrad.shape, F32),
            pltpu.HBM((2, tile, tile), F32),
            pltpu.HBM((2, nblk, HALO, LANES), F32),
            pltpu.HBM((2, nblk, HALO, LANES), F32),
            pltpu.HBM((2, rows, LANES), BF16),
            pltpu.HBM((2, rows, LANES), BF16),
            pltpu.HBM((chunks, CHUNK, LANES), F32),
            pltpu.HBM((chunks, CHUNK, LANES), BF16),
        ),
        in_specs=[SM, SM] + [VM] * (len(halo) + 6),
        out_specs=(VM,) * 3 + (pl.BlockSpec(memory_space=pltpu.HBM),) * 7,
        input_output_aliases={first: 0, first + 1: 1, first + 2: 2},
        scratch_shapes=[
            pltpu.VMEM((2, 2, side, side), F32),
            pltpu.VMEM((modes, 2 * side, side), BF16),
            pltpu.VMEM((modes, 2 * side, side), BF16),
            pltpu.VMEM((modes * side, 2 * side), BF16),
            pltpu.VMEM((modes * side, 2 * side), BF16),
            pltpu.VMEM((2, rows, LANES), BF16),
            pltpu.VMEM((2, rows, LANES), BF16),
            pltpu.VMEM((chunks, CHUNK, LANES), F32),
            pltpu.VMEM((chunks, CHUNK, LANES), BF16),
            pltpu.SemaphoreType.DMA((2 * nblk + 8,)),
        ],
        compiler_params=pltpu.CompilerParams(vmem_limit_bytes=20 * 1024 * 1024),
        name="frames",
    )(count, pos, *halo, *prepared)[3:]


def row_margin_kernel(
    strip_a_hbm, strip_b_hbm, got_a_ref, got_b_ref, out_a_ref, out_b_ref, strip_a_ref, strip_b_ref, sem_a, sem_b
):
    nblk, rows = strip_a_ref.shape[1], got_a_ref.shape[1]
    row_odd, core = place()
    copy_a = pltpu.make_async_copy(strip_a_hbm, strip_a_ref, sem_a)
    copy_b = pltpu.make_async_copy(strip_b_hbm, strip_b_ref, sem_b)
    copy_a.start()
    copy_b.start()
    copy_a.wait()
    copy_b.wait()

    def emit(own_ref, out_ref, start):
        for c in range(2):
            for b in range(nblk):
                out_ref[c, b] = own_ref[c, b].astype(BF16)
            for got_ref, blk in ((got_a_ref, (1 - core) * (nblk - 1)), (got_b_ref, core * (nblk - 1))):
                out_ref[c, blk] = (own_ref[c, blk] + got_ref[c, start : start + HALO, :].astype(F32)).astype(BF16)

    @pl.when(row_odd == 0)
    def _():
        emit(strip_a_ref, out_a_ref, rows - HALO)
        emit(strip_b_ref, out_b_ref, 0)

    @pl.when(row_odd == 1)
    def _():
        emit(strip_a_ref, out_a_ref, 0)
        emit(strip_b_ref, out_b_ref, rows - HALO)


def row_margins(strip_a, strip_b, got_a, got_b):
    shape = jax.ShapeDtypeStruct(strip_a.shape, BF16)
    return pl.pallas_call(
        row_margin_kernel,
        out_shape=(shape, shape),
        in_specs=[pl.BlockSpec(memory_space=pltpu.HBM)] * 2 + [VM] * 2,
        out_specs=(VM, VM),
        scratch_shapes=[
            pltpu.VMEM(strip_a.shape, F32),
            pltpu.VMEM(strip_b.shape, F32),
            pltpu.SemaphoreType.DMA(()),
            pltpu.SemaphoreType.DMA(()),
        ],
        compiler_params=pltpu.CompilerParams(vmem_limit_bytes=16 * 1024 * 1024),
        cost_estimate=pl.CostEstimate(flops=5000000000, transcendentals=0, bytes_accessed=0),
        name="row_margins",
    )(*[pltpu.with_memory_space_constraint(x, pltpu.HBM) for x in (strip_a, strip_b)], got_a, got_b)


def add_cols_kernel(part_ref, col_a_ref, col_b_ref, obj_ref):
    tile = part_ref.shape[1]
    inner = slice(HALO, HALO + tile)
    at_b = pl.program_id(0) == lax.axis_index("core")

    @pl.when(at_b)
    def _():
        obj_ref[...] = part_ref[...] + col_b_ref[:, inner, :].astype(F32)

    @pl.when(jnp.logical_not(at_b))
    def _():
        obj_ref[...] = part_ref[...] + col_a_ref[:, inner, :].astype(F32)


def add_cols(part, col_a, col_b):
    tile, cols = part.shape[1:]
    edge = pl.BlockSpec((2, tile, LANES), lambda i: (0, 0, i * (cols // LANES - 1)))
    return pl.pallas_call(
        add_cols_kernel,
        grid=(2,),
        out_shape=jax.ShapeDtypeStruct(part.shape, F32),
        in_specs=[edge, VM, VM],
        out_specs=edge,
        input_output_aliases={0: 0},
        cost_estimate=pl.CostEstimate(flops=5000000000, transcendentals=0, bytes_accessed=0),
        compiler_params=pltpu.CompilerParams(vmem_limit_bytes=16 * 1024 * 1024),
        name="add_cols",
    )(part, col_a, col_b)


def add_rows_kernel(part_ref, row_a_ref, row_b_ref, obj_ref):
    nblk = row_a_ref.shape[1]
    at_b = pl.program_id(0) == lax.axis_index("row") % 2

    def add(row_ref):
        for c in range(2):
            for b in range(nblk):
                cols = slice(b * LANES, (b + 1) * LANES)
                obj_ref[c, :, cols] = part_ref[c, :, cols] + row_ref[c, b].astype(F32)

    @pl.when(at_b)
    def _():
        add(row_b_ref)

    @pl.when(jnp.logical_not(at_b))
    def _():
        add(row_a_ref)


def add_rows(part, row_a, row_b):
    tile, cols = part.shape[1:]
    edge = pl.BlockSpec((2, HALO, cols), lambda i: (0, i * (tile // HALO - 1), 0))
    return pl.pallas_call(
        add_rows_kernel,
        grid=(2,),
        out_shape=jax.ShapeDtypeStruct(part.shape, F32),
        in_specs=[edge, VM, VM],
        out_specs=edge,
        input_output_aliases={0: 0},
        cost_estimate=pl.CostEstimate(flops=5000000000, transcendentals=0, bytes_accessed=0),
        compiler_params=pltpu.CompilerParams(vmem_limit_bytes=16 * 1024 * 1024),
        name="add_rows",
    )(part, row_a, row_b)


def probe_kernel(mine_ref, theirs_ref, out_ref):
    core = lax.axis_index("core")
    modes, side = out_ref.shape[1], out_ref.shape[2]
    for part_ref, at in ((mine_ref, core), (theirs_ref, 1 - core)):
        for m in range(modes):
            for i in range(side // CHUNK):
                for j in range(side // LANES):
                    k = (m * (side // CHUNK) + i) * (side // LANES) + j
                    out_ref[at, m, i * CHUNK : (i + 1) * CHUNK, j * LANES : (j + 1) * LANES] = part_ref[k].astype(F32)


def finish_probe(mine, theirs, shape):
    return pl.pallas_call(
        probe_kernel,
        out_shape=jax.ShapeDtypeStruct(shape, F32),
        in_specs=[VM, VM],
        out_specs=VM,
        compiler_params=pltpu.CompilerParams(vmem_limit_bytes=16 * 1024 * 1024),
        name="finish_probe",
    )(mine, theirs)


def trade(value, axis, phase):
    n = lax.axis_size(axis)
    pairs = [(i, ((i + phase) ^ 1) - phase) for i in range(n)]
    return lax.ppermute(value, axis, [(i, j) for i, j in pairs if 0 <= j < n])


def shards(object_field, probe_modes, measured_amp, scan_positions, frame_counts):
    slots = measured_amp.shape[2]
    to_edge_a, to_edge_b, to_row_a, to_row_b, to_col_a, to_col_b = margins(object_field)
    edge_b = trade(to_edge_b, "row", 1)
    edge_a = trade(to_edge_a, "row", 0)
    col_b = trade(to_col_b, COL, 1)
    col_a = trade(to_col_a, COL, 0)
    row_b = trade(to_row_b, "row", 1)
    row_a = trade(to_row_a, "row", 0)
    to_cor_a, to_cor_b = corners(edge_a, edge_b)
    cor_b = trade(to_cor_b, COL, 1)
    cor_a = trade(to_cor_a, COL, 0)
    prepared = prepare(object_field, probe_modes, measured_amp[0, 0], fourier_tables(probe_modes.shape[-1]))
    part, strip_a, strip_b, out_a, out_b, keep, send = run_frames(
        frame_counts, scan_positions, (edge_a, edge_b, row_a, row_b, col_a, col_b, cor_a, cor_b), prepared
    )
    scale = 1.0 / math.sqrt(lax.axis_size("row") * lax.axis_size(COL) * slots)
    pair = (keep + trade(send, COL, 0).astype(F32)).astype(BF16)
    got_a = trade(out_a, COL, 0)
    got_b = trade(out_b, COL, 1)
    peers = lax.all_to_all(pair, PEERS, 0, 0, tiled=True)
    rows_a, rows_b = row_margins(strip_a, strip_b, got_a, got_b)
    part = add_cols(part, got_a, got_b)
    peers, part = lax.optimization_barrier((peers, part))
    back_a = trade(rows_a, "row", 0)
    back_b = trade(rows_b, "row", 1)
    total = (jnp.sum(peers.astype(F32), axis=0) * scale).astype(BF16)
    mine = lax.all_to_all(jnp.broadcast_to(total[None], send.shape), PEERS, 0, 0, tiled=True)
    obj = add_rows(part, back_a, back_b)
    mine, obj = lax.optimization_barrier((mine, obj))
    return obj, finish_probe(mine, trade(mine, COL, 0), probe_modes.shape)


def solution(mesh):
    n_col = mesh.shape["col"]
    fine = Mesh(mesh.devices.reshape(mesh.shape["row"], n_col // 2, 2), ("row",) + COL)
    in_specs = (
        P(None, "row", COL),
        P(),
        P("row", COL, None, None, None),
        P("row", COL, None, None),
        P("row", COL),
    )
    out_specs = (P(None, "row", COL), P())
    return jax.shard_map(shards, mesh=fine, in_specs=in_specs, out_specs=out_specs, check_vma=False)
```

```python
import functools
import math

import jax
import jax.numpy as jnp
import numpy as np
from jax import lax
from jax.experimental import pallas as pl
from jax.experimental.pallas import tpu as pltpu
from jax.sharding import Mesh
from jax.sharding import PartitionSpec as P

HALO = 128
LANES = 128
CHUNK = 16
BF16 = jnp.bfloat16
F32 = jnp.float32
COL = ("colc", "core")
PEERS = ("row", "colc")
VM = pl.BlockSpec(memory_space=pltpu.VMEM)
SM = pl.BlockSpec(memory_space=pltpu.SMEM)


def fourier_tables(side):
    indices = np.arange(side)
    angles = 2.0 * math.pi / side * (indices[:, None] * indices[None, :] % side)
    real = jnp.asarray((np.cos(angles) / math.sqrt(side)).astype(np.float32)).astype(BF16)
    imag = jnp.asarray((-np.sin(angles) / math.sqrt(side)).astype(np.float32)).astype(BF16)
    return jnp.stack([jnp.block([[real, -imag], [imag, real]]), jnp.block([[real, imag], [-imag, real]])])


def place():
    return lax.axis_index("row") % 2, lax.axis_index("core")


def matmul(a, b):
    return jnp.dot(a, b, preferred_element_type=F32)


def margins_kernel(obj, row_a, row_b, col_a, col_b, sems):
    tile = obj.shape[1]
    row_odd, core = place()
    copies = []

    def put(src, dst):
        copies.append(pltpu.make_async_copy(src, dst, sems.at[len(copies)]))
        copies[-1].start()

    for row, at in ((row_b, row_odd), (row_a, 1 - row_odd)):
        put(obj.at[:, pl.ds(pl.multiple_of(at * (tile - HALO), HALO), HALO), :], row)
    for col, at in ((col_b, core), (col_a, 1 - core)):
        put(obj.at[:, :, pl.ds(pl.multiple_of(at * (tile - HALO), HALO), HALO)], col)
    for copy in copies:
        copy.wait()


def margins(obj):
    tile = obj.shape[1]
    row = jax.ShapeDtypeStruct((2, HALO, tile), BF16)
    col = jax.ShapeDtypeStruct((2, tile, HALO), BF16)
    return pl.pallas_call(
        margins_kernel,
        out_shape=(row, row, col, col),
        in_specs=[pl.BlockSpec(memory_space=pltpu.HBM)],
        out_specs=(VM,) * 4,
        scratch_shapes=[pltpu.SemaphoreType.DMA((4,))],
        compiler_params=pltpu.CompilerParams(vmem_limit_bytes=8 * 1024 * 1024),
        name="margins",
    )(pltpu.with_memory_space_constraint(obj, pltpu.HBM))


def corners_kernel(row_a, row_b, cor_a, cor_b):
    tile = row_a.shape[2]
    core = lax.axis_index("core")

    def emit(cor, cols):
        cor[0:2] = row_a[:, :, cols]
        cor[2:4] = row_b[:, :, cols]

    low, high = slice(0, HALO), slice(tile - HALO, tile)

    @pl.when(core == 0)
    def _():
        emit(cor_a, high)
        emit(cor_b, low)

    @pl.when(core == 1)
    def _():
        emit(cor_a, low)
        emit(cor_b, high)


def corners(row_a, row_b):
    shape = jax.ShapeDtypeStruct((4, HALO, HALO), BF16)
    return pl.pallas_call(
        corners_kernel,
        out_shape=(shape, shape),
        in_specs=[VM, VM],
        out_specs=(VM, VM),
        compiler_params=pltpu.CompilerParams(vmem_limit_bytes=8 * 1024 * 1024),
        name="corners",
    )(row_a, row_b)


def frames_kernel(
    count_ref, pos_ref, row_a_ref, row_b_ref, col_a_ref, col_b_ref, cor_a_ref, cor_b_ref,
    ext_ref, grad_ref, pgrad_ref, probe_ref, amp_ref, tables_ref,
    ext, grad, pgrad, obj_hbm, strip_a_hbm, strip_b_hbm, out_a_hbm, out_b_hbm, keep_out, send,
    patch, waves, chi, firsts, backs, out_a, out_b, sems,
):
    side = probe_ref.shape[-1]
    modes = probe_ref.shape[1]
    tile = col_a_ref.shape[1]
    nblk = tile // LANES
    count = count_ref[0, 0]
    row_odd, core = place()
    row_a = pl.multiple_of((1 - row_odd) * (HALO + tile), HALO)
    row_b = pl.multiple_of(row_odd * (HALO + tile), HALO)
    col_a = (1 - core) * (nblk + 1)
    col_b = core * (nblk + 1)
    lt_ref, rt_ref = tables_ref.at[0], tables_ref.at[1]
    for c in range(2):
        for b in range(nblk):
            for at, ref in ((row_a, row_a_ref), (row_b, row_b_ref)):
                ext[c, b + 1, pl.ds(at, HALO), :] = ref[c, :, b * LANES : (b + 1) * LANES].astype(F32)
        for col, own_ref, cor_ref in ((col_a, col_a_ref, cor_a_ref), (col_b, col_b_ref, cor_b_ref)):
            ext[c, col, pl.ds(row_a, HALO), :] = cor_ref[c].astype(F32)
            ext[c, col, HALO : HALO + tile, :] = own_ref[c].astype(F32)
            ext[c, col, pl.ds(row_b, HALO), :] = cor_ref[2 + c].astype(F32)
    lane = lax.broadcasted_iota(jnp.int32, (side, LANES), 1)

    def gather(s, slot):
        row = pos_ref[0, 0, 0, s]
        col = pos_ref[0, 0, 1, s]
        cq = col // LANES
        cr = col % LANES
        back_shift = (LANES - cr) % LANES
        keep = lane < LANES - cr
        for c in range(2):
            rolled = [
                pltpu.roll(ext[c, jnp.minimum(cq + j, nblk + 1), pl.ds(row, side), :], back_shift, 1)
                for j in range(side // LANES + 1)
            ]
            for j in range(side // LANES):
                patch[slot, c, :, j * LANES : (j + 1) * LANES] = jnp.where(keep, rolled[j], rolled[j + 1])

    def exits(slot):
        patch_r = patch[slot, 0]
        patch_i = patch[slot, 1]
        for m in range(modes):
            pr = probe_ref[0, m]
            pi = probe_ref[1, m]
            waves[m, 0:side, :] = (pr * patch_r - pi * patch_i).astype(BF16)
            waves[m, side:, :] = (pr * patch_i + pi * patch_r).astype(BF16)

    def left(table, src, dst):
        for m in range(modes):
            f = matmul(table, src[m]).astype(BF16)
            dst[m * side : (m + 1) * side, 0:side] = f[:side]
            dst[m * side : (m + 1) * side, side:] = f[side:]

    def make_chi(s):
        psi = matmul(firsts[...], rt_ref[...])
        psi_r = [psi[m * side : (m + 1) * side, :side] for m in range(modes)]
        psi_i = [psi[m * side : (m + 1) * side, side:] for m in range(modes)]
        power = sum(psi_r[m] * psi_r[m] + psi_i[m] * psi_i[m] for m in range(modes))
        factor = 1.0 - amp_ref[s].astype(F32) * lax.rsqrt(jnp.maximum(power, 0.25))
        for m in range(modes):
            chi[m, 0:side, :] = (psi_r[m] * factor).astype(BF16)
            chi[m, side:, :] = (psi_i[m] * factor).astype(BF16)

    def finish(s, slot, back):
        row = pos_ref[0, 0, 0, s]
        col = pos_ref[0, 0, 1, s]
        cq = col // LANES
        cr = col % LANES
        patch_r = patch[slot, 0]
        patch_i = patch[slot, 1]
        sum_r = jnp.zeros((side, side), F32)
        sum_i = jnp.zeros((side, side), F32)
        for m in range(modes):
            pr = probe_ref[0, m]
            pi = probe_ref[1, m]
            g_r = back[m * side : (m + 1) * side, :side]
            g_i = back[m * side : (m + 1) * side, side:]
            sum_r = sum_r + (pr * g_r + pi * g_i)
            sum_i = sum_i + (pr * g_i - pi * g_r)
            pgrad[0, m] += patch_r * g_r + patch_i * g_i
            pgrad[1, m] += patch_r * g_i - patch_i * g_r
        for c, v in enumerate((sum_r, sum_i)):
            parts = [pltpu.roll(v[:, j * LANES : (j + 1) * LANES], cr, 1) for j in range(side // LANES)]
            for j in range(side // LANES + 1):
                low = parts[j - 1] if j > 0 else jnp.zeros((side, LANES), F32)
                high = parts[j] if j < side // LANES else jnp.zeros((side, LANES), F32)
                grad[c, jnp.minimum(cq + j, nblk + 1), pl.ds(row, side), :] += jnp.where(lane >= cr, high, low)

    gather(0, 0)
    exits(0)
    left(lt_ref[...], waves, firsts)
    make_chi(0)

    def step(s, carry):
        slot = s % 2
        gather(s + 1, 1 - slot)
        left(rt_ref[...], chi, backs)
        exits(1 - slot)
        back = matmul(backs[...], lt_ref[...])
        left(lt_ref[...], waves, firsts)
        finish(s, slot, back)
        make_chi(s + 1)
        return carry

    lax.fori_loop(0, count - 1, step, 0)
    last = count - 1
    left(rt_ref[...], chi, backs)
    finish(last, last % 2, matmul(backs[...], lt_ref[...]))
    copies = []

    def put(src, dst):
        copies.append(pltpu.make_async_copy(src, dst, sems.at[len(copies)]))
        copies[-1].start()

    for c in range(2):
        for b in range(nblk):
            put(grad.at[c, b + 1, HALO : HALO + tile, :], obj_hbm.at[c, :, b * LANES : (b + 1) * LANES])
        put(grad.at[c, 1 : nblk + 1, pl.ds(row_a, HALO), :], strip_a_hbm.at[c])
        put(grad.at[c, 1 : nblk + 1, pl.ds(row_b, HALO), :], strip_b_hbm.at[c])
    for c in range(2):
        out_a[c] = grad[c, col_a].astype(BF16)
        out_b[c] = grad[c, col_b].astype(BF16)
    put(out_a, out_a_hbm)
    put(out_b, out_b_hbm)
    for m in range(modes):
        for i in range(side // CHUNK):
            for j in range(side // LANES):
                k = (m * (side // CHUNK) + i) * (side // LANES) + j
                at = (m, slice(i * CHUNK, (i + 1) * CHUNK), slice(j * LANES, (j + 1) * LANES))
                send[k] = pgrad[(1 - core,) + at].astype(BF16)
                keep_out[k] = pgrad[(core,) + at]
    for copy in copies:
        copy.wait()


def prepare_kernel(mid_hbm, probe_hbm, amp_hbm, tables_hbm, ext, grad, pgrad, probe, amp, tables, mid, sems):
    tile = mid.shape[1]
    copies = [
        pltpu.make_async_copy(src, dst, sems.at[i])
        for i, (src, dst) in enumerate(((mid_hbm, mid), (probe_hbm, probe), (amp_hbm, amp), (tables_hbm, tables)))
    ]
    for copy in copies:
        copy.start()
    grad[...] = jnp.zeros_like(grad)
    pgrad[...] = jnp.zeros_like(pgrad)
    copies[0].wait()
    for c in range(2):
        for b in range(tile // LANES):
            ext[c, b + 1, HALO : HALO + tile, :] = mid[c, :, b * LANES : (b + 1) * LANES].astype(F32)
    for copy in copies[1:]:
        copy.wait()


def prepare(mid, probe, amp, tables):
    tile = mid.shape[1]
    big = pltpu.VMEM((2, tile // LANES + 2, tile + 2 * HALO, LANES), F32)
    hbm = pl.BlockSpec(memory_space=pltpu.HBM)
    return pl.pallas_call(
        prepare_kernel,
        out_shape=(big, big, pltpu.VMEM(probe.shape, F32), pltpu.VMEM(probe.shape, F32), pltpu.VMEM(amp.shape, BF16),
                   pltpu.VMEM(tables.shape, BF16)),
        in_specs=[hbm] * 4,
        out_specs=(VM,) * 6,
        scratch_shapes=[pltpu.VMEM(mid.shape, BF16), pltpu.SemaphoreType.DMA((4,))],
        compiler_params=pltpu.CompilerParams(vmem_limit_bytes=16 * 1024 * 1024),
        cost_estimate=pl.CostEstimate(flops=5000000000, transcendentals=0, bytes_accessed=0),
        name="prepare",
    )(*[pltpu.with_memory_space_constraint(x, pltpu.HBM) for x in (mid, probe, amp, tables)])


def run_frames(count, pos, halo, prepared):
    ext, grad, pgrad, probe, amp, tables = prepared
    side = probe.shape[-1]
    modes = probe.shape[1]
    nblk = ext.shape[1] - 2
    rows = ext.shape[2]
    tile = rows - 2 * HALO
    chunks = modes * side * side // (CHUNK * LANES)
    first = 2 + len(halo)
    return pl.pallas_call(
        frames_kernel,
        out_shape=(
            pltpu.VMEM(ext.shape, F32),
            pltpu.VMEM(grad.shape, F32),
            pltpu.VMEM(pgrad.shape, F32),
            pltpu.HBM((2, tile, tile), F32),
            pltpu.HBM((2, nblk, HALO, LANES), F32),
            pltpu.HBM((2, nblk, HALO, LANES), F32),
            pltpu.HBM((2, rows, LANES), BF16),
            pltpu.HBM((2, rows, LANES), BF16),
            pltpu.VMEM((chunks, CHUNK, LANES), F32),
            pltpu.VMEM((chunks, CHUNK, LANES), BF16),
        ),
        in_specs=[SM, SM] + [VM] * (len(halo) + 6),
        out_specs=(VM,) * 3 + (pl.BlockSpec(memory_space=pltpu.HBM),) * 5 + (VM,) * 2,
        input_output_aliases={first: 0, first + 1: 1, first + 2: 2},
        scratch_shapes=[
            pltpu.VMEM((2, 2, side, side), F32),
            pltpu.VMEM((modes, 2 * side, side), BF16),
            pltpu.VMEM((modes, 2 * side, side), BF16),
            pltpu.VMEM((modes * side, 2 * side), BF16),
            pltpu.VMEM((modes * side, 2 * side), BF16),
            pltpu.VMEM((2, rows, LANES), BF16),
            pltpu.VMEM((2, rows, LANES), BF16),
            pltpu.SemaphoreType.DMA((2 * nblk + 6,)),
        ],
        compiler_params=pltpu.CompilerParams(vmem_limit_bytes=8 * 1024 * 1024),
        name="frames",
    )(count, pos, *halo, *prepared)


def row_margin_kernel(
    strip_a_hbm, strip_b_hbm, got_a_ref, got_b_ref, out_a_ref, out_b_ref, strip_a_ref, strip_b_ref, sem_a, sem_b
):
    nblk, rows = strip_a_ref.shape[1], got_a_ref.shape[1]
    row_odd, core = place()
    copy_a = pltpu.make_async_copy(strip_a_hbm, strip_a_ref, sem_a)
    copy_b = pltpu.make_async_copy(strip_b_hbm, strip_b_ref, sem_b)
    copy_a.start()
    copy_b.start()
    copy_a.wait()
    copy_b.wait()

    def emit(own_ref, out_ref, start):
        for c in range(2):
            for b in range(nblk):
                out_ref[c, b] = own_ref[c, b].astype(BF16)
            for got_ref, blk in ((got_a_ref, (1 - core) * (nblk - 1)), (got_b_ref, core * (nblk - 1))):
                out_ref[c, blk] = (own_ref[c, blk] + got_ref[c, start : start + HALO, :].astype(F32)).astype(BF16)

    @pl.when(row_odd == 0)
    def _():
        emit(strip_a_ref, out_a_ref, rows - HALO)
        emit(strip_b_ref, out_b_ref, 0)

    @pl.when(row_odd == 1)
    def _():
        emit(strip_a_ref, out_a_ref, 0)
        emit(strip_b_ref, out_b_ref, rows - HALO)


def row_margins(strip_a, strip_b, got_a, got_b):
    shape = jax.ShapeDtypeStruct(strip_a.shape, BF16)
    return pl.pallas_call(
        row_margin_kernel,
        out_shape=(shape, shape),
        in_specs=[pl.BlockSpec(memory_space=pltpu.HBM)] * 2 + [VM] * 2,
        out_specs=(VM, VM),
        scratch_shapes=[
            pltpu.VMEM(strip_a.shape, F32),
            pltpu.VMEM(strip_b.shape, F32),
            pltpu.SemaphoreType.DMA(()),
            pltpu.SemaphoreType.DMA(()),
        ],
        compiler_params=pltpu.CompilerParams(vmem_limit_bytes=16 * 1024 * 1024),
        cost_estimate=pl.CostEstimate(flops=5000000000, transcendentals=0, bytes_accessed=0),
        name="row_margins",
    )(*[pltpu.with_memory_space_constraint(x, pltpu.HBM) for x in (strip_a, strip_b)], got_a, got_b)


def peer_sum_kernel(scale, got_ref, out_ref):
    total = jnp.sum(got_ref[...].astype(F32), axis=0) * scale
    out_ref[...] = jnp.broadcast_to(total.astype(BF16)[None], out_ref.shape)


def peer_sum(got, scale):
    return pl.pallas_call(
        functools.partial(peer_sum_kernel, scale),
        out_shape=jax.ShapeDtypeStruct(got.shape, BF16),
        in_specs=[VM],
        out_specs=VM,
        compiler_params=pltpu.CompilerParams(vmem_limit_bytes=8 * 1024 * 1024),
        cost_estimate=pl.CostEstimate(flops=5000000000, transcendentals=0, bytes_accessed=0),
        name="peer_sum",
    )(got)


def object_kernel(part_hbm, col_a_ref, col_b_ref, row_a_ref, row_b_ref, obj_hbm, acc, in_sems, out_sems):
    nblk, tile = acc.shape[1], acc.shape[2]
    row_odd, core = place()
    inner = slice(HALO, HALO + tile)
    row_a = pl.multiple_of((1 - row_odd) * (tile - HALO), HALO)
    row_b = pl.multiple_of(row_odd * (tile - HALO), HALO)
    blocks = [(c, b) for c in range(2) for b in range(nblk)]
    fetches, copies = [], []
    for i, (c, b) in enumerate(blocks):
        cols = slice(b * LANES, (b + 1) * LANES)
        fetches.append(pltpu.make_async_copy(part_hbm.at[c, :, cols], acc.at[c, b], in_sems.at[i]))
        copies.append(pltpu.make_async_copy(acc.at[c, b], obj_hbm.at[c, :, cols], out_sems.at[i]))
        fetches[i].start()
    for i, (c, b) in enumerate(blocks):
        fetches[i].wait()
        if b == 0:
            acc[c, b] += jnp.where(core == 0, col_b_ref[c, inner, :], col_a_ref[c, inner, :]).astype(F32)
        if b == nblk - 1:
            acc[c, b] += jnp.where(core == 0, col_a_ref[c, inner, :], col_b_ref[c, inner, :]).astype(F32)
        acc[c, b, pl.ds(row_a, HALO), :] += row_a_ref[c, b].astype(F32)
        acc[c, b, pl.ds(row_b, HALO), :] += row_b_ref[c, b].astype(F32)
        copies[i].start()
    for copy in copies:
        copy.wait()


def finish_object(part, col_a, col_b, row_a, row_b):
    tile = part.shape[1]
    nblk = part.shape[2] // LANES
    return pl.pallas_call(
        object_kernel,
        out_shape=pltpu.HBM(part.shape, F32),
        in_specs=[pl.BlockSpec(memory_space=pltpu.HBM)] + [VM] * 4,
        out_specs=pl.BlockSpec(memory_space=pltpu.HBM),
        scratch_shapes=[
            pltpu.VMEM((2, nblk, tile, LANES), F32),
            pltpu.SemaphoreType.DMA((2 * nblk,)),
            pltpu.SemaphoreType.DMA((2 * nblk,)),
        ],
        compiler_params=pltpu.CompilerParams(vmem_limit_bytes=8 * 1024 * 1024),
        cost_estimate=pl.CostEstimate(flops=5000000000, transcendentals=0, bytes_accessed=0),
        name="finish_object",
    )(pltpu.with_memory_space_constraint(part, pltpu.HBM), col_a, col_b, row_a, row_b)


def probe_kernel(mine_ref, theirs_ref, out_ref):
    core = lax.axis_index("core")
    modes, side = out_ref.shape[1], out_ref.shape[2]
    for part_ref, at in ((mine_ref, core), (theirs_ref, 1 - core)):
        for m in range(modes):
            for i in range(side // CHUNK):
                for j in range(side // LANES):
                    k = (m * (side // CHUNK) + i) * (side // LANES) + j
                    out_ref[at, m, i * CHUNK : (i + 1) * CHUNK, j * LANES : (j + 1) * LANES] = part_ref[k].astype(F32)


def finish_probe(mine, theirs, shape):
    return pl.pallas_call(
        probe_kernel,
        out_shape=jax.ShapeDtypeStruct(shape, F32),
        in_specs=[VM, VM],
        out_specs=VM,
        compiler_params=pltpu.CompilerParams(vmem_limit_bytes=16 * 1024 * 1024),
        name="finish_probe",
    )(mine, theirs)


def trade(value, axis, phase):
    n = lax.axis_size(axis)
    pairs = [(i, ((i + phase) ^ 1) - phase) for i in range(n)]
    return lax.ppermute(value, axis, [(i, j) for i, j in pairs if 0 <= j < n])


def shards(object_field, probe_modes, measured_amp, scan_positions, frame_counts):
    slots = measured_amp.shape[2]
    to_row_a, to_row_b, to_col_a, to_col_b = margins(object_field)
    row_b = trade(to_row_b, "row", 1)
    row_a = trade(to_row_a, "row", 0)
    col_b = trade(to_col_b, COL, 1)
    col_a = trade(to_col_a, COL, 0)
    to_cor_a, to_cor_b = corners(row_a, row_b)
    cor_b = trade(to_cor_b, COL, 1)
    cor_a = trade(to_cor_a, COL, 0)
    prepared = prepare(object_field, probe_modes, measured_amp[0, 0], fourier_tables(probe_modes.shape[-1]))
    _, _, _, part, strip_a, strip_b, out_a, out_b, keep, send = run_frames(
        frame_counts, scan_positions, (row_a, row_b, col_a, col_b, cor_a, cor_b), prepared
    )
    scale = 1.0 / math.sqrt(lax.axis_size("row") * lax.axis_size(COL) * slots)
    pair = (keep + trade(send, COL, 0).astype(F32)).astype(BF16)
    got_a = trade(out_a, COL, 0)
    got_b = trade(out_b, COL, 1)
    peers = lax.all_to_all(pair, PEERS, 0, 0, tiled=True)
    rows_a, rows_b = row_margins(strip_a, strip_b, got_a, got_b)
    back_a = trade(rows_a, "row", 0)
    back_b = trade(rows_b, "row", 1)
    peers, rows_a, rows_b = lax.optimization_barrier((peers, rows_a, rows_b))
    mine = lax.all_to_all(peer_sum(peers, scale), PEERS, 0, 0, tiled=True)
    obj = finish_object(part, got_a, got_b, back_a, back_b)
    mine, obj = lax.optimization_barrier((mine, obj))
    return obj, finish_probe(mine, trade(mine, COL, 0), probe_modes.shape)


def solution(mesh):
    n_col = mesh.shape["col"]
    fine = Mesh(mesh.devices.reshape(mesh.shape["row"], n_col // 2, 2), ("row",) + COL)
    in_specs = (
        P(None, "row", COL),
        P(),
        P("row", COL, None, None, None),
        P("row", COL, None, None),
        P("row", COL),
    )
    out_specs = (P(None, "row", COL), P())
    return jax.shard_map(shards, mesh=fine, in_specs=in_specs, out_specs=out_specs, check_vma=False)
```

```python
import functools
import math

import jax
import jax.numpy as jnp
import numpy as np
from jax import lax
from jax.experimental import pallas as pl
from jax.experimental.pallas import tpu as pltpu
from jax.sharding import Mesh
from jax.sharding import PartitionSpec as P

HALO = 128
LANES = 128
CHUNK = 16
BF16 = jnp.bfloat16
F32 = jnp.float32
COL = ("colc", "core")
PEERS = ("row", "colc")
VM = pl.BlockSpec(memory_space=pltpu.VMEM)
SM = pl.BlockSpec(memory_space=pltpu.SMEM)


def fourier_tables(side):
    indices = np.arange(side)
    angles = 2.0 * math.pi / side * (indices[:, None] * indices[None, :] % side)
    real = jnp.asarray((np.cos(angles) / math.sqrt(side)).astype(np.float32)).astype(BF16)
    imag = jnp.asarray((-np.sin(angles) / math.sqrt(side)).astype(np.float32)).astype(BF16)
    return jnp.stack([jnp.block([[real, -imag], [imag, real]]), jnp.block([[real, imag], [-imag, real]])])


def place():
    return lax.axis_index("row") % 2, lax.axis_index("core")


def joined():
    row, n_row = lax.axis_index("row"), lax.axis_size("row")
    col, n_col = lax.axis_index(COL), lax.axis_size(COL)
    return (row > 0) & (row < n_row - 1), (col > 0) & (col < n_col - 1)


def live(cond, value):
    return jnp.where(cond, value, jnp.zeros_like(value))


def matmul(a, b):
    return jnp.dot(a, b, preferred_element_type=F32)


def margins_kernel(obj, row_a, row_b, col_a, col_b, sems):
    tile = obj.shape[1]
    row_odd, core = place()
    copies = []

    def put(src, dst):
        copies.append(pltpu.make_async_copy(src, dst, sems.at[len(copies)]))
        copies[-1].start()

    for row, at in ((row_b, row_odd), (row_a, 1 - row_odd)):
        put(obj.at[:, pl.ds(pl.multiple_of(at * (tile - HALO), HALO), HALO), :], row)
    for col, at in ((col_b, core), (col_a, 1 - core)):
        put(obj.at[:, :, pl.ds(pl.multiple_of(at * (tile - HALO), HALO), HALO)], col)
    for copy in copies:
        copy.wait()


def margins(obj):
    tile = obj.shape[1]
    row = jax.ShapeDtypeStruct((2, HALO, tile), BF16)
    col = jax.ShapeDtypeStruct((2, tile, HALO), BF16)
    return pl.pallas_call(
        margins_kernel,
        out_shape=(row, row, col, col),
        in_specs=[pl.BlockSpec(memory_space=pltpu.HBM)],
        out_specs=(VM,) * 4,
        scratch_shapes=[pltpu.SemaphoreType.DMA((4,))],
        compiler_params=pltpu.CompilerParams(vmem_limit_bytes=8 * 1024 * 1024),
        name="margins",
    )(pltpu.with_memory_space_constraint(obj, pltpu.HBM))


def corners_kernel(row_a, row_b, cor_a, cor_b):
    tile = row_a.shape[2]
    core = lax.axis_index("core")

    def emit(cor, cols):
        cor[0:2] = row_a[:, :, cols]
        cor[2:4] = row_b[:, :, cols]

    low, high = slice(0, HALO), slice(tile - HALO, tile)

    @pl.when(core == 0)
    def _():
        emit(cor_a, high)
        emit(cor_b, low)

    @pl.when(core == 1)
    def _():
        emit(cor_a, low)
        emit(cor_b, high)


def corners(row_a, row_b):
    shape = jax.ShapeDtypeStruct((4, HALO, HALO), BF16)
    return pl.pallas_call(
        corners_kernel,
        out_shape=(shape, shape),
        in_specs=[VM, VM],
        out_specs=(VM, VM),
        compiler_params=pltpu.CompilerParams(vmem_limit_bytes=8 * 1024 * 1024),
        name="corners",
    )(row_a, row_b)


def frames_kernel(
    count_ref, pos_ref, row_a_ref, row_b_ref, col_a_ref, col_b_ref, cor_a_ref, cor_b_ref,
    ext_ref, grad_ref, pgrad_ref, probe_ref, amp_ref, tables_ref,
    ext, grad, pgrad, obj_hbm, strip_a_hbm, strip_b_hbm, out_a_hbm, out_b_hbm, keep_out, send,
    patch, waves, chi, firsts, backs, out_a, out_b, sems,
):
    side = probe_ref.shape[-1]
    modes = probe_ref.shape[1]
    tile = col_a_ref.shape[1]
    nblk = tile // LANES
    count = count_ref[0, 0]
    row_odd, core = place()
    row_in, col_in = joined()
    row_a = pl.multiple_of((1 - row_odd) * (HALO + tile), HALO)
    row_b = pl.multiple_of(row_odd * (HALO + tile), HALO)
    col_a = (1 - core) * (nblk + 1)
    col_b = core * (nblk + 1)
    lt_ref, rt_ref = tables_ref.at[0], tables_ref.at[1]
    for c in range(2):
        for b in range(nblk):
            cols = slice(b * LANES, (b + 1) * LANES)
            ext[c, b + 1, pl.ds(row_a, HALO), :] = row_a_ref[c, :, cols].astype(F32)
            ext[c, b + 1, pl.ds(row_b, HALO), :] = live(row_in, row_b_ref[c, :, cols].astype(F32))
        ext[c, col_a, pl.ds(row_a, HALO), :] = cor_a_ref[c].astype(F32)
        ext[c, col_a, HALO : HALO + tile, :] = col_a_ref[c].astype(F32)
        ext[c, col_a, pl.ds(row_b, HALO), :] = live(row_in, cor_a_ref[2 + c].astype(F32))
        ext[c, col_b, pl.ds(row_a, HALO), :] = live(col_in, cor_b_ref[c].astype(F32))
        ext[c, col_b, HALO : HALO + tile, :] = live(col_in, col_b_ref[c].astype(F32))
        ext[c, col_b, pl.ds(row_b, HALO), :] = live(row_in & col_in, cor_b_ref[2 + c].astype(F32))
    lane = lax.broadcasted_iota(jnp.int32, (side, LANES), 1)

    def gather(s, slot):
        row = pos_ref[0, 0, 0, s]
        col = pos_ref[0, 0, 1, s]
        cq = col // LANES
        cr = col % LANES
        back_shift = (LANES - cr) % LANES
        keep = lane < LANES - cr
        for c in range(2):
            rolled = [
                pltpu.roll(ext[c, jnp.minimum(cq + j, nblk + 1), pl.ds(row, side), :], back_shift, 1)
                for j in range(side // LANES + 1)
            ]
            for j in range(side // LANES):
                patch[slot, c, :, j * LANES : (j + 1) * LANES] = jnp.where(keep, rolled[j], rolled[j + 1])

    def exits(slot):
        patch_r = patch[slot, 0]
        patch_i = patch[slot, 1]
        for m in range(modes):
            pr = probe_ref[0, m]
            pi = probe_ref[1, m]
            waves[m, 0:side, :] = (pr * patch_r - pi * patch_i).astype(BF16)
            waves[m, side:, :] = (pr * patch_i + pi * patch_r).astype(BF16)

    def left(table, src, dst):
        for m in range(modes):
            f = matmul(table, src[m]).astype(BF16)
            dst[m * side : (m + 1) * side, 0:side] = f[:side]
            dst[m * side : (m + 1) * side, side:] = f[side:]

    def make_chi(s):
        psi = matmul(firsts[...], rt_ref[...])
        psi_r = [psi[m * side : (m + 1) * side, :side] for m in range(modes)]
        psi_i = [psi[m * side : (m + 1) * side, side:] for m in range(modes)]
        power = sum(psi_r[m] * psi_r[m] + psi_i[m] * psi_i[m] for m in range(modes))
        factor = 1.0 - amp_ref[s].astype(F32) * lax.rsqrt(jnp.maximum(power, 0.25))
        for m in range(modes):
            chi[m, 0:side, :] = (psi_r[m] * factor).astype(BF16)
            chi[m, side:, :] = (psi_i[m] * factor).astype(BF16)

    def finish(s, slot, back):
        row = pos_ref[0, 0, 0, s]
        col = pos_ref[0, 0, 1, s]
        cq = col // LANES
        cr = col % LANES
        patch_r = patch[slot, 0]
        patch_i = patch[slot, 1]
        sum_r = jnp.zeros((side, side), F32)
        sum_i = jnp.zeros((side, side), F32)
        for m in range(modes):
            pr = probe_ref[0, m]
            pi = probe_ref[1, m]
            g_r = back[m * side : (m + 1) * side, :side]
            g_i = back[m * side : (m + 1) * side, side:]
            sum_r = sum_r + (pr * g_r + pi * g_i)
            sum_i = sum_i + (pr * g_i - pi * g_r)
            pgrad[0, m] += patch_r * g_r + patch_i * g_i
            pgrad[1, m] += patch_r * g_i - patch_i * g_r
        for c, v in enumerate((sum_r, sum_i)):
            parts = [pltpu.roll(v[:, j * LANES : (j + 1) * LANES], cr, 1) for j in range(side // LANES)]
            for j in range(side // LANES + 1):
                low = parts[j - 1] if j > 0 else jnp.zeros((side, LANES), F32)
                high = parts[j] if j < side // LANES else jnp.zeros((side, LANES), F32)
                grad[c, jnp.minimum(cq + j, nblk + 1), pl.ds(row, side), :] += jnp.where(lane >= cr, high, low)

    gather(0, 0)
    exits(0)
    left(lt_ref[...], waves, firsts)
    make_chi(0)

    def step(s, carry):
        slot = s % 2
        gather(s + 1, 1 - slot)
        left(rt_ref[...], chi, backs)
        exits(1 - slot)
        back = matmul(backs[...], lt_ref[...])
        left(lt_ref[...], waves, firsts)
        finish(s, slot, back)
        make_chi(s + 1)
        return carry

    lax.fori_loop(0, count - 1, step, 0)
    last = count - 1
    left(rt_ref[...], chi, backs)
    finish(last, last % 2, matmul(backs[...], lt_ref[...]))
    copies = []

    def put(src, dst):
        copies.append(pltpu.make_async_copy(src, dst, sems.at[len(copies)]))
        copies[-1].start()

    for c in range(2):
        for b in range(nblk):
            put(grad.at[c, b + 1, HALO : HALO + tile, :], obj_hbm.at[c, :, b * LANES : (b + 1) * LANES])
        put(grad.at[c, 1 : nblk + 1, pl.ds(row_a, HALO), :], strip_a_hbm.at[c])
        put(grad.at[c, 1 : nblk + 1, pl.ds(row_b, HALO), :], strip_b_hbm.at[c])
    for c in range(2):
        out_a[c] = grad[c, col_a].astype(BF16)
        out_b[c] = grad[c, col_b].astype(BF16)
    put(out_a, out_a_hbm)
    put(out_b, out_b_hbm)
    for m in range(modes):
        for i in range(side // CHUNK):
            for j in range(side // LANES):
                k = (m * (side // CHUNK) + i) * (side // LANES) + j
                at = (m, slice(i * CHUNK, (i + 1) * CHUNK), slice(j * LANES, (j + 1) * LANES))
                send[k] = pgrad[(1 - core,) + at].astype(BF16)
                keep_out[k] = pgrad[(core,) + at]
    for copy in copies:
        copy.wait()


def prepare_kernel(mid_hbm, probe_hbm, amp_hbm, tables_hbm, ext, grad, pgrad, probe, amp, tables, mid, sems):
    tile = mid.shape[1]
    copies = [
        pltpu.make_async_copy(src, dst, sems.at[i])
        for i, (src, dst) in enumerate(((mid_hbm, mid), (probe_hbm, probe), (amp_hbm, amp), (tables_hbm, tables)))
    ]
    for copy in copies:
        copy.start()
    grad[...] = jnp.zeros_like(grad)
    pgrad[...] = jnp.zeros_like(pgrad)
    copies[0].wait()
    for c in range(2):
        for b in range(tile // LANES):
            ext[c, b + 1, HALO : HALO + tile, :] = mid[c, :, b * LANES : (b + 1) * LANES].astype(F32)
    for copy in copies[1:]:
        copy.wait()


def prepare(mid, probe, amp, tables):
    tile = mid.shape[1]
    big = pltpu.VMEM((2, tile // LANES + 2, tile + 2 * HALO, LANES), F32)
    hbm = pl.BlockSpec(memory_space=pltpu.HBM)
    return pl.pallas_call(
        prepare_kernel,
        out_shape=(big, big, pltpu.VMEM(probe.shape, F32), pltpu.VMEM(probe.shape, F32), pltpu.VMEM(amp.shape, BF16),
                   pltpu.VMEM(tables.shape, BF16)),
        in_specs=[hbm] * 4,
        out_specs=(VM,) * 6,
        scratch_shapes=[pltpu.VMEM(mid.shape, BF16), pltpu.SemaphoreType.DMA((4,))],
        compiler_params=pltpu.CompilerParams(vmem_limit_bytes=16 * 1024 * 1024),
        cost_estimate=pl.CostEstimate(flops=5000000000, transcendentals=0, bytes_accessed=0),
        name="prepare",
    )(*[pltpu.with_memory_space_constraint(x, pltpu.HBM) for x in (mid, probe, amp, tables)])


def run_frames(count, pos, halo, prepared):
    ext, grad, pgrad, probe, amp, tables = prepared
    side = probe.shape[-1]
    modes = probe.shape[1]
    nblk = ext.shape[1] - 2
    rows = ext.shape[2]
    tile = rows - 2 * HALO
    chunks = modes * side * side // (CHUNK * LANES)
    first = 2 + len(halo)
    return pl.pallas_call(
        frames_kernel,
        out_shape=(
            pltpu.VMEM(ext.shape, F32),
            pltpu.VMEM(grad.shape, F32),
            pltpu.VMEM(pgrad.shape, F32),
            pltpu.HBM((2, tile, tile), F32),
            pltpu.HBM((2, nblk, HALO, LANES), F32),
            pltpu.HBM((2, nblk, HALO, LANES), F32),
            pltpu.HBM((2, rows, LANES), BF16),
            pltpu.HBM((2, rows, LANES), BF16),
            pltpu.VMEM((chunks, CHUNK, LANES), F32),
            pltpu.VMEM((chunks, CHUNK, LANES), BF16),
        ),
        in_specs=[SM, SM] + [VM] * (len(halo) + 6),
        out_specs=(VM,) * 3 + (pl.BlockSpec(memory_space=pltpu.HBM),) * 5 + (VM,) * 2,
        input_output_aliases={first: 0, first + 1: 1, first + 2: 2},
        scratch_shapes=[
            pltpu.VMEM((2, 2, side, side), F32),
            pltpu.VMEM((modes, 2 * side, side), BF16),
            pltpu.VMEM((modes, 2 * side, side), BF16),
            pltpu.VMEM((modes * side, 2 * side), BF16),
            pltpu.VMEM((modes * side, 2 * side), BF16),
            pltpu.VMEM((2, rows, LANES), BF16),
            pltpu.VMEM((2, rows, LANES), BF16),
            pltpu.SemaphoreType.DMA((2 * nblk + 6,)),
        ],
        compiler_params=pltpu.CompilerParams(vmem_limit_bytes=8 * 1024 * 1024),
        name="frames",
    )(count, pos, *halo, *prepared)


def row_margin_kernel(
    strip_a_hbm, strip_b_hbm, got_a_ref, got_b_ref, out_a_ref, out_b_ref, strip_a_ref, strip_b_ref, sem_a, sem_b
):
    nblk, rows = strip_a_ref.shape[1], got_a_ref.shape[1]
    row_odd, core = place()
    _, col_in = joined()
    copy_a = pltpu.make_async_copy(strip_a_hbm, strip_a_ref, sem_a)
    copy_b = pltpu.make_async_copy(strip_b_hbm, strip_b_ref, sem_b)
    copy_a.start()
    copy_b.start()
    copy_a.wait()
    copy_b.wait()

    def emit(own_ref, out_ref, start):
        for c in range(2):
            for b in range(nblk):
                out_ref[c, b] = own_ref[c, b].astype(BF16)
            at = slice(start, start + HALO)
            blk_a, blk_b = (1 - core) * (nblk - 1), core * (nblk - 1)
            out_ref[c, blk_a] = (own_ref[c, blk_a] + got_a_ref[c, at, :].astype(F32)).astype(BF16)
            out_ref[c, blk_b] = (own_ref[c, blk_b] + live(col_in, got_b_ref[c, at, :].astype(F32))).astype(BF16)

    @pl.when(row_odd == 0)
    def _():
        emit(strip_a_ref, out_a_ref, rows - HALO)
        emit(strip_b_ref, out_b_ref, 0)

    @pl.when(row_odd == 1)
    def _():
        emit(strip_a_ref, out_a_ref, 0)
        emit(strip_b_ref, out_b_ref, rows - HALO)


def row_margins(strip_a, strip_b, got_a, got_b):
    shape = jax.ShapeDtypeStruct(strip_a.shape, BF16)
    return pl.pallas_call(
        row_margin_kernel,
        out_shape=(shape, shape),
        in_specs=[pl.BlockSpec(memory_space=pltpu.HBM)] * 2 + [VM] * 2,
        out_specs=(VM, VM),
        scratch_shapes=[
            pltpu.VMEM(strip_a.shape, F32),
            pltpu.VMEM(strip_b.shape, F32),
            pltpu.SemaphoreType.DMA(()),
            pltpu.SemaphoreType.DMA(()),
        ],
        compiler_params=pltpu.CompilerParams(vmem_limit_bytes=16 * 1024 * 1024),
        cost_estimate=pl.CostEstimate(flops=5000000000, transcendentals=0, bytes_accessed=0),
        name="row_margins",
    )(*[pltpu.with_memory_space_constraint(x, pltpu.HBM) for x in (strip_a, strip_b)], got_a, got_b)


def peer_sum_kernel(scale, got_ref, out_ref):
    total = jnp.sum(got_ref[...].astype(F32), axis=0) * scale
    out_ref[...] = jnp.broadcast_to(total.astype(BF16)[None], out_ref.shape)


def peer_sum(got, scale):
    return pl.pallas_call(
        functools.partial(peer_sum_kernel, scale),
        out_shape=jax.ShapeDtypeStruct(got.shape, BF16),
        in_specs=[VM],
        out_specs=VM,
        compiler_params=pltpu.CompilerParams(vmem_limit_bytes=8 * 1024 * 1024),
        cost_estimate=pl.CostEstimate(flops=5000000000, transcendentals=0, bytes_accessed=0),
        name="peer_sum",
    )(got)


def object_kernel(part_hbm, col_a_ref, col_b_ref, row_a_ref, row_b_ref, obj_hbm, acc, in_sems, out_sems):
    nblk, tile = acc.shape[1], acc.shape[2]
    row_odd, core = place()
    row_in, col_in = joined()
    inner = slice(HALO, HALO + tile)
    row_a = pl.multiple_of((1 - row_odd) * (tile - HALO), HALO)
    row_b = pl.multiple_of(row_odd * (tile - HALO), HALO)
    blocks = [(c, b) for c in range(2) for b in range(nblk)]
    fetches, copies = [], []
    for i, (c, b) in enumerate(blocks):
        cols = slice(b * LANES, (b + 1) * LANES)
        fetches.append(pltpu.make_async_copy(part_hbm.at[c, :, cols], acc.at[c, b], in_sems.at[i]))
        copies.append(pltpu.make_async_copy(acc.at[c, b], obj_hbm.at[c, :, cols], out_sems.at[i]))
        fetches[i].start()
    for i, (c, b) in enumerate(blocks):
        fetches[i].wait()
        if b == 0:
            got_a, got_b = col_a_ref[c, inner, :].astype(F32), live(col_in, col_b_ref[c, inner, :].astype(F32))
            acc[c, b] += jnp.where(core == 0, got_b, got_a)
        if b == nblk - 1:
            got_a, got_b = col_a_ref[c, inner, :].astype(F32), live(col_in, col_b_ref[c, inner, :].astype(F32))
            acc[c, b] += jnp.where(core == 0, got_a, got_b)
        acc[c, b, pl.ds(row_a, HALO), :] += row_a_ref[c, b].astype(F32)
        acc[c, b, pl.ds(row_b, HALO), :] += live(row_in, row_b_ref[c, b].astype(F32))
        copies[i].start()
    for copy in copies:
        copy.wait()


def finish_object(part, col_a, col_b, row_a, row_b):
    tile = part.shape[1]
    nblk = part.shape[2] // LANES
    return pl.pallas_call(
        object_kernel,
        out_shape=pltpu.HBM(part.shape, F32),
        in_specs=[pl.BlockSpec(memory_space=pltpu.HBM)] + [VM] * 4,
        out_specs=pl.BlockSpec(memory_space=pltpu.HBM),
        scratch_shapes=[
            pltpu.VMEM((2, nblk, tile, LANES), F32),
            pltpu.SemaphoreType.DMA((2 * nblk,)),
            pltpu.SemaphoreType.DMA((2 * nblk,)),
        ],
        compiler_params=pltpu.CompilerParams(vmem_limit_bytes=8 * 1024 * 1024),
        cost_estimate=pl.CostEstimate(flops=5000000000, transcendentals=0, bytes_accessed=0),
        name="finish_object",
    )(pltpu.with_memory_space_constraint(part, pltpu.HBM), col_a, col_b, row_a, row_b)


def probe_kernel(mine_ref, theirs_ref, out_ref):
    core = lax.axis_index("core")
    modes, side = out_ref.shape[1], out_ref.shape[2]
    for part_ref, at in ((mine_ref, core), (theirs_ref, 1 - core)):
        for m in range(modes):
            for i in range(side // CHUNK):
                for j in range(side // LANES):
                    k = (m * (side // CHUNK) + i) * (side // LANES) + j
                    out_ref[at, m, i * CHUNK : (i + 1) * CHUNK, j * LANES : (j + 1) * LANES] = part_ref[k].astype(F32)


def finish_probe(mine, theirs, shape):
    return pl.pallas_call(
        probe_kernel,
        out_shape=jax.ShapeDtypeStruct(shape, F32),
        in_specs=[VM, VM],
        out_specs=VM,
        compiler_params=pltpu.CompilerParams(vmem_limit_bytes=16 * 1024 * 1024),
        name="finish_probe",
    )(mine, theirs)


def trade(value, axis, phase):
    n = lax.axis_size(axis)
    return lax.ppermute(value, axis, [(i, (((i + phase) ^ 1) - phase) % n) for i in range(n)])


def shards(object_field, probe_modes, measured_amp, scan_positions, frame_counts):
    slots = measured_amp.shape[2]
    to_row_a, to_row_b, to_col_a, to_col_b = margins(object_field)
    row_b = trade(to_row_b, "row", 1)
    row_a = trade(to_row_a, "row", 0)
    col_b = trade(to_col_b, COL, 1)
    col_a = trade(to_col_a, COL, 0)
    to_cor_a, to_cor_b = corners(row_a, row_b)
    cor_b = trade(to_cor_b, COL, 1)
    cor_a = trade(to_cor_a, COL, 0)
    prepared = prepare(object_field, probe_modes, measured_amp[0, 0], fourier_tables(probe_modes.shape[-1]))
    _, _, _, part, strip_a, strip_b, out_a, out_b, keep, send = run_frames(
        frame_counts, scan_positions, (row_a, row_b, col_a, col_b, cor_a, cor_b), prepared
    )
    scale = 1.0 / math.sqrt(lax.axis_size("row") * lax.axis_size(COL) * slots)
    pair = (keep + trade(send, COL, 0).astype(F32)).astype(BF16)
    got_a = trade(out_a, COL, 0)
    got_b = trade(out_b, COL, 1)
    peers = lax.all_to_all(pair, PEERS, 0, 0, tiled=True)
    rows_a, rows_b = row_margins(strip_a, strip_b, got_a, got_b)
    back_a = trade(rows_a, "row", 0)
    back_b = trade(rows_b, "row", 1)
    peers, rows_a, rows_b = lax.optimization_barrier((peers, rows_a, rows_b))
    mine = lax.all_to_all(peer_sum(peers, scale), PEERS, 0, 0, tiled=True)
    obj = finish_object(part, got_a, got_b, back_a, back_b)
    mine, obj = lax.optimization_barrier((mine, obj))
    return obj, finish_probe(mine, trade(mine, COL, 0), probe_modes.shape)


def solution(mesh):
    n_col = mesh.shape["col"]
    fine = Mesh(mesh.devices.reshape(mesh.shape["row"], n_col // 2, 2), ("row",) + COL)
    in_specs = (
        P(None, "row", COL),
        P(),
        P("row", COL, None, None, None),
        P("row", COL, None, None),
        P("row", COL),
    )
    out_specs = (P(None, "row", COL), P())
    return jax.shard_map(shards, mesh=fine, in_specs=in_specs, out_specs=out_specs, check_vma=False)
```

```python
import functools
import math

import jax
import jax.numpy as jnp
import numpy as np
from jax import lax
from jax.experimental import pallas as pl
from jax.experimental.pallas import tpu as pltpu
from jax.sharding import Mesh
from jax.sharding import PartitionSpec as P

HALO = 128
LANES = 128
CHUNK = 16
BF16 = jnp.bfloat16
F32 = jnp.float32
COL = ("colc", "core")
PEERS = ("row", "colc")
VM = pl.BlockSpec(memory_space=pltpu.VMEM)
SM = pl.BlockSpec(memory_space=pltpu.SMEM)


def fourier_tables(side):
    indices = np.arange(side)
    angles = 2.0 * math.pi / side * (indices[:, None] * indices[None, :] % side)
    real = jnp.asarray((np.cos(angles) / math.sqrt(side)).astype(np.float32)).astype(BF16)
    imag = jnp.asarray((-np.sin(angles) / math.sqrt(side)).astype(np.float32)).astype(BF16)
    return jnp.stack([jnp.block([[real, -imag], [imag, real]]), jnp.block([[real, imag], [-imag, real]])])


def place():
    return lax.axis_index("row") % 2, lax.axis_index("core")


def joined():
    row, n_row = lax.axis_index("row"), lax.axis_size("row")
    col, n_col = lax.axis_index(COL), lax.axis_size(COL)
    return (row > 0) & (row < n_row - 1), (col > 0) & (col < n_col - 1)


def live(cond, value):
    return jnp.where(cond, value, jnp.zeros_like(value))


def matmul(a, b):
    return jnp.dot(a, b, preferred_element_type=F32)


def margins_kernel(obj, row_a, edge_b, row_b, col_a, col_b, sems):
    tile = obj.shape[1]
    row_odd, core = place()
    copies = []

    def put(src, dst):
        copies.append(pltpu.make_async_copy(src, dst, sems.at[len(copies)]))
        copies[-1].start()

    rows_b = pl.ds(pl.multiple_of(row_odd * (tile - HALO), HALO), HALO)
    put(obj.at[:, rows_b, 0:HALO], edge_b.at[0:2])
    put(obj.at[:, rows_b, tile - HALO :], edge_b.at[2:4])
    put(obj.at[:, pl.ds(pl.multiple_of((1 - row_odd) * (tile - HALO), HALO), HALO), :], row_a)
    put(obj.at[:, rows_b, HALO : tile - HALO], row_b)
    for col, at in ((col_b, core), (col_a, 1 - core)):
        put(obj.at[:, :, pl.ds(pl.multiple_of(at * (tile - HALO), HALO), HALO)], col)
    for copy in copies:
        copy.wait()


def margins(obj):
    tile = obj.shape[1]
    row = jax.ShapeDtypeStruct((2, HALO, tile), BF16)
    edge = jax.ShapeDtypeStruct((4, HALO, HALO), BF16)
    inside = jax.ShapeDtypeStruct((2, HALO, tile - 2 * HALO), BF16)
    col = jax.ShapeDtypeStruct((2, tile, HALO), BF16)
    return pl.pallas_call(
        margins_kernel,
        out_shape=(row, edge, inside, col, col),
        in_specs=[pl.BlockSpec(memory_space=pltpu.HBM)],
        out_specs=(VM,) * 5,
        scratch_shapes=[pltpu.SemaphoreType.DMA((6,))],
        compiler_params=pltpu.CompilerParams(vmem_limit_bytes=8 * 1024 * 1024),
        name="margins",
    )(pltpu.with_memory_space_constraint(obj, pltpu.HBM))


def corners_kernel(row_a, edge_b, cor_a, cor_b):
    tile = row_a.shape[2]
    core = lax.axis_index("core")

    def emit(cor, side):
        cor[0:2] = row_a[:, :, side * (tile - HALO) : side * (tile - HALO) + HALO]
        cor[2:4] = edge_b[2 * side : 2 * side + 2]

    low, high = 0, 1

    @pl.when(core == 0)
    def _():
        emit(cor_a, high)
        emit(cor_b, low)

    @pl.when(core == 1)
    def _():
        emit(cor_a, low)
        emit(cor_b, high)


def corners(row_a, edge_b):
    shape = jax.ShapeDtypeStruct(edge_b.shape, BF16)
    return pl.pallas_call(
        corners_kernel,
        out_shape=(shape, shape),
        in_specs=[VM, VM],
        out_specs=(VM, VM),
        compiler_params=pltpu.CompilerParams(vmem_limit_bytes=8 * 1024 * 1024),
        name="corners",
    )(row_a, edge_b)


def frames_kernel(
    count_ref, pos_ref, row_a_ref, edge_b_ref, row_b_ref, col_a_ref, col_b_ref, cor_a_ref, cor_b_ref,
    ext_ref, grad_ref, pgrad_ref, probe_ref, amp_ref, tables_ref,
    ext, grad, pgrad, obj_hbm, strip_a_hbm, strip_b_hbm, out_a_hbm, out_b_hbm, keep_out, send,
    patch, waves, chi, firsts, backs, out_a, out_b, sems,
):
    side = probe_ref.shape[-1]
    modes = probe_ref.shape[1]
    tile = col_a_ref.shape[1]
    nblk = tile // LANES
    count = count_ref[0, 0]
    row_odd, core = place()
    row_in, col_in = joined()
    row_a = pl.multiple_of((1 - row_odd) * (HALO + tile), HALO)
    row_b = pl.multiple_of(row_odd * (HALO + tile), HALO)
    col_a = (1 - core) * (nblk + 1)
    col_b = core * (nblk + 1)
    lt_ref, rt_ref = tables_ref.at[0], tables_ref.at[1]
    for c in range(2):
        for b in range(nblk):
            cols = slice(b * LANES, (b + 1) * LANES)
            ext[c, b + 1, pl.ds(row_a, HALO), :] = row_a_ref[c, :, cols].astype(F32)
            if b in (0, nblk - 1):
                part = edge_b_ref[c + 2 * min(b, 1)]
            else:
                part = row_b_ref[c, :, (b - 1) * LANES : b * LANES]
            ext[c, b + 1, pl.ds(row_b, HALO), :] = live(row_in, part.astype(F32))
        ext[c, col_a, pl.ds(row_a, HALO), :] = cor_a_ref[c].astype(F32)
        ext[c, col_a, HALO : HALO + tile, :] = col_a_ref[c].astype(F32)
        ext[c, col_a, pl.ds(row_b, HALO), :] = live(row_in, cor_a_ref[2 + c].astype(F32))
        ext[c, col_b, pl.ds(row_a, HALO), :] = live(col_in, cor_b_ref[c].astype(F32))
        ext[c, col_b, HALO : HALO + tile, :] = live(col_in, col_b_ref[c].astype(F32))
        ext[c, col_b, pl.ds(row_b, HALO), :] = live(row_in & col_in, cor_b_ref[2 + c].astype(F32))
    lane = lax.broadcasted_iota(jnp.int32, (side, LANES), 1)

    def gather(s, slot):
        row = pos_ref[0, 0, 0, s]
        col = pos_ref[0, 0, 1, s]
        cq = col // LANES
        cr = col % LANES
        back_shift = (LANES - cr) % LANES
        keep = lane < LANES - cr
        for c in range(2):
            rolled = [
                pltpu.roll(ext[c, jnp.minimum(cq + j, nblk + 1), pl.ds(row, side), :], back_shift, 1)
                for j in range(side // LANES + 1)
            ]
            for j in range(side // LANES):
                patch[slot, c, :, j * LANES : (j + 1) * LANES] = jnp.where(keep, rolled[j], rolled[j + 1])

    def exits(slot):
        patch_r = patch[slot, 0]
        patch_i = patch[slot, 1]
        for m in range(modes):
            pr = probe_ref[0, m]
            pi = probe_ref[1, m]
            waves[m, 0:side, :] = (pr * patch_r - pi * patch_i).astype(BF16)
            waves[m, side:, :] = (pr * patch_i + pi * patch_r).astype(BF16)

    def left(table, src, dst):
        for m in range(modes):
            f = matmul(table, src[m]).astype(BF16)
            dst[m * side : (m + 1) * side, 0:side] = f[:side]
            dst[m * side : (m + 1) * side, side:] = f[side:]

    def make_chi(s):
        psi = matmul(firsts[...], rt_ref[...])
        psi_r = [psi[m * side : (m + 1) * side, :side] for m in range(modes)]
        psi_i = [psi[m * side : (m + 1) * side, side:] for m in range(modes)]
        power = sum(psi_r[m] * psi_r[m] + psi_i[m] * psi_i[m] for m in range(modes))
        factor = 1.0 - amp_ref[s].astype(F32) * lax.rsqrt(jnp.maximum(power, 0.25))
        for m in range(modes):
            chi[m, 0:side, :] = (psi_r[m] * factor).astype(BF16)
            chi[m, side:, :] = (psi_i[m] * factor).astype(BF16)

    def finish(s, slot, back):
        row = pos_ref[0, 0, 0, s]
        col = pos_ref[0, 0, 1, s]
        cq = col // LANES
        cr = col % LANES
        patch_r = patch[slot, 0]
        patch_i = patch[slot, 1]
        sum_r = jnp.zeros((side, side), F32)
        sum_i = jnp.zeros((side, side), F32)
        for m in range(modes):
            pr = probe_ref[0, m]
            pi = probe_ref[1, m]
            g_r = back[m * side : (m + 1) * side, :side]
            g_i = back[m * side : (m + 1) * side, side:]
            sum_r = sum_r + (pr * g_r + pi * g_i)
            sum_i = sum_i + (pr * g_i - pi * g_r)
            pgrad[0, m] += patch_r * g_r + patch_i * g_i
            pgrad[1, m] += patch_r * g_i - patch_i * g_r
        for c, v in enumerate((sum_r, sum_i)):
            parts = [pltpu.roll(v[:, j * LANES : (j + 1) * LANES], cr, 1) for j in range(side // LANES)]
            for j in range(side // LANES + 1):
                low = parts[j - 1] if j > 0 else jnp.zeros((side, LANES), F32)
                high = parts[j] if j < side // LANES else jnp.zeros((side, LANES), F32)
                grad[c, jnp.minimum(cq + j, nblk + 1), pl.ds(row, side), :] += jnp.where(lane >= cr, high, low)

    gather(0, 0)
    exits(0)
    left(lt_ref[...], waves, firsts)
    make_chi(0)

    def step(s, carry):
        slot = s % 2
        gather(s + 1, 1 - slot)
        left(rt_ref[...], chi, backs)
        exits(1 - slot)
        back = matmul(backs[...], lt_ref[...])
        left(lt_ref[...], waves, firsts)
        finish(s, slot, back)
        make_chi(s + 1)
        return carry

    lax.fori_loop(0, count - 1, step, 0)
    last = count - 1
    left(rt_ref[...], chi, backs)
    finish(last, last % 2, matmul(backs[...], lt_ref[...]))
    copies = []

    def put(src, dst):
        copies.append(pltpu.make_async_copy(src, dst, sems.at[len(copies)]))
        copies[-1].start()

    for c in range(2):
        for b in range(nblk):
            put(grad.at[c, b + 1, HALO : HALO + tile, :], obj_hbm.at[c, :, b * LANES : (b + 1) * LANES])
        put(grad.at[c, 1 : nblk + 1, pl.ds(row_a, HALO), :], strip_a_hbm.at[c])
        put(grad.at[c, 1 : nblk + 1, pl.ds(row_b, HALO), :], strip_b_hbm.at[c])
    for c in range(2):
        out_a[c] = grad[c, col_a].astype(BF16)
        out_b[c] = grad[c, col_b].astype(BF16)
    put(out_a, out_a_hbm)
    put(out_b, out_b_hbm)
    for m in range(modes):
        for i in range(side // CHUNK):
            for j in range(side // LANES):
                k = (m * (side // CHUNK) + i) * (side // LANES) + j
                at = (m, slice(i * CHUNK, (i + 1) * CHUNK), slice(j * LANES, (j + 1) * LANES))
                send[k] = pgrad[(1 - core,) + at].astype(BF16)
                keep_out[k] = pgrad[(core,) + at]
    for copy in copies:
        copy.wait()


def prepare_kernel(mid_hbm, probe_hbm, amp_hbm, tables_hbm, ext, grad, pgrad, probe, amp, tables, mid, sems):
    tile = mid.shape[1]
    copies = [
        pltpu.make_async_copy(src, dst, sems.at[i])
        for i, (src, dst) in enumerate(((mid_hbm, mid), (probe_hbm, probe), (amp_hbm, amp), (tables_hbm, tables)))
    ]
    for copy in copies:
        copy.start()
    grad[...] = jnp.zeros_like(grad)
    pgrad[...] = jnp.zeros_like(pgrad)
    copies[0].wait()
    for c in range(2):
        for b in range(tile // LANES):
            ext[c, b + 1, HALO : HALO + tile, :] = mid[c, :, b * LANES : (b + 1) * LANES].astype(F32)
    for copy in copies[1:]:
        copy.wait()


def prepare(mid, probe, amp, tables):
    tile = mid.shape[1]
    big = pltpu.VMEM((2, tile // LANES + 2, tile + 2 * HALO, LANES), F32)
    hbm = pl.BlockSpec(memory_space=pltpu.HBM)
    return pl.pallas_call(
        prepare_kernel,
        out_shape=(big, big, pltpu.VMEM(probe.shape, F32), pltpu.VMEM(probe.shape, F32), pltpu.VMEM(amp.shape, BF16),
                   pltpu.VMEM(tables.shape, BF16)),
        in_specs=[hbm] * 4,
        out_specs=(VM,) * 6,
        scratch_shapes=[pltpu.VMEM(mid.shape, BF16), pltpu.SemaphoreType.DMA((4,))],
        compiler_params=pltpu.CompilerParams(vmem_limit_bytes=16 * 1024 * 1024),
        cost_estimate=pl.CostEstimate(flops=5000000000, transcendentals=0, bytes_accessed=0),
        name="prepare",
    )(*[pltpu.with_memory_space_constraint(x, pltpu.HBM) for x in (mid, probe, amp, tables)])


def run_frames(count, pos, halo, prepared):
    ext, grad, pgrad, probe, amp, tables = prepared
    side = probe.shape[-1]
    modes = probe.shape[1]
    nblk = ext.shape[1] - 2
    rows = ext.shape[2]
    tile = rows - 2 * HALO
    chunks = modes * side * side // (CHUNK * LANES)
    first = 2 + len(halo)
    return pl.pallas_call(
        frames_kernel,
        out_shape=(
            pltpu.VMEM(ext.shape, F32),
            pltpu.VMEM(grad.shape, F32),
            pltpu.VMEM(pgrad.shape, F32),
            pltpu.HBM((2, tile, tile), F32),
            pltpu.HBM((2, nblk, HALO, LANES), F32),
            pltpu.HBM((2, nblk, HALO, LANES), F32),
            pltpu.HBM((2, rows, LANES), BF16),
            pltpu.HBM((2, rows, LANES), BF16),
            pltpu.VMEM((chunks, CHUNK, LANES), F32),
            pltpu.VMEM((chunks, CHUNK, LANES), BF16),
        ),
        in_specs=[SM, SM] + [VM] * (len(halo) + 6),
        out_specs=(VM,) * 3 + (pl.BlockSpec(memory_space=pltpu.HBM),) * 5 + (VM,) * 2,
        input_output_aliases={first: 0, first + 1: 1, first + 2: 2},
        scratch_shapes=[
            pltpu.VMEM((2, 2, side, side), F32),
            pltpu.VMEM((modes, 2 * side, side), BF16),
            pltpu.VMEM((modes, 2 * side, side), BF16),
            pltpu.VMEM((modes * side, 2 * side), BF16),
            pltpu.VMEM((modes * side, 2 * side), BF16),
            pltpu.VMEM((2, rows, LANES), BF16),
            pltpu.VMEM((2, rows, LANES), BF16),
            pltpu.SemaphoreType.DMA((2 * nblk + 6,)),
        ],
        compiler_params=pltpu.CompilerParams(vmem_limit_bytes=8 * 1024 * 1024),
        name="frames",
    )(count, pos, *halo, *prepared)


def row_margin_kernel(
    strip_a_hbm, strip_b_hbm, got_a_ref, got_b_ref, out_a_ref, out_b_ref, strip_a_ref, strip_b_ref, sem_a, sem_b
):
    nblk, rows = strip_a_ref.shape[1], got_a_ref.shape[1]
    row_odd, core = place()
    _, col_in = joined()
    copy_a = pltpu.make_async_copy(strip_a_hbm, strip_a_ref, sem_a)
    copy_b = pltpu.make_async_copy(strip_b_hbm, strip_b_ref, sem_b)
    copy_a.start()
    copy_b.start()
    copy_a.wait()
    copy_b.wait()

    def emit(own_ref, out_ref, start):
        for c in range(2):
            for b in range(nblk):
                out_ref[c, b] = own_ref[c, b].astype(BF16)
            at = slice(start, start + HALO)
            blk_a, blk_b = (1 - core) * (nblk - 1), core * (nblk - 1)
            out_ref[c, blk_a] = (own_ref[c, blk_a] + got_a_ref[c, at, :].astype(F32)).astype(BF16)
            out_ref[c, blk_b] = (own_ref[c, blk_b] + live(col_in, got_b_ref[c, at, :].astype(F32))).astype(BF16)

    @pl.when(row_odd == 0)
    def _():
        emit(strip_a_ref, out_a_ref, rows - HALO)
        emit(strip_b_ref, out_b_ref, 0)

    @pl.when(row_odd == 1)
    def _():
        emit(strip_a_ref, out_a_ref, 0)
        emit(strip_b_ref, out_b_ref, rows - HALO)


def row_margins(strip_a, strip_b, got_a, got_b):
    shape = jax.ShapeDtypeStruct(strip_a.shape, BF16)
    return pl.pallas_call(
        row_margin_kernel,
        out_shape=(shape, shape),
        in_specs=[pl.BlockSpec(memory_space=pltpu.HBM)] * 2 + [VM] * 2,
        out_specs=(VM, VM),
        scratch_shapes=[
            pltpu.VMEM(strip_a.shape, F32),
            pltpu.VMEM(strip_b.shape, F32),
            pltpu.SemaphoreType.DMA(()),
            pltpu.SemaphoreType.DMA(()),
        ],
        compiler_params=pltpu.CompilerParams(vmem_limit_bytes=16 * 1024 * 1024),
        cost_estimate=pl.CostEstimate(flops=5000000000, transcendentals=0, bytes_accessed=0),
        name="row_margins",
    )(*[pltpu.with_memory_space_constraint(x, pltpu.HBM) for x in (strip_a, strip_b)], got_a, got_b)


def peer_sum_kernel(scale, got_ref, out_ref):
    total = jnp.sum(got_ref[...].astype(F32), axis=0) * scale
    out_ref[...] = jnp.broadcast_to(total.astype(BF16)[None], out_ref.shape)


def peer_sum(got, scale):
    return pl.pallas_call(
        functools.partial(peer_sum_kernel, scale),
        out_shape=jax.ShapeDtypeStruct(got.shape, BF16),
        in_specs=[VM],
        out_specs=VM,
        compiler_params=pltpu.CompilerParams(vmem_limit_bytes=8 * 1024 * 1024),
        cost_estimate=pl.CostEstimate(flops=5000000000, transcendentals=0, bytes_accessed=0),
        name="peer_sum",
    )(got)


def object_kernel(part_hbm, col_a_ref, col_b_ref, row_a_ref, row_b_ref, obj_hbm, acc, in_sems, out_sems):
    nblk, tile = acc.shape[1], acc.shape[2]
    row_odd, core = place()
    row_in, col_in = joined()
    inner = slice(HALO, HALO + tile)
    row_a = pl.multiple_of((1 - row_odd) * (tile - HALO), HALO)
    row_b = pl.multiple_of(row_odd * (tile - HALO), HALO)
    blocks = [(c, b) for c in range(2) for b in range(nblk)]
    fetches, copies = [], []
    for i, (c, b) in enumerate(blocks):
        cols = slice(b * LANES, (b + 1) * LANES)
        fetches.append(pltpu.make_async_copy(part_hbm.at[c, :, cols], acc.at[c, b], in_sems.at[i]))
        copies.append(pltpu.make_async_copy(acc.at[c, b], obj_hbm.at[c, :, cols], out_sems.at[i]))
        fetches[i].start()
    for i, (c, b) in enumerate(blocks):
        fetches[i].wait()
        if b == 0:
            got_a, got_b = col_a_ref[c, inner, :].astype(F32), live(col_in, col_b_ref[c, inner, :].astype(F32))
            acc[c, b] += jnp.where(core == 0, got_b, got_a)
        if b == nblk - 1:
            got_a, got_b = col_a_ref[c, inner, :].astype(F32), live(col_in, col_b_ref[c, inner, :].astype(F32))
            acc[c, b] += jnp.where(core == 0, got_a, got_b)
        acc[c, b, pl.ds(row_a, HALO), :] += row_a_ref[c, b].astype(F32)
        acc[c, b, pl.ds(row_b, HALO), :] += live(row_in, row_b_ref[c, b].astype(F32))
        copies[i].start()
    for copy in copies:
        copy.wait()


def finish_object(part, col_a, col_b, row_a, row_b):
    tile = part.shape[1]
    nblk = part.shape[2] // LANES
    return pl.pallas_call(
        object_kernel,
        out_shape=pltpu.HBM(part.shape, F32),
        in_specs=[pl.BlockSpec(memory_space=pltpu.HBM)] + [VM] * 4,
        out_specs=pl.BlockSpec(memory_space=pltpu.HBM),
        scratch_shapes=[
            pltpu.VMEM((2, nblk, tile, LANES), F32),
            pltpu.SemaphoreType.DMA((2 * nblk,)),
            pltpu.SemaphoreType.DMA((2 * nblk,)),
        ],
        compiler_params=pltpu.CompilerParams(vmem_limit_bytes=8 * 1024 * 1024),
        cost_estimate=pl.CostEstimate(flops=5000000000, transcendentals=0, bytes_accessed=0),
        name="finish_object",
    )(pltpu.with_memory_space_constraint(part, pltpu.HBM), col_a, col_b, row_a, row_b)


def probe_kernel(mine_ref, theirs_ref, out_ref):
    core = lax.axis_index("core")
    modes, side = out_ref.shape[1], out_ref.shape[2]
    for part_ref, at in ((mine_ref, core), (theirs_ref, 1 - core)):
        for m in range(modes):
            for i in range(side // CHUNK):
                for j in range(side // LANES):
                    k = (m * (side // CHUNK) + i) * (side // LANES) + j
                    out_ref[at, m, i * CHUNK : (i + 1) * CHUNK, j * LANES : (j + 1) * LANES] = part_ref[k].astype(F32)


def finish_probe(mine, theirs, shape):
    return pl.pallas_call(
        probe_kernel,
        out_shape=jax.ShapeDtypeStruct(shape, F32),
        in_specs=[VM, VM],
        out_specs=VM,
        compiler_params=pltpu.CompilerParams(vmem_limit_bytes=16 * 1024 * 1024),
        name="finish_probe",
    )(mine, theirs)


def trade(value, axis, phase):
    n = lax.axis_size(axis)
    return lax.ppermute(value, axis, [(i, (((i + phase) ^ 1) - phase) % n) for i in range(n)])


def shards(object_field, probe_modes, measured_amp, scan_positions, frame_counts):
    slots = measured_amp.shape[2]
    to_row_a, to_edge_b, to_row_b, to_col_a, to_col_b = margins(object_field)
    edge_b = trade(to_edge_b, "row", 1)
    row_a = trade(to_row_a, "row", 0)
    row_b = trade(to_row_b, "row", 1)
    col_b = trade(to_col_b, COL, 1)
    col_a = trade(to_col_a, COL, 0)
    to_cor_a, to_cor_b = corners(row_a, edge_b)
    cor_b = trade(to_cor_b, COL, 1)
    cor_a = trade(to_cor_a, COL, 0)
    prepared = prepare(object_field, probe_modes, measured_amp[0, 0], fourier_tables(probe_modes.shape[-1]))
    _, _, _, part, strip_a, strip_b, out_a, out_b, keep, send = run_frames(
        frame_counts, scan_positions, (row_a, edge_b, row_b, col_a, col_b, cor_a, cor_b), prepared
    )
    scale = 1.0 / math.sqrt(lax.axis_size("row") * lax.axis_size(COL) * slots)
    pair = (keep + trade(send, COL, 0).astype(F32)).astype(BF16)
    got_a = trade(out_a, COL, 0)
    got_b = trade(out_b, COL, 1)
    peers = lax.all_to_all(pair, PEERS, 0, 0, tiled=True)
    rows_a, rows_b = row_margins(strip_a, strip_b, got_a, got_b)
    back_a = trade(rows_a, "row", 0)
    back_b = trade(rows_b, "row", 1)
    peers, rows_a, rows_b = lax.optimization_barrier((peers, rows_a, rows_b))
    mine = lax.all_to_all(peer_sum(peers, scale), PEERS, 0, 0, tiled=True)
    obj = finish_object(part, got_a, got_b, back_a, back_b)
    mine, obj = lax.optimization_barrier((mine, obj))
    return obj, finish_probe(mine, trade(mine, COL, 0), probe_modes.shape)


def solution(mesh):
    n_col = mesh.shape["col"]
    fine = Mesh(mesh.devices.reshape(mesh.shape["row"], n_col // 2, 2), ("row",) + COL)
    in_specs = (
        P(None, "row", COL),
        P(),
        P("row", COL, None, None, None),
        P("row", COL, None, None),
        P("row", COL),
    )
    out_specs = (P(None, "row", COL), P())
    return jax.shard_map(shards, mesh=fine, in_specs=in_specs, out_specs=out_specs, check_vma=False)
```

```python
import functools
import math

import jax
import jax.numpy as jnp
import numpy as np
from jax import lax
from jax.experimental import pallas as pl
from jax.experimental.pallas import tpu as pltpu
from jax.sharding import Mesh
from jax.sharding import PartitionSpec as P

HALO = 128
LANES = 128
CHUNK = 16
BF16 = jnp.bfloat16
F32 = jnp.float32
COL = ("colc", "core")
PEERS = ("row", "colc")
VM = pl.BlockSpec(memory_space=pltpu.VMEM)
SM = pl.BlockSpec(memory_space=pltpu.SMEM)


def fourier_tables(side):
    indices = np.arange(side)
    angles = 2.0 * math.pi / side * (indices[:, None] * indices[None, :] % side)
    real = jnp.asarray((np.cos(angles) / math.sqrt(side)).astype(np.float32)).astype(BF16)
    imag = jnp.asarray((-np.sin(angles) / math.sqrt(side)).astype(np.float32)).astype(BF16)
    return jnp.stack([jnp.block([[real, -imag], [imag, real]]), jnp.block([[real, imag], [-imag, real]])])


def place():
    return lax.axis_index("row") % 2, lax.axis_index("core")


def joined():
    row, n_row = lax.axis_index("row"), lax.axis_size("row")
    col, n_col = lax.axis_index(COL), lax.axis_size(COL)
    return (row > 0) & (row < n_row - 1), (col > 0) & (col < n_col - 1)


def live(cond, value):
    return jnp.where(cond, value, jnp.zeros_like(value))


def matmul(a, b):
    return jnp.dot(a, b, preferred_element_type=F32)


def margins_kernel(obj, row_a, edge_b, row_b, col_a, col_b, sems):
    tile = obj.shape[1]
    row_odd, core = place()
    copies = []

    def put(src, dst):
        copies.append(pltpu.make_async_copy(src, dst, sems.at[len(copies)]))
        copies[-1].start()

    rows_b = pl.ds(pl.multiple_of(row_odd * (tile - HALO), HALO), HALO)
    put(obj.at[:, rows_b, 0:HALO], edge_b.at[0:2])
    put(obj.at[:, rows_b, tile - HALO :], edge_b.at[2:4])
    put(obj.at[:, pl.ds(pl.multiple_of((1 - row_odd) * (tile - HALO), HALO), HALO), :], row_a)
    put(obj.at[:, rows_b, HALO : tile - HALO], row_b)
    for col, at in ((col_b, core), (col_a, 1 - core)):
        put(obj.at[:, :, pl.ds(pl.multiple_of(at * (tile - HALO), HALO), HALO)], col)
    for copy in copies:
        copy.wait()


def margins(obj):
    tile = obj.shape[1]
    row = jax.ShapeDtypeStruct((2, HALO, tile), BF16)
    edge = jax.ShapeDtypeStruct((4, HALO, HALO), BF16)
    inside = jax.ShapeDtypeStruct((2, HALO, tile - 2 * HALO), BF16)
    col = jax.ShapeDtypeStruct((2, tile, HALO), BF16)
    return pl.pallas_call(
        margins_kernel,
        out_shape=(row, edge, inside, col, col),
        in_specs=[pl.BlockSpec(memory_space=pltpu.HBM)],
        out_specs=(VM,) * 5,
        scratch_shapes=[pltpu.SemaphoreType.DMA((6,))],
        compiler_params=pltpu.CompilerParams(vmem_limit_bytes=8 * 1024 * 1024),
        name="margins",
    )(pltpu.with_memory_space_constraint(obj, pltpu.HBM))


def corners_kernel(row_a, edge_b, cor_a, cor_b):
    tile = row_a.shape[2]
    core = lax.axis_index("core")

    def emit(cor, side):
        cor[0:2] = row_a[:, :, side * (tile - HALO) : side * (tile - HALO) + HALO]
        cor[2:4] = edge_b[2 * side : 2 * side + 2]

    low, high = 0, 1

    @pl.when(core == 0)
    def _():
        emit(cor_a, high)
        emit(cor_b, low)

    @pl.when(core == 1)
    def _():
        emit(cor_a, low)
        emit(cor_b, high)


def corners(row_a, edge_b):
    shape = jax.ShapeDtypeStruct(edge_b.shape, BF16)
    return pl.pallas_call(
        corners_kernel,
        out_shape=(shape, shape),
        in_specs=[VM, VM],
        out_specs=(VM, VM),
        compiler_params=pltpu.CompilerParams(vmem_limit_bytes=8 * 1024 * 1024),
        name="corners",
    )(row_a, edge_b)


def frames_kernel(
    count_ref, pos_ref, row_a_ref, edge_b_ref, row_b_ref, col_a_ref, col_b_ref, cor_a_ref, cor_b_ref,
    ext_ref, grad_ref, pgrad_ref, probe_ref, amp_ref, tables_ref,
    ext, grad, pgrad, obj_hbm, strip_a_hbm, strip_b_hbm, out_a_hbm, out_b_hbm, keep_out, send,
    patch, waves, chi, firsts, backs, out_a, out_b, sems,
):
    side = probe_ref.shape[-1]
    modes = probe_ref.shape[1]
    tile = col_a_ref.shape[1]
    nblk = tile // LANES
    count = count_ref[0, 0]
    row_odd, core = place()
    row_in, col_in = joined()
    row_a = pl.multiple_of((1 - row_odd) * (HALO + tile), HALO)
    row_b = pl.multiple_of(row_odd * (HALO + tile), HALO)
    col_a = (1 - core) * (nblk + 1)
    col_b = core * (nblk + 1)
    lt_ref, rt_ref = tables_ref.at[0], tables_ref.at[1]
    for c in range(2):
        for b in range(nblk):
            cols = slice(b * LANES, (b + 1) * LANES)
            ext[c, b + 1, pl.ds(row_a, HALO), :] = row_a_ref[c, :, cols].astype(F32)
            if b in (0, nblk - 1):
                part = edge_b_ref[c + 2 * min(b, 1)]
            else:
                part = row_b_ref[c, :, (b - 1) * LANES : b * LANES]
            ext[c, b + 1, pl.ds(row_b, HALO), :] = live(row_in, part.astype(F32))
        ext[c, col_a, pl.ds(row_a, HALO), :] = cor_a_ref[c].astype(F32)
        ext[c, col_a, HALO : HALO + tile, :] = col_a_ref[c].astype(F32)
        ext[c, col_a, pl.ds(row_b, HALO), :] = live(row_in, cor_a_ref[2 + c].astype(F32))
        ext[c, col_b, pl.ds(row_a, HALO), :] = live(col_in, cor_b_ref[c].astype(F32))
        ext[c, col_b, HALO : HALO + tile, :] = live(col_in, col_b_ref[c].astype(F32))
        ext[c, col_b, pl.ds(row_b, HALO), :] = live(row_in & col_in, cor_b_ref[2 + c].astype(F32))
    lane = lax.broadcasted_iota(jnp.int32, (side, LANES), 1)

    def gather(s, slot):
        row = pos_ref[0, 0, 0, s]
        col = pos_ref[0, 0, 1, s]
        cq = col // LANES
        cr = col % LANES
        back_shift = (LANES - cr) % LANES
        keep = lane < LANES - cr
        for c in range(2):
            rolled = [
                pltpu.roll(ext[c, jnp.minimum(cq + j, nblk + 1), pl.ds(row, side), :], back_shift, 1)
                for j in range(side // LANES + 1)
            ]
            for j in range(side // LANES):
                patch[slot, c, :, j * LANES : (j + 1) * LANES] = jnp.where(keep, rolled[j], rolled[j + 1])

    def exits(slot):
        patch_r = patch[slot, 0]
        patch_i = patch[slot, 1]
        for m in range(modes):
            pr = probe_ref[0, m]
            pi = probe_ref[1, m]
            waves[m, 0:side, :] = (pr * patch_r - pi * patch_i).astype(BF16)
            waves[m, side:, :] = (pr * patch_i + pi * patch_r).astype(BF16)

    def left(table, src, dst):
        for m in range(modes):
            f = matmul(table, src[m]).astype(BF16)
            dst[m * side : (m + 1) * side, 0:side] = f[:side]
            dst[m * side : (m + 1) * side, side:] = f[side:]

    def make_chi(s):
        psi = matmul(firsts[...], rt_ref[...])
        psi_r = [psi[m * side : (m + 1) * side, :side] for m in range(modes)]
        psi_i = [psi[m * side : (m + 1) * side, side:] for m in range(modes)]
        power = sum(psi_r[m] * psi_r[m] + psi_i[m] * psi_i[m] for m in range(modes))
        factor = 1.0 - amp_ref[s].astype(F32) * lax.rsqrt(jnp.maximum(power, 0.25))
        for m in range(modes):
            chi[m, 0:side, :] = (psi_r[m] * factor).astype(BF16)
            chi[m, side:, :] = (psi_i[m] * factor).astype(BF16)

    def finish(s, slot, back):
        row = pos_ref[0, 0, 0, s]
        col = pos_ref[0, 0, 1, s]
        cq = col // LANES
        cr = col % LANES
        patch_r = patch[slot, 0]
        patch_i = patch[slot, 1]
        sum_r = jnp.zeros((side, side), F32)
        sum_i = jnp.zeros((side, side), F32)
        for m in range(modes):
            pr = probe_ref[0, m]
            pi = probe_ref[1, m]
            g_r = back[m * side : (m + 1) * side, :side]
            g_i = back[m * side : (m + 1) * side, side:]
            sum_r = sum_r + (pr * g_r + pi * g_i)
            sum_i = sum_i + (pr * g_i - pi * g_r)
            pgrad[0, m] += patch_r * g_r + patch_i * g_i
            pgrad[1, m] += patch_r * g_i - patch_i * g_r
        for c, v in enumerate((sum_r, sum_i)):
            parts = [pltpu.roll(v[:, j * LANES : (j + 1) * LANES], cr, 1) for j in range(side // LANES)]
            for j in range(side // LANES + 1):
                low = parts[j - 1] if j > 0 else jnp.zeros((side, LANES), F32)
                high = parts[j] if j < side // LANES else jnp.zeros((side, LANES), F32)
                grad[c, jnp.minimum(cq + j, nblk + 1), pl.ds(row, side), :] += jnp.where(lane >= cr, high, low)

    gather(0, 0)
    exits(0)
    left(lt_ref[...], waves, firsts)
    make_chi(0)

    def step(s, carry):
        slot = s % 2
        gather(s + 1, 1 - slot)
        left(rt_ref[...], chi, backs)
        exits(1 - slot)
        back = matmul(backs[...], lt_ref[...])
        left(lt_ref[...], waves, firsts)
        finish(s, slot, back)
        make_chi(s + 1)
        return carry

    lax.fori_loop(0, count - 1, step, 0)
    last = count - 1
    left(rt_ref[...], chi, backs)
    finish(last, last % 2, matmul(backs[...], lt_ref[...]))
    copies = []

    def put(src, dst):
        copies.append(pltpu.make_async_copy(src, dst, sems.at[len(copies)]))
        copies[-1].start()

    for c in range(2):
        for b in range(nblk):
            put(grad.at[c, b + 1, HALO : HALO + tile, :], obj_hbm.at[c, :, b * LANES : (b + 1) * LANES])
        put(grad.at[c, 1 : nblk + 1, pl.ds(row_a, HALO), :], strip_a_hbm.at[c])
        put(grad.at[c, 1 : nblk + 1, pl.ds(row_b, HALO), :], strip_b_hbm.at[c])
    for c in range(2):
        out_a[c] = grad[c, col_a].astype(BF16)
        out_b[c] = grad[c, col_b].astype(BF16)
    put(out_a, out_a_hbm)
    put(out_b, out_b_hbm)
    for m in range(modes):
        for i in range(side // CHUNK):
            for j in range(side // LANES):
                k = (m * (side // CHUNK) + i) * (side // LANES) + j
                at = (m, slice(i * CHUNK, (i + 1) * CHUNK), slice(j * LANES, (j + 1) * LANES))
                send[k] = pgrad[(1 - core,) + at].astype(BF16)
                keep_out[k] = pgrad[(core,) + at]
    for copy in copies:
        copy.wait()


def prepare_kernel(mid_hbm, probe_hbm, amp_hbm, tables_hbm, ext, grad, pgrad, probe, amp, tables, mid, sems):
    tile = mid.shape[1]
    copies = [
        pltpu.make_async_copy(src, dst, sems.at[i])
        for i, (src, dst) in enumerate(((mid_hbm, mid), (probe_hbm, probe), (amp_hbm, amp), (tables_hbm, tables)))
    ]
    for copy in copies:
        copy.start()
    grad[...] = jnp.zeros_like(grad)
    pgrad[...] = jnp.zeros_like(pgrad)
    copies[0].wait()
    for c in range(2):
        for b in range(tile // LANES):
            ext[c, b + 1, HALO : HALO + tile, :] = mid[c, :, b * LANES : (b + 1) * LANES].astype(F32)
    for copy in copies[1:]:
        copy.wait()


def prepare(mid, probe, amp, tables):
    tile = mid.shape[1]
    big = pltpu.VMEM((2, tile // LANES + 2, tile + 2 * HALO, LANES), F32)
    hbm = pl.BlockSpec(memory_space=pltpu.HBM)
    return pl.pallas_call(
        prepare_kernel,
        out_shape=(big, big, pltpu.VMEM(probe.shape, F32), pltpu.VMEM(probe.shape, F32), pltpu.VMEM(amp.shape, BF16),
                   pltpu.VMEM(tables.shape, BF16)),
        in_specs=[hbm] * 4,
        out_specs=(VM,) * 6,
        scratch_shapes=[pltpu.VMEM(mid.shape, BF16), pltpu.SemaphoreType.DMA((4,))],
        compiler_params=pltpu.CompilerParams(vmem_limit_bytes=16 * 1024 * 1024),
        cost_estimate=pl.CostEstimate(flops=5000000000, transcendentals=0, bytes_accessed=0),
        name="prepare",
    )(*[pltpu.with_memory_space_constraint(x, pltpu.HBM) for x in (mid, probe, amp, tables)])


def run_frames(count, pos, halo, prepared):
    ext, grad, pgrad, probe, amp, tables = prepared
    side = probe.shape[-1]
    modes = probe.shape[1]
    nblk = ext.shape[1] - 2
    rows = ext.shape[2]
    tile = rows - 2 * HALO
    chunks = modes * side * side // (CHUNK * LANES)
    first = 2 + len(halo)
    return pl.pallas_call(
        frames_kernel,
        out_shape=(
            pltpu.VMEM(ext.shape, F32),
            pltpu.VMEM(grad.shape, F32),
            pltpu.VMEM(pgrad.shape, F32),
            pltpu.HBM((2, tile, tile), F32),
            pltpu.HBM((2, nblk, HALO, LANES), F32),
            pltpu.HBM((2, nblk, HALO, LANES), F32),
            pltpu.HBM((2, rows, LANES), BF16),
            pltpu.HBM((2, rows, LANES), BF16),
            pltpu.VMEM((chunks, CHUNK, LANES), F32),
            pltpu.VMEM((chunks, CHUNK, LANES), BF16),
        ),
        in_specs=[SM, SM] + [VM] * (len(halo) + 6),
        out_specs=(VM,) * 3 + (pl.BlockSpec(memory_space=pltpu.HBM),) * 5 + (VM,) * 2,
        input_output_aliases={first: 0, first + 1: 1, first + 2: 2},
        scratch_shapes=[
            pltpu.VMEM((2, 2, side, side), F32),
            pltpu.VMEM((modes, 2 * side, side), BF16),
            pltpu.VMEM((modes, 2 * side, side), BF16),
            pltpu.VMEM((modes * side, 2 * side), BF16),
            pltpu.VMEM((modes * side, 2 * side), BF16),
            pltpu.VMEM((2, rows, LANES), BF16),
            pltpu.VMEM((2, rows, LANES), BF16),
            pltpu.SemaphoreType.DMA((2 * nblk + 6,)),
        ],
        compiler_params=pltpu.CompilerParams(vmem_limit_bytes=8 * 1024 * 1024),
        name="frames",
    )(count, pos, *halo, *prepared)


def row_margin_kernel(
    strip_a_hbm, strip_b_hbm, got_a_ref, got_b_ref, out_a_ref, out_b_ref, strip_a_ref, strip_b_ref, sem_a, sem_b
):
    nblk, rows = strip_a_ref.shape[1], got_a_ref.shape[1]
    row_odd, core = place()
    _, col_in = joined()
    copy_a = pltpu.make_async_copy(strip_a_hbm, strip_a_ref, sem_a)
    copy_b = pltpu.make_async_copy(strip_b_hbm, strip_b_ref, sem_b)
    copy_a.start()
    copy_b.start()
    copy_a.wait()
    copy_b.wait()

    def emit(own_ref, out_ref, start):
        for c in range(2):
            for b in range(nblk):
                out_ref[c, b] = own_ref[c, b].astype(BF16)
            at = slice(start, start + HALO)
            blk_a, blk_b = (1 - core) * (nblk - 1), core * (nblk - 1)
            out_ref[c, blk_a] = (own_ref[c, blk_a] + got_a_ref[c, at, :].astype(F32)).astype(BF16)
            out_ref[c, blk_b] = (own_ref[c, blk_b] + live(col_in, got_b_ref[c, at, :].astype(F32))).astype(BF16)

    @pl.when(row_odd == 0)
    def _():
        emit(strip_a_ref, out_a_ref, rows - HALO)
        emit(strip_b_ref, out_b_ref, 0)

    @pl.when(row_odd == 1)
    def _():
        emit(strip_a_ref, out_a_ref, 0)
        emit(strip_b_ref, out_b_ref, rows - HALO)


def row_margins(strip_a, strip_b, got_a, got_b):
    shape = jax.ShapeDtypeStruct(strip_a.shape, BF16)
    return pl.pallas_call(
        row_margin_kernel,
        out_shape=(shape, shape),
        in_specs=[pl.BlockSpec(memory_space=pltpu.HBM)] * 2 + [VM] * 2,
        out_specs=(VM, VM),
        scratch_shapes=[
            pltpu.VMEM(strip_a.shape, F32),
            pltpu.VMEM(strip_b.shape, F32),
            pltpu.SemaphoreType.DMA(()),
            pltpu.SemaphoreType.DMA(()),
        ],
        compiler_params=pltpu.CompilerParams(vmem_limit_bytes=16 * 1024 * 1024),
        cost_estimate=pl.CostEstimate(flops=5000000000, transcendentals=0, bytes_accessed=0),
        name="row_margins",
    )(*[pltpu.with_memory_space_constraint(x, pltpu.HBM) for x in (strip_a, strip_b)], got_a, got_b)


def peer_sum_kernel(scale, got_ref, out_ref):
    total = jnp.sum(got_ref[...].astype(F32), axis=0) * scale
    out_ref[...] = jnp.broadcast_to(total.astype(BF16)[None], out_ref.shape)


def peer_sum(got, scale):
    return pl.pallas_call(
        functools.partial(peer_sum_kernel, scale),
        out_shape=jax.ShapeDtypeStruct(got.shape, BF16),
        in_specs=[VM],
        out_specs=VM,
        compiler_params=pltpu.CompilerParams(vmem_limit_bytes=8 * 1024 * 1024),
        cost_estimate=pl.CostEstimate(flops=5000000000, transcendentals=0, bytes_accessed=0),
        name="peer_sum",
    )(got)


def object_kernel(part_hbm, col_a_ref, col_b_ref, row_a_ref, row_b_ref, obj_hbm, acc, in_sems, out_sems):
    nblk, tile = acc.shape[1], acc.shape[2]
    row_odd, core = place()
    row_in, col_in = joined()
    inner = slice(HALO, HALO + tile)
    row_a = pl.multiple_of((1 - row_odd) * (tile - HALO), HALO)
    row_b = pl.multiple_of(row_odd * (tile - HALO), HALO)
    blocks = [(c, b) for c in range(2) for b in range(nblk)]
    fetches, copies = [], []
    for i, (c, b) in enumerate(blocks):
        cols = slice(b * LANES, (b + 1) * LANES)
        fetches.append(pltpu.make_async_copy(part_hbm.at[c, :, cols], acc.at[c, b], in_sems.at[i]))
        copies.append(pltpu.make_async_copy(acc.at[c, b], obj_hbm.at[c, :, cols], out_sems.at[i]))
        fetches[i].start()
    for i, (c, b) in enumerate(blocks):
        fetches[i].wait()
        if b == 0:
            got_a, got_b = col_a_ref[c, inner, :].astype(F32), live(col_in, col_b_ref[c, inner, :].astype(F32))
            acc[c, b] += jnp.where(core == 0, got_b, got_a)
        if b == nblk - 1:
            got_a, got_b = col_a_ref[c, inner, :].astype(F32), live(col_in, col_b_ref[c, inner, :].astype(F32))
            acc[c, b] += jnp.where(core == 0, got_a, got_b)
        acc[c, b, pl.ds(row_a, HALO), :] += row_a_ref[c, b].astype(F32)
        acc[c, b, pl.ds(row_b, HALO), :] += live(row_in, row_b_ref[c, b].astype(F32))
        copies[i].start()
    for copy in copies:
        copy.wait()


def finish_object(part, col_a, col_b, row_a, row_b):
    tile = part.shape[1]
    nblk = part.shape[2] // LANES
    return pl.pallas_call(
        object_kernel,
        out_shape=pltpu.HBM(part.shape, F32),
        in_specs=[pl.BlockSpec(memory_space=pltpu.HBM)] + [VM] * 4,
        out_specs=pl.BlockSpec(memory_space=pltpu.HBM),
        scratch_shapes=[
            pltpu.VMEM((2, nblk, tile, LANES), F32),
            pltpu.SemaphoreType.DMA((2 * nblk,)),
            pltpu.SemaphoreType.DMA((2 * nblk,)),
        ],
        compiler_params=pltpu.CompilerParams(vmem_limit_bytes=8 * 1024 * 1024),
        cost_estimate=pl.CostEstimate(flops=5000000000, transcendentals=0, bytes_accessed=0),
        name="finish_object",
    )(pltpu.with_memory_space_constraint(part, pltpu.HBM), col_a, col_b, row_a, row_b)


def probe_kernel(mine_ref, theirs_ref, out_ref):
    core = lax.axis_index("core")
    modes, side = out_ref.shape[1], out_ref.shape[2]
    for part_ref, at in ((mine_ref, core), (theirs_ref, 1 - core)):
        for m in range(modes):
            for i in range(side // CHUNK):
                for j in range(side // LANES):
                    k = (m * (side // CHUNK) + i) * (side // LANES) + j
                    out_ref[at, m, i * CHUNK : (i + 1) * CHUNK, j * LANES : (j + 1) * LANES] = part_ref[k].astype(F32)


def finish_probe(mine, theirs, shape):
    return pl.pallas_call(
        probe_kernel,
        out_shape=jax.ShapeDtypeStruct(shape, F32),
        in_specs=[VM, VM],
        out_specs=VM,
        compiler_params=pltpu.CompilerParams(vmem_limit_bytes=16 * 1024 * 1024),
        name="finish_probe",
    )(mine, theirs)


def trade(value, axis, phase):
    n_row, n_col = lax.axis_size("row"), lax.axis_size(COL)
    pairs = []
    for r in range(n_row):
        for c in range(n_col):
            if axis == "row":
                at = ((r + phase) ^ 1) - phase
                to = (at, c) if 0 <= at < n_row else (r, c ^ 1)
            else:
                at = ((c + phase) ^ 1) - phase
                to = (r, at) if 0 <= at < n_col else (r ^ 1, c)
            pairs.append((r * n_col + c, to[0] * n_col + to[1]))
    return lax.ppermute(value, ("row",) + COL, pairs)


def shards(object_field, probe_modes, measured_amp, scan_positions, frame_counts):
    slots = measured_amp.shape[2]
    to_row_a, to_edge_b, to_row_b, to_col_a, to_col_b = margins(object_field)
    edge_b = trade(to_edge_b, "row", 1)
    row_a = trade(to_row_a, "row", 0)
    row_b = trade(to_row_b, "row", 1)
    col_b = trade(to_col_b, COL, 1)
    col_a = trade(to_col_a, COL, 0)
    to_cor_a, to_cor_b = corners(row_a, edge_b)
    cor_b = trade(to_cor_b, COL, 1)
    cor_a = trade(to_cor_a, COL, 0)
    prepared = prepare(object_field, probe_modes, measured_amp[0, 0], fourier_tables(probe_modes.shape[-1]))
    _, _, _, part, strip_a, strip_b, out_a, out_b, keep, send = run_frames(
        frame_counts, scan_positions, (row_a, edge_b, row_b, col_a, col_b, cor_a, cor_b), prepared
    )
    scale = 1.0 / math.sqrt(lax.axis_size("row") * lax.axis_size(COL) * slots)
    pair = (keep + trade(send, COL, 0).astype(F32)).astype(BF16)
    got_a = trade(out_a, COL, 0)
    got_b = trade(out_b, COL, 1)
    peers = lax.all_to_all(pair, PEERS, 0, 0, tiled=True)
    rows_a, rows_b = row_margins(strip_a, strip_b, got_a, got_b)
    back_a = trade(rows_a, "row", 0)
    back_b = trade(rows_b, "row", 1)
    peers, rows_a, rows_b = lax.optimization_barrier((peers, rows_a, rows_b))
    mine = lax.all_to_all(peer_sum(peers, scale), PEERS, 0, 0, tiled=True)
    obj = finish_object(part, got_a, got_b, back_a, back_b)
    mine, obj = lax.optimization_barrier((mine, obj))
    return obj, finish_probe(mine, trade(mine, COL, 0), probe_modes.shape)


def solution(mesh):
    n_col = mesh.shape["col"]
    fine = Mesh(mesh.devices.reshape(mesh.shape["row"], n_col // 2, 2), ("row",) + COL)
    in_specs = (
        P(None, "row", COL),
        P(),
        P("row", COL, None, None, None),
        P("row", COL, None, None),
        P("row", COL),
    )
    out_specs = (P(None, "row", COL), P())
    return jax.shard_map(shards, mesh=fine, in_specs=in_specs, out_specs=out_specs, check_vma=False)
```

```python
import functools
import math

import jax
import jax.numpy as jnp
import numpy as np
from jax import lax
from jax.experimental import pallas as pl
from jax.experimental.pallas import tpu as pltpu
from jax.sharding import Mesh
from jax.sharding import PartitionSpec as P

HALO = 128
LANES = 128
CHUNK = 16
BF16 = jnp.bfloat16
F32 = jnp.float32
COL = ("colc", "core")
PEERS = ("row", "colc")
VM = pl.BlockSpec(memory_space=pltpu.VMEM)
SM = pl.BlockSpec(memory_space=pltpu.SMEM)


def fourier_tables(side):
    indices = np.arange(side)
    angles = 2.0 * math.pi / side * (indices[:, None] * indices[None, :] % side)
    real = jnp.asarray((np.cos(angles) / math.sqrt(side)).astype(np.float32)).astype(BF16)
    imag = jnp.asarray((-np.sin(angles) / math.sqrt(side)).astype(np.float32)).astype(BF16)
    return jnp.stack([jnp.block([[real, -imag], [imag, real]]), jnp.block([[real, imag], [-imag, real]])])


def place():
    return lax.axis_index("row") % 2, lax.axis_index("core")


def joined():
    row, n_row = lax.axis_index("row"), lax.axis_size("row")
    col, n_col = lax.axis_index(COL), lax.axis_size(COL)
    return (row > 0) & (row < n_row - 1), (col > 0) & (col < n_col - 1)


def live(cond, value):
    return jnp.where(cond, value, jnp.zeros_like(value))


def matmul(a, b):
    return jnp.dot(a, b, preferred_element_type=F32)


def margins_kernel(obj, row_a, edge_b, row_b, col_a, col_b, sems):
    tile = obj.shape[1]
    row_odd, core = place()
    copies = []

    def put(src, dst):
        copies.append(pltpu.make_async_copy(src, dst, sems.at[len(copies)]))
        copies[-1].start()

    rows_b = pl.ds(pl.multiple_of(row_odd * (tile - HALO), HALO), HALO)
    put(obj.at[:, rows_b, 0:HALO], edge_b.at[0:2])
    put(obj.at[:, rows_b, tile - HALO :], edge_b.at[2:4])
    put(obj.at[:, pl.ds(pl.multiple_of((1 - row_odd) * (tile - HALO), HALO), HALO), :], row_a)
    put(obj.at[:, rows_b, HALO : tile - HALO], row_b)
    for col, at in ((col_b, core), (col_a, 1 - core)):
        put(obj.at[:, :, pl.ds(pl.multiple_of(at * (tile - HALO), HALO), HALO)], col)
    for copy in copies:
        copy.wait()


def margins(obj):
    tile = obj.shape[1]
    row = jax.ShapeDtypeStruct((2, HALO, tile), BF16)
    edge = jax.ShapeDtypeStruct((4, HALO, HALO), BF16)
    inside = jax.ShapeDtypeStruct((2, HALO, tile - 2 * HALO), BF16)
    col = jax.ShapeDtypeStruct((2, tile, HALO), BF16)
    return pl.pallas_call(
        margins_kernel,
        out_shape=(row, edge, inside, col, col),
        in_specs=[pl.BlockSpec(memory_space=pltpu.HBM)],
        out_specs=(VM,) * 5,
        scratch_shapes=[pltpu.SemaphoreType.DMA((6,))],
        compiler_params=pltpu.CompilerParams(vmem_limit_bytes=8 * 1024 * 1024),
        name="margins",
    )(pltpu.with_memory_space_constraint(obj, pltpu.HBM))


def corners_kernel(row_a, edge_b, cor_a, cor_b):
    tile = row_a.shape[2]
    core = lax.axis_index("core")

    def emit(cor, side):
        cor[0:2] = row_a[:, :, side * (tile - HALO) : side * (tile - HALO) + HALO]
        cor[2:4] = edge_b[2 * side : 2 * side + 2]

    low, high = 0, 1

    @pl.when(core == 0)
    def _():
        emit(cor_a, high)
        emit(cor_b, low)

    @pl.when(core == 1)
    def _():
        emit(cor_a, low)
        emit(cor_b, high)


def corners(row_a, edge_b):
    shape = jax.ShapeDtypeStruct(edge_b.shape, BF16)
    return pl.pallas_call(
        corners_kernel,
        out_shape=(shape, shape),
        in_specs=[VM, VM],
        out_specs=(VM, VM),
        compiler_params=pltpu.CompilerParams(vmem_limit_bytes=8 * 1024 * 1024),
        name="corners",
    )(row_a, edge_b)


def frames_kernel(
    count_ref, pos_ref, row_a_ref, edge_b_ref, row_b_ref, col_a_ref, col_b_ref, cor_a_ref, cor_b_ref,
    ext_ref, grad_ref, pgrad_ref, probe_ref, amp_ref, tables_ref,
    ext, grad, pgrad, obj_hbm, strip_a_hbm, strip_b_hbm, out_a_hbm, out_b_hbm, keep_out, send,
    patch, waves, chi, firsts, backs, out_a, out_b, sems,
):
    side = probe_ref.shape[-1]
    modes = probe_ref.shape[1]
    tile = col_a_ref.shape[1]
    nblk = tile // LANES
    count = count_ref[0, 0]
    row_odd, core = place()
    row_in, col_in = joined()
    row_a = pl.multiple_of((1 - row_odd) * (HALO + tile), HALO)
    row_b = pl.multiple_of(row_odd * (HALO + tile), HALO)
    col_a = (1 - core) * (nblk + 1)
    col_b = core * (nblk + 1)
    lt_ref, rt_ref = tables_ref.at[0], tables_ref.at[1]
    for c in range(2):
        for b in range(nblk):
            cols = slice(b * LANES, (b + 1) * LANES)
            ext[c, b + 1, pl.ds(row_a, HALO), :] = row_a_ref[c, :, cols].astype(F32)
            if b in (0, nblk - 1):
                part = edge_b_ref[c + 2 * min(b, 1)]
            else:
                part = row_b_ref[c, :, (b - 1) * LANES : b * LANES]
            ext[c, b + 1, pl.ds(row_b, HALO), :] = live(row_in, part.astype(F32))
        ext[c, col_a, pl.ds(row_a, HALO), :] = cor_a_ref[c].astype(F32)
        ext[c, col_a, HALO : HALO + tile, :] = col_a_ref[c].astype(F32)
        ext[c, col_a, pl.ds(row_b, HALO), :] = live(row_in, cor_a_ref[2 + c].astype(F32))
        ext[c, col_b, pl.ds(row_a, HALO), :] = live(col_in, cor_b_ref[c].astype(F32))
        ext[c, col_b, HALO : HALO + tile, :] = live(col_in, col_b_ref[c].astype(F32))
        ext[c, col_b, pl.ds(row_b, HALO), :] = live(row_in & col_in, cor_b_ref[2 + c].astype(F32))
    lane = lax.broadcasted_iota(jnp.int32, (side, LANES), 1)

    def gather(s, slot):
        row = pos_ref[0, 0, 0, s]
        col = pos_ref[0, 0, 1, s]
        cq = col // LANES
        cr = col % LANES
        back_shift = (LANES - cr) % LANES
        keep = lane < LANES - cr
        for c in range(2):
            rolled = [
                pltpu.roll(ext[c, jnp.minimum(cq + j, nblk + 1), pl.ds(row, side), :], back_shift, 1)
                for j in range(side // LANES + 1)
            ]
            for j in range(side // LANES):
                patch[slot, c, :, j * LANES : (j + 1) * LANES] = jnp.where(keep, rolled[j], rolled[j + 1])

    def exits(slot):
        patch_r = patch[slot, 0]
        patch_i = patch[slot, 1]
        for m in range(modes):
            pr = probe_ref[0, m]
            pi = probe_ref[1, m]
            waves[m, 0:side, :] = (pr * patch_r - pi * patch_i).astype(BF16)
            waves[m, side:, :] = (pr * patch_i + pi * patch_r).astype(BF16)

    def left(table, src, dst):
        for m in range(modes):
            f = matmul(table, src[m]).astype(BF16)
            dst[m * side : (m + 1) * side, 0:side] = f[:side]
            dst[m * side : (m + 1) * side, side:] = f[side:]

    def make_chi(s):
        psi = matmul(firsts[...], rt_ref[...])
        psi_r = [psi[m * side : (m + 1) * side, :side] for m in range(modes)]
        psi_i = [psi[m * side : (m + 1) * side, side:] for m in range(modes)]
        power = sum(psi_r[m] * psi_r[m] + psi_i[m] * psi_i[m] for m in range(modes))
        factor = 1.0 - amp_ref[s].astype(F32) * lax.rsqrt(jnp.maximum(power, 0.25))
        for m in range(modes):
            chi[m, 0:side, :] = (psi_r[m] * factor).astype(BF16)
            chi[m, side:, :] = (psi_i[m] * factor).astype(BF16)

    def finish(s, slot, back):
        row = pos_ref[0, 0, 0, s]
        col = pos_ref[0, 0, 1, s]
        cq = col // LANES
        cr = col % LANES
        patch_r = patch[slot, 0]
        patch_i = patch[slot, 1]
        sum_r = jnp.zeros((side, side), F32)
        sum_i = jnp.zeros((side, side), F32)
        for m in range(modes):
            pr = probe_ref[0, m]
            pi = probe_ref[1, m]
            g_r = back[m * side : (m + 1) * side, :side]
            g_i = back[m * side : (m + 1) * side, side:]
            sum_r = sum_r + (pr * g_r + pi * g_i)
            sum_i = sum_i + (pr * g_i - pi * g_r)
            pgrad[0, m] += patch_r * g_r + patch_i * g_i
            pgrad[1, m] += patch_r * g_i - patch_i * g_r
        for c, v in enumerate((sum_r, sum_i)):
            parts = [pltpu.roll(v[:, j * LANES : (j + 1) * LANES], cr, 1) for j in range(side // LANES)]
            for j in range(side // LANES + 1):
                low = parts[j - 1] if j > 0 else jnp.zeros((side, LANES), F32)
                high = parts[j] if j < side // LANES else jnp.zeros((side, LANES), F32)
                grad[c, jnp.minimum(cq + j, nblk + 1), pl.ds(row, side), :] += jnp.where(lane >= cr, high, low)

    gather(0, 0)
    exits(0)
    left(lt_ref[...], waves, firsts)
    make_chi(0)

    def step(s, carry):
        slot = s % 2
        gather(s + 1, 1 - slot)
        left(rt_ref[...], chi, backs)
        exits(1 - slot)
        back = matmul(backs[...], lt_ref[...])
        left(lt_ref[...], waves, firsts)
        finish(s, slot, back)
        make_chi(s + 1)
        return carry

    lax.fori_loop(0, count - 1, step, 0)
    last = count - 1
    left(rt_ref[...], chi, backs)
    finish(last, last % 2, matmul(backs[...], lt_ref[...]))
    copies = []

    def put(src, dst):
        copies.append(pltpu.make_async_copy(src, dst, sems.at[len(copies)]))
        copies[-1].start()

    for c in range(2):
        for b in range(nblk):
            put(grad.at[c, b + 1, HALO : HALO + tile, :], obj_hbm.at[c, b])
        put(grad.at[c, 1 : nblk + 1, pl.ds(row_a, HALO), :], strip_a_hbm.at[c])
        put(grad.at[c, 1 : nblk + 1, pl.ds(row_b, HALO), :], strip_b_hbm.at[c])
    for c in range(2):
        out_a[c] = grad[c, col_a].astype(BF16)
        out_b[c] = grad[c, col_b].astype(BF16)
    put(out_a, out_a_hbm)
    put(out_b, out_b_hbm)
    for m in range(modes):
        for i in range(side // CHUNK):
            for j in range(side // LANES):
                k = (m * (side // CHUNK) + i) * (side // LANES) + j
                at = (m, slice(i * CHUNK, (i + 1) * CHUNK), slice(j * LANES, (j + 1) * LANES))
                send[k] = pgrad[(1 - core,) + at].astype(BF16)
                keep_out[k] = pgrad[(core,) + at]
    for copy in copies:
        copy.wait()


def prepare_kernel(mid_hbm, probe_hbm, amp_hbm, tables_hbm, ext, grad, pgrad, probe, amp, tables, mid, sems):
    tile = mid.shape[1]
    copies = [
        pltpu.make_async_copy(src, dst, sems.at[i])
        for i, (src, dst) in enumerate(((mid_hbm, mid), (probe_hbm, probe), (amp_hbm, amp), (tables_hbm, tables)))
    ]
    for copy in copies:
        copy.start()
    grad[...] = jnp.zeros_like(grad)
    pgrad[...] = jnp.zeros_like(pgrad)
    copies[0].wait()
    for c in range(2):
        for b in range(tile // LANES):
            ext[c, b + 1, HALO : HALO + tile, :] = mid[c, :, b * LANES : (b + 1) * LANES].astype(F32)
    for copy in copies[1:]:
        copy.wait()


def prepare(mid, probe, amp, tables):
    tile = mid.shape[1]
    big = pltpu.VMEM((2, tile // LANES + 2, tile + 2 * HALO, LANES), F32)
    hbm = pl.BlockSpec(memory_space=pltpu.HBM)
    return pl.pallas_call(
        prepare_kernel,
        out_shape=(big, big, pltpu.VMEM(probe.shape, F32), pltpu.VMEM(probe.shape, F32), pltpu.VMEM(amp.shape, BF16),
                   pltpu.VMEM(tables.shape, BF16)),
        in_specs=[hbm] * 4,
        out_specs=(VM,) * 6,
        scratch_shapes=[pltpu.VMEM(mid.shape, BF16), pltpu.SemaphoreType.DMA((4,))],
        compiler_params=pltpu.CompilerParams(vmem_limit_bytes=16 * 1024 * 1024),
        cost_estimate=pl.CostEstimate(flops=5000000000, transcendentals=0, bytes_accessed=0),
        name="prepare",
    )(*[pltpu.with_memory_space_constraint(x, pltpu.HBM) for x in (mid, probe, amp, tables)])


def run_frames(count, pos, halo, prepared):
    ext, grad, pgrad, probe, amp, tables = prepared
    side = probe.shape[-1]
    modes = probe.shape[1]
    nblk = ext.shape[1] - 2
    rows = ext.shape[2]
    tile = rows - 2 * HALO
    chunks = modes * side * side // (CHUNK * LANES)
    first = 2 + len(halo)
    return pl.pallas_call(
        frames_kernel,
        out_shape=(
            pltpu.VMEM(ext.shape, F32),
            pltpu.VMEM(grad.shape, F32),
            pltpu.VMEM(pgrad.shape, F32),
            pltpu.HBM((2, nblk, tile, LANES), F32),
            pltpu.HBM((2, nblk, HALO, LANES), F32),
            pltpu.HBM((2, nblk, HALO, LANES), F32),
            pltpu.HBM((2, rows, LANES), BF16),
            pltpu.HBM((2, rows, LANES), BF16),
            pltpu.VMEM((chunks, CHUNK, LANES), F32),
            pltpu.VMEM((chunks, CHUNK, LANES), BF16),
        ),
        in_specs=[SM, SM] + [VM] * (len(halo) + 6),
        out_specs=(VM,) * 3 + (pl.BlockSpec(memory_space=pltpu.HBM),) * 5 + (VM,) * 2,
        input_output_aliases={first: 0, first + 1: 1, first + 2: 2},
        scratch_shapes=[
            pltpu.VMEM((2, 2, side, side), F32),
            pltpu.VMEM((modes, 2 * side, side), BF16),
            pltpu.VMEM((modes, 2 * side, side), BF16),
            pltpu.VMEM((modes * side, 2 * side), BF16),
            pltpu.VMEM((modes * side, 2 * side), BF16),
            pltpu.VMEM((2, rows, LANES), BF16),
            pltpu.VMEM((2, rows, LANES), BF16),
            pltpu.SemaphoreType.DMA((2 * nblk + 6,)),
        ],
        compiler_params=pltpu.CompilerParams(vmem_limit_bytes=8 * 1024 * 1024),
        name="frames",
    )(count, pos, *halo, *prepared)


def row_margin_kernel(
    strip_a_hbm, strip_b_hbm, got_a_ref, got_b_ref, out_a_ref, out_b_ref, strip_a_ref, strip_b_ref, sem_a, sem_b
):
    nblk, rows = strip_a_ref.shape[1], got_a_ref.shape[1]
    row_odd, core = place()
    _, col_in = joined()
    copy_a = pltpu.make_async_copy(strip_a_hbm, strip_a_ref, sem_a)
    copy_b = pltpu.make_async_copy(strip_b_hbm, strip_b_ref, sem_b)
    copy_a.start()
    copy_b.start()
    copy_a.wait()
    copy_b.wait()

    def emit(own_ref, out_ref, start):
        for c in range(2):
            for b in range(nblk):
                out_ref[c, b] = own_ref[c, b].astype(BF16)
            at = slice(start, start + HALO)
            blk_a, blk_b = (1 - core) * (nblk - 1), core * (nblk - 1)
            out_ref[c, blk_a] = (own_ref[c, blk_a] + got_a_ref[c, at, :].astype(F32)).astype(BF16)
            out_ref[c, blk_b] = (own_ref[c, blk_b] + live(col_in, got_b_ref[c, at, :].astype(F32))).astype(BF16)

    @pl.when(row_odd == 0)
    def _():
        emit(strip_a_ref, out_a_ref, rows - HALO)
        emit(strip_b_ref, out_b_ref, 0)

    @pl.when(row_odd == 1)
    def _():
        emit(strip_a_ref, out_a_ref, 0)
        emit(strip_b_ref, out_b_ref, rows - HALO)


def row_margins(strip_a, strip_b, got_a, got_b):
    shape = jax.ShapeDtypeStruct(strip_a.shape, BF16)
    return pl.pallas_call(
        row_margin_kernel,
        out_shape=(shape, shape),
        in_specs=[pl.BlockSpec(memory_space=pltpu.HBM)] * 2 + [VM] * 2,
        out_specs=(VM, VM),
        scratch_shapes=[
            pltpu.VMEM(strip_a.shape, F32),
            pltpu.VMEM(strip_b.shape, F32),
            pltpu.SemaphoreType.DMA(()),
            pltpu.SemaphoreType.DMA(()),
        ],
        compiler_params=pltpu.CompilerParams(vmem_limit_bytes=16 * 1024 * 1024),
        cost_estimate=pl.CostEstimate(flops=5000000000, transcendentals=0, bytes_accessed=0),
        name="row_margins",
    )(*[pltpu.with_memory_space_constraint(x, pltpu.HBM) for x in (strip_a, strip_b)], got_a, got_b)


def peer_sum_kernel(scale, got_ref, out_ref):
    total = jnp.sum(got_ref[...].astype(F32), axis=0) * scale
    out_ref[...] = jnp.broadcast_to(total.astype(BF16)[None], out_ref.shape)


def peer_sum(got, scale):
    return pl.pallas_call(
        functools.partial(peer_sum_kernel, scale),
        out_shape=jax.ShapeDtypeStruct(got.shape, BF16),
        in_specs=[VM],
        out_specs=VM,
        compiler_params=pltpu.CompilerParams(vmem_limit_bytes=8 * 1024 * 1024),
        cost_estimate=pl.CostEstimate(flops=5000000000, transcendentals=0, bytes_accessed=0),
        name="peer_sum",
    )(got)


def object_kernel(part_hbm, col_a_ref, col_b_ref, row_a_ref, row_b_ref, obj_hbm, acc, in_sems, out_sems):
    nblk, tile = acc.shape[1], acc.shape[2]
    row_odd, core = place()
    row_in, col_in = joined()
    inner = slice(HALO, HALO + tile)
    row_a = pl.multiple_of((1 - row_odd) * (tile - HALO), HALO)
    row_b = pl.multiple_of(row_odd * (tile - HALO), HALO)
    blocks = [(c, b) for c in range(2) for b in range(nblk)]
    fetches, copies = [], []
    for i, (c, b) in enumerate(blocks):
        cols = slice(b * LANES, (b + 1) * LANES)
        fetches.append(pltpu.make_async_copy(part_hbm.at[c, b], acc.at[c, b], in_sems.at[i]))
        copies.append(pltpu.make_async_copy(acc.at[c, b], obj_hbm.at[c, :, cols], out_sems.at[i]))
        fetches[i].start()
    for i, (c, b) in enumerate(blocks):
        fetches[i].wait()
        if b == 0:
            got_a, got_b = col_a_ref[c, inner, :].astype(F32), live(col_in, col_b_ref[c, inner, :].astype(F32))
            acc[c, b] += jnp.where(core == 0, got_b, got_a)
        if b == nblk - 1:
            got_a, got_b = col_a_ref[c, inner, :].astype(F32), live(col_in, col_b_ref[c, inner, :].astype(F32))
            acc[c, b] += jnp.where(core == 0, got_a, got_b)
        acc[c, b, pl.ds(row_a, HALO), :] += row_a_ref[c, b].astype(F32)
        acc[c, b, pl.ds(row_b, HALO), :] += live(row_in, row_b_ref[c, b].astype(F32))
        copies[i].start()
    for copy in copies:
        copy.wait()


def finish_object(part, col_a, col_b, row_a, row_b):
    nblk, tile = part.shape[1:3]
    return pl.pallas_call(
        object_kernel,
        out_shape=pltpu.HBM((2, tile, nblk * LANES), F32),
        in_specs=[pl.BlockSpec(memory_space=pltpu.HBM)] + [VM] * 4,
        out_specs=pl.BlockSpec(memory_space=pltpu.HBM),
        scratch_shapes=[
            pltpu.VMEM((2, nblk, tile, LANES), F32),
            pltpu.SemaphoreType.DMA((2 * nblk,)),
            pltpu.SemaphoreType.DMA((2 * nblk,)),
        ],
        compiler_params=pltpu.CompilerParams(vmem_limit_bytes=8 * 1024 * 1024),
        cost_estimate=pl.CostEstimate(flops=5000000000, transcendentals=0, bytes_accessed=0),
        name="finish_object",
    )(pltpu.with_memory_space_constraint(part, pltpu.HBM), col_a, col_b, row_a, row_b)


def put_half(part_ref, half):
    modes, side = half.shape[0], half.shape[1]
    for m in range(modes):
        for i in range(side // CHUNK):
            for j in range(side // LANES):
                k = (m * (side // CHUNK) + i) * (side // LANES) + j
                half[m, i * CHUNK : (i + 1) * CHUNK, j * LANES : (j + 1) * LANES] = part_ref[k].astype(F32)


def mine_kernel(part_ref, out_hbm, half, sem):
    put_half(part_ref, half)
    copy = pltpu.make_async_copy(half, out_hbm.at[lax.axis_index("core")], sem)
    copy.start()
    copy.wait()


def theirs_kernel(part_ref, so_far_hbm, out_hbm, half, sem):
    del so_far_hbm
    put_half(part_ref, half)
    copy = pltpu.make_async_copy(half, out_hbm.at[1 - lax.axis_index("core")], sem)
    copy.start()
    copy.wait()


def finish_mine(mine, shape):
    hbm = pl.BlockSpec(memory_space=pltpu.HBM)
    return pl.pallas_call(
        mine_kernel,
        out_shape=pltpu.HBM(shape, F32),
        in_specs=[VM],
        out_specs=hbm,
        scratch_shapes=[pltpu.VMEM(shape[1:], F32), pltpu.SemaphoreType.DMA(())],
        compiler_params=pltpu.CompilerParams(vmem_limit_bytes=8 * 1024 * 1024),
        cost_estimate=pl.CostEstimate(flops=5000000000, transcendentals=0, bytes_accessed=0),
        name="finish_mine",
    )(mine)


def finish_theirs(theirs, so_far):
    hbm = pl.BlockSpec(memory_space=pltpu.HBM)
    return pl.pallas_call(
        theirs_kernel,
        out_shape=pltpu.HBM(so_far.shape, F32),
        in_specs=[VM, hbm],
        out_specs=hbm,
        input_output_aliases={1: 0},
        scratch_shapes=[pltpu.VMEM(so_far.shape[1:], F32), pltpu.SemaphoreType.DMA(())],
        compiler_params=pltpu.CompilerParams(vmem_limit_bytes=8 * 1024 * 1024),
        name="finish_theirs",
    )(theirs, so_far)


def trade(value, axis, phase):
    n_row, n_col = lax.axis_size("row"), lax.axis_size(COL)
    pairs = []
    for r in range(n_row):
        for c in range(n_col):
            if axis == "row":
                at = ((r + phase) ^ 1) - phase
                to = (at, c) if 0 <= at < n_row else (r, c ^ 1)
            else:
                at = ((c + phase) ^ 1) - phase
                to = (r, at) if 0 <= at < n_col else (r ^ 1, c)
            pairs.append((r * n_col + c, to[0] * n_col + to[1]))
    return lax.ppermute(value, ("row",) + COL, pairs)


def shards(object_field, probe_modes, measured_amp, scan_positions, frame_counts):
    slots = measured_amp.shape[2]
    to_row_a, to_edge_b, to_row_b, to_col_a, to_col_b = margins(object_field)
    edge_b = trade(to_edge_b, "row", 1)
    row_a = trade(to_row_a, "row", 0)
    row_b = trade(to_row_b, "row", 1)
    col_b = trade(to_col_b, COL, 1)
    col_a = trade(to_col_a, COL, 0)
    to_cor_a, to_cor_b = corners(row_a, edge_b)
    cor_b = trade(to_cor_b, COL, 1)
    cor_a = trade(to_cor_a, COL, 0)
    prepared = prepare(object_field, probe_modes, measured_amp[0, 0], fourier_tables(probe_modes.shape[-1]))
    _, _, _, part, strip_a, strip_b, out_a, out_b, keep, send = run_frames(
        frame_counts, scan_positions, (row_a, edge_b, row_b, col_a, col_b, cor_a, cor_b), prepared
    )
    scale = 1.0 / math.sqrt(lax.axis_size("row") * lax.axis_size(COL) * slots)
    pair = (keep + trade(send, COL, 0).astype(F32)).astype(BF16)
    got_a = trade(out_a, COL, 0)
    got_b = trade(out_b, COL, 1)
    peers = lax.all_to_all(pair, PEERS, 0, 0, tiled=True)
    rows_a, rows_b = row_margins(strip_a, strip_b, got_a, got_b)
    back_a = trade(rows_a, "row", 0)
    back_b = trade(rows_b, "row", 1)
    peers, rows_a, rows_b = lax.optimization_barrier((peers, rows_a, rows_b))
    mine = lax.all_to_all(peer_sum(peers, scale), PEERS, 0, 0, tiled=True)
    obj = finish_object(part, got_a, got_b, back_a, back_b)
    mine, obj = lax.optimization_barrier((mine, obj))
    theirs = trade(mine, COL, 0)
    return obj, finish_theirs(theirs, finish_mine(mine, probe_modes.shape))


def solution(mesh):
    n_col = mesh.shape["col"]
    fine = Mesh(mesh.devices.reshape(mesh.shape["row"], n_col // 2, 2), ("row",) + COL)
    in_specs = (
        P(None, "row", COL),
        P(),
        P("row", COL, None, None, None),
        P("row", COL, None, None),
        P("row", COL),
    )
    out_specs = (P(None, "row", COL), P())
    return jax.shard_map(shards, mesh=fine, in_specs=in_specs, out_specs=out_specs, check_vma=False)
```

```python
import functools
import math

import jax
import jax.numpy as jnp
import numpy as np
from jax import lax
from jax.experimental import pallas as pl
from jax.experimental.pallas import tpu as pltpu
from jax.sharding import Mesh
from jax.sharding import PartitionSpec as P

HALO = 128
LANES = 128
CHUNK = 16
BF16 = jnp.bfloat16
F32 = jnp.float32
COL = ("colc", "core")
PEERS = ("row", "colc")
VM = pl.BlockSpec(memory_space=pltpu.VMEM)
SM = pl.BlockSpec(memory_space=pltpu.SMEM)


def fourier_tables(side):
    indices = np.arange(side)
    angles = 2.0 * math.pi / side * (indices[:, None] * indices[None, :] % side)
    real = jnp.asarray((np.cos(angles) / math.sqrt(side)).astype(np.float32)).astype(BF16)
    imag = jnp.asarray((-np.sin(angles) / math.sqrt(side)).astype(np.float32)).astype(BF16)
    return jnp.stack([jnp.block([[real, -imag], [imag, real]]), jnp.block([[real, imag], [-imag, real]])])


def place():
    return lax.axis_index("row") % 2, lax.axis_index("core")


def joined():
    row, n_row = lax.axis_index("row"), lax.axis_size("row")
    col, n_col = lax.axis_index(COL), lax.axis_size(COL)
    return (row > 0) & (row < n_row - 1), (col > 0) & (col < n_col - 1)


def live(cond, value):
    return jnp.where(cond, value, jnp.zeros_like(value))


def matmul(a, b):
    return jnp.dot(a, b, preferred_element_type=F32)


def margins_kernel(obj, edge_b, row_a, col_b, col_a, row_b, sems):
    tile = obj.shape[1]
    row_odd, core = place()
    copies = []

    def put(src, dst):
        copies.append(pltpu.make_async_copy(src, dst, sems.at[len(copies)]))
        copies[-1].start()

    rows_b = pl.ds(pl.multiple_of(row_odd * (tile - HALO), HALO), HALO)
    put(obj.at[:, rows_b, 0:HALO], edge_b.at[0:2])
    put(obj.at[:, rows_b, tile - HALO :], edge_b.at[2:4])
    put(obj.at[:, pl.ds(pl.multiple_of((1 - row_odd) * (tile - HALO), HALO), HALO), :], row_a)
    put(obj.at[:, rows_b, HALO : tile - HALO], row_b)
    for col, at in ((col_b, core), (col_a, 1 - core)):
        put(obj.at[:, :, pl.ds(pl.multiple_of(at * (tile - HALO), HALO), HALO)], col)
    for copy in copies:
        copy.wait()


def margins(obj):
    tile = obj.shape[1]
    row = jax.ShapeDtypeStruct((2, HALO, tile), BF16)
    edge = jax.ShapeDtypeStruct((4, HALO, HALO), BF16)
    inside = jax.ShapeDtypeStruct((2, HALO, tile - 2 * HALO), BF16)
    col = jax.ShapeDtypeStruct((2, tile, HALO), BF16)
    return pl.pallas_call(
        margins_kernel,
        out_shape=(edge, row, col, col, inside),
        in_specs=[pl.BlockSpec(memory_space=pltpu.HBM)],
        out_specs=(VM,) * 5,
        scratch_shapes=[pltpu.SemaphoreType.DMA((6,))],
        compiler_params=pltpu.CompilerParams(vmem_limit_bytes=8 * 1024 * 1024),
        name="margins",
    )(pltpu.with_memory_space_constraint(obj, pltpu.HBM))


def corners_kernel(row_a, edge_b, cor_a, cor_b):
    tile = row_a.shape[2]
    core = lax.axis_index("core")

    def emit(cor, side):
        cor[0:2] = row_a[:, :, side * (tile - HALO) : side * (tile - HALO) + HALO]
        cor[2:4] = edge_b[2 * side : 2 * side + 2]

    low, high = 0, 1

    @pl.when(core == 0)
    def _():
        emit(cor_a, high)
        emit(cor_b, low)

    @pl.when(core == 1)
    def _():
        emit(cor_a, low)
        emit(cor_b, high)


def corners(row_a, edge_b):
    shape = jax.ShapeDtypeStruct(edge_b.shape, BF16)
    return pl.pallas_call(
        corners_kernel,
        out_shape=(shape, shape),
        in_specs=[VM, VM],
        out_specs=(VM, VM),
        compiler_params=pltpu.CompilerParams(vmem_limit_bytes=8 * 1024 * 1024),
        name="corners",
    )(row_a, edge_b)


def frames_kernel(
    count_ref, pos_ref, edge_b_ref, row_a_ref, col_b_ref, col_a_ref, row_b_ref, cor_b_ref, cor_a_ref,
    ext_ref, grad_ref, pgrad_ref, probe_ref, amp_ref, tables_ref,
    ext, grad, pgrad, obj_hbm, strip_a_hbm, strip_b_hbm, out_a_hbm, out_b_hbm, keep_out, send,
    patch, waves, chi, firsts, backs, out_a, out_b, sems,
):
    side = probe_ref.shape[-1]
    modes = probe_ref.shape[1]
    tile = col_a_ref.shape[1]
    nblk = tile // LANES
    count = count_ref[0, 0]
    row_odd, core = place()
    row_in, col_in = joined()
    row_a = pl.multiple_of((1 - row_odd) * (HALO + tile), HALO)
    row_b = pl.multiple_of(row_odd * (HALO + tile), HALO)
    col_a = (1 - core) * (nblk + 1)
    col_b = core * (nblk + 1)
    lt_ref, rt_ref = tables_ref.at[0], tables_ref.at[1]
    for c in range(2):
        for b in range(nblk):
            cols = slice(b * LANES, (b + 1) * LANES)
            ext[c, b + 1, pl.ds(row_a, HALO), :] = row_a_ref[c, :, cols].astype(F32)
            if b in (0, nblk - 1):
                part = edge_b_ref[c + 2 * min(b, 1)]
            else:
                part = row_b_ref[c, :, (b - 1) * LANES : b * LANES]
            ext[c, b + 1, pl.ds(row_b, HALO), :] = live(row_in, part.astype(F32))
        ext[c, col_a, pl.ds(row_a, HALO), :] = cor_a_ref[c].astype(F32)
        ext[c, col_a, HALO : HALO + tile, :] = col_a_ref[c].astype(F32)
        ext[c, col_a, pl.ds(row_b, HALO), :] = live(row_in, cor_a_ref[2 + c].astype(F32))
        ext[c, col_b, pl.ds(row_a, HALO), :] = live(col_in, cor_b_ref[c].astype(F32))
        ext[c, col_b, HALO : HALO + tile, :] = live(col_in, col_b_ref[c].astype(F32))
        ext[c, col_b, pl.ds(row_b, HALO), :] = live(row_in & col_in, cor_b_ref[2 + c].astype(F32))
    lane = lax.broadcasted_iota(jnp.int32, (side, LANES), 1)

    def gather(s, slot):
        row = pos_ref[0, 0, 0, s]
        col = pos_ref[0, 0, 1, s]
        cq = col // LANES
        cr = col % LANES
        back_shift = (LANES - cr) % LANES
        keep = lane < LANES - cr
        for c in range(2):
            rolled = [
                pltpu.roll(ext[c, jnp.minimum(cq + j, nblk + 1), pl.ds(row, side), :], back_shift, 1)
                for j in range(side // LANES + 1)
            ]
            for j in range(side // LANES):
                patch[slot, c, :, j * LANES : (j + 1) * LANES] = jnp.where(keep, rolled[j], rolled[j + 1])

    def exits(slot):
        patch_r = patch[slot, 0]
        patch_i = patch[slot, 1]
        for m in range(modes):
            pr = probe_ref[0, m]
            pi = probe_ref[1, m]
            waves[m, 0:side, :] = (pr * patch_r - pi * patch_i).astype(BF16)
            waves[m, side:, :] = (pr * patch_i + pi * patch_r).astype(BF16)

    def left(table, src, dst):
        for m in range(modes):
            f = matmul(table, src[m]).astype(BF16)
            dst[m * side : (m + 1) * side, 0:side] = f[:side]
            dst[m * side : (m + 1) * side, side:] = f[side:]

    def make_chi(s):
        psi = matmul(firsts[...], rt_ref[...])
        psi_r = [psi[m * side : (m + 1) * side, :side] for m in range(modes)]
        psi_i = [psi[m * side : (m + 1) * side, side:] for m in range(modes)]
        power = sum(psi_r[m] * psi_r[m] + psi_i[m] * psi_i[m] for m in range(modes))
        factor = 1.0 - amp_ref[s].astype(F32) * lax.rsqrt(jnp.maximum(power, 0.25))
        for m in range(modes):
            chi[m, 0:side, :] = (psi_r[m] * factor).astype(BF16)
            chi[m, side:, :] = (psi_i[m] * factor).astype(BF16)

    def finish(s, slot, back):
        row = pos_ref[0, 0, 0, s]
        col = pos_ref[0, 0, 1, s]
        cq = col // LANES
        cr = col % LANES
        patch_r = patch[slot, 0]
        patch_i = patch[slot, 1]
        sum_r = jnp.zeros((side, side), F32)
        sum_i = jnp.zeros((side, side), F32)
        for m in range(modes):
            pr = probe_ref[0, m]
            pi = probe_ref[1, m]
            g_r = back[m * side : (m + 1) * side, :side]
            g_i = back[m * side : (m + 1) * side, side:]
            sum_r = sum_r + (pr * g_r + pi * g_i)
            sum_i = sum_i + (pr * g_i - pi * g_r)
            pgrad[0, m] += patch_r * g_r + patch_i * g_i
            pgrad[1, m] += patch_r * g_i - patch_i * g_r
        for c, v in enumerate((sum_r, sum_i)):
            parts = [pltpu.roll(v[:, j * LANES : (j + 1) * LANES], cr, 1) for j in range(side // LANES)]
            for j in range(side // LANES + 1):
                low = parts[j - 1] if j > 0 else jnp.zeros((side, LANES), F32)
                high = parts[j] if j < side // LANES else jnp.zeros((side, LANES), F32)
                grad[c, jnp.minimum(cq + j, nblk + 1), pl.ds(row, side), :] += jnp.where(lane >= cr, high, low)

    gather(0, 0)
    exits(0)
    left(lt_ref[...], waves, firsts)
    make_chi(0)

    def step(s, carry):
        slot = s % 2
        gather(s + 1, 1 - slot)
        left(rt_ref[...], chi, backs)
        exits(1 - slot)
        back = matmul(backs[...], lt_ref[...])
        left(lt_ref[...], waves, firsts)
        finish(s, slot, back)
        make_chi(s + 1)
        return carry

    lax.fori_loop(0, count - 1, step, 0)
    last = count - 1
    left(rt_ref[...], chi, backs)
    finish(last, last % 2, matmul(backs[...], lt_ref[...]))
    copies = []

    def put(src, dst):
        copies.append(pltpu.make_async_copy(src, dst, sems.at[len(copies)]))
        copies[-1].start()

    for c in range(2):
        for b in range(nblk):
            put(grad.at[c, b + 1, HALO : HALO + tile, :], obj_hbm.at[c, b])
        put(grad.at[c, 1 : nblk + 1, pl.ds(row_a, HALO), :], strip_a_hbm.at[c])
        put(grad.at[c, 1 : nblk + 1, pl.ds(row_b, HALO), :], strip_b_hbm.at[c])
    for c in range(2):
        out_a[c] = grad[c, col_a].astype(BF16)
        out_b[c] = grad[c, col_b].astype(BF16)
    put(out_a, out_a_hbm)
    put(out_b, out_b_hbm)
    for m in range(modes):
        for i in range(side // CHUNK):
            for j in range(side // LANES):
                k = (m * (side // CHUNK) + i) * (side // LANES) + j
                at = (m, slice(i * CHUNK, (i + 1) * CHUNK), slice(j * LANES, (j + 1) * LANES))
                send[k] = pgrad[(1 - core,) + at].astype(BF16)
                keep_out[k] = pgrad[(core,) + at]
    for copy in copies:
        copy.wait()


def prepare_kernel(mid_hbm, probe_hbm, amp_hbm, tables_hbm, ext, grad, pgrad, probe, amp, tables, mid, sems):
    tile = mid.shape[1]
    copies = [
        pltpu.make_async_copy(src, dst, sems.at[i])
        for i, (src, dst) in enumerate(((mid_hbm, mid), (probe_hbm, probe), (amp_hbm, amp), (tables_hbm, tables)))
    ]
    for copy in copies:
        copy.start()
    grad[...] = jnp.zeros_like(grad)
    pgrad[...] = jnp.zeros_like(pgrad)
    copies[0].wait()
    for c in range(2):
        for b in range(tile // LANES):
            ext[c, b + 1, HALO : HALO + tile, :] = mid[c, :, b * LANES : (b + 1) * LANES].astype(F32)
    for copy in copies[1:]:
        copy.wait()


def prepare(mid, probe, amp, tables):
    tile = mid.shape[1]
    big = pltpu.VMEM((2, tile // LANES + 2, tile + 2 * HALO, LANES), F32)
    hbm = pl.BlockSpec(memory_space=pltpu.HBM)
    return pl.pallas_call(
        prepare_kernel,
        out_shape=(big, big, pltpu.VMEM(probe.shape, F32), pltpu.VMEM(probe.shape, F32), pltpu.VMEM(amp.shape, BF16),
                   pltpu.VMEM(tables.shape, BF16)),
        in_specs=[hbm] * 4,
        out_specs=(VM,) * 6,
        scratch_shapes=[pltpu.VMEM(mid.shape, BF16), pltpu.SemaphoreType.DMA((4,))],
        compiler_params=pltpu.CompilerParams(vmem_limit_bytes=16 * 1024 * 1024),
        cost_estimate=pl.CostEstimate(flops=5000000000, transcendentals=0, bytes_accessed=0),
        name="prepare",
    )(*[pltpu.with_memory_space_constraint(x, pltpu.HBM) for x in (mid, probe, amp, tables)])


def run_frames(count, pos, halo, prepared):
    ext, grad, pgrad, probe, amp, tables = prepared
    side = probe.shape[-1]
    modes = probe.shape[1]
    nblk = ext.shape[1] - 2
    rows = ext.shape[2]
    tile = rows - 2 * HALO
    chunks = modes * side * side // (CHUNK * LANES)
    first = 2 + len(halo)
    return pl.pallas_call(
        frames_kernel,
        out_shape=(
            pltpu.VMEM(ext.shape, F32),
            pltpu.VMEM(grad.shape, F32),
            pltpu.VMEM(pgrad.shape, F32),
            pltpu.HBM((2, nblk, tile, LANES), F32),
            pltpu.HBM((2, nblk, HALO, LANES), F32),
            pltpu.HBM((2, nblk, HALO, LANES), F32),
            pltpu.HBM((2, rows, LANES), BF16),
            pltpu.HBM((2, rows, LANES), BF16),
            pltpu.VMEM((chunks, CHUNK, LANES), F32),
            pltpu.VMEM((chunks, CHUNK, LANES), BF16),
        ),
        in_specs=[SM, SM] + [VM] * (len(halo) + 6),
        out_specs=(VM,) * 3 + (pl.BlockSpec(memory_space=pltpu.HBM),) * 5 + (VM,) * 2,
        input_output_aliases={first: 0, first + 1: 1, first + 2: 2},
        scratch_shapes=[
            pltpu.VMEM((2, 2, side, side), F32),
            pltpu.VMEM((modes, 2 * side, side), BF16),
            pltpu.VMEM((modes, 2 * side, side), BF16),
            pltpu.VMEM((modes * side, 2 * side), BF16),
            pltpu.VMEM((modes * side, 2 * side), BF16),
            pltpu.VMEM((2, rows, LANES), BF16),
            pltpu.VMEM((2, rows, LANES), BF16),
            pltpu.SemaphoreType.DMA((2 * nblk + 6,)),
        ],
        compiler_params=pltpu.CompilerParams(vmem_limit_bytes=8 * 1024 * 1024),
        name="frames",
    )(count, pos, *halo, *prepared)


def row_margin_kernel(
    strip_a_hbm, strip_b_hbm, got_a_ref, got_b_ref, out_a_ref, out_b_ref, strip_a_ref, strip_b_ref, sem_a, sem_b
):
    nblk, rows = strip_a_ref.shape[1], got_a_ref.shape[1]
    row_odd, core = place()
    _, col_in = joined()
    copy_a = pltpu.make_async_copy(strip_a_hbm, strip_a_ref, sem_a)
    copy_b = pltpu.make_async_copy(strip_b_hbm, strip_b_ref, sem_b)
    copy_a.start()
    copy_b.start()
    copy_a.wait()
    copy_b.wait()

    def emit(own_ref, out_ref, start):
        for c in range(2):
            for b in range(nblk):
                out_ref[c, b] = own_ref[c, b].astype(BF16)
            at = slice(start, start + HALO)
            blk_a, blk_b = (1 - core) * (nblk - 1), core * (nblk - 1)
            out_ref[c, blk_a] = (own_ref[c, blk_a] + got_a_ref[c, at, :].astype(F32)).astype(BF16)
            out_ref[c, blk_b] = (own_ref[c, blk_b] + live(col_in, got_b_ref[c, at, :].astype(F32))).astype(BF16)

    @pl.when(row_odd == 0)
    def _():
        emit(strip_a_ref, out_a_ref, rows - HALO)
        emit(strip_b_ref, out_b_ref, 0)

    @pl.when(row_odd == 1)
    def _():
        emit(strip_a_ref, out_a_ref, 0)
        emit(strip_b_ref, out_b_ref, rows - HALO)


def row_margins(strip_a, strip_b, got_a, got_b):
    shape = jax.ShapeDtypeStruct(strip_a.shape, BF16)
    return pl.pallas_call(
        row_margin_kernel,
        out_shape=(shape, shape),
        in_specs=[pl.BlockSpec(memory_space=pltpu.HBM)] * 2 + [VM] * 2,
        out_specs=(VM, VM),
        scratch_shapes=[
            pltpu.VMEM(strip_a.shape, F32),
            pltpu.VMEM(strip_b.shape, F32),
            pltpu.SemaphoreType.DMA(()),
            pltpu.SemaphoreType.DMA(()),
        ],
        compiler_params=pltpu.CompilerParams(vmem_limit_bytes=16 * 1024 * 1024),
        cost_estimate=pl.CostEstimate(flops=5000000000, transcendentals=0, bytes_accessed=0),
        name="row_margins",
    )(*[pltpu.with_memory_space_constraint(x, pltpu.HBM) for x in (strip_a, strip_b)], got_a, got_b)


def peer_sum_kernel(scale, got_ref, out_ref):
    total = jnp.sum(got_ref[...].astype(F32), axis=0) * scale
    out_ref[...] = jnp.broadcast_to(total.astype(BF16)[None], out_ref.shape)


def peer_sum(got, scale):
    return pl.pallas_call(
        functools.partial(peer_sum_kernel, scale),
        out_shape=jax.ShapeDtypeStruct(got.shape, BF16),
        in_specs=[VM],
        out_specs=VM,
        compiler_params=pltpu.CompilerParams(vmem_limit_bytes=8 * 1024 * 1024),
        cost_estimate=pl.CostEstimate(flops=5000000000, transcendentals=0, bytes_accessed=0),
        name="peer_sum",
    )(got)


def object_kernel(part_hbm, col_a_ref, col_b_ref, row_a_ref, row_b_ref, obj_hbm, acc, in_sems, out_sems):
    nblk, tile = acc.shape[1], acc.shape[2]
    row_odd, core = place()
    row_in, col_in = joined()
    inner = slice(HALO, HALO + tile)
    row_a = pl.multiple_of((1 - row_odd) * (tile - HALO), HALO)
    row_b = pl.multiple_of(row_odd * (tile - HALO), HALO)
    blocks = [(c, b) for c in range(2) for b in range(nblk)]
    fetches, copies = [], []
    for i, (c, b) in enumerate(blocks):
        cols = slice(b * LANES, (b + 1) * LANES)
        fetches.append(pltpu.make_async_copy(part_hbm.at[c, b], acc.at[c, b], in_sems.at[i]))
        copies.append(pltpu.make_async_copy(acc.at[c, b], obj_hbm.at[c, :, cols], out_sems.at[i]))
        fetches[i].start()
    for i, (c, b) in enumerate(blocks):
        fetches[i].wait()
        if b == 0:
            got_a, got_b = col_a_ref[c, inner, :].astype(F32), live(col_in, col_b_ref[c, inner, :].astype(F32))
            acc[c, b] += jnp.where(core == 0, got_b, got_a)
        if b == nblk - 1:
            got_a, got_b = col_a_ref[c, inner, :].astype(F32), live(col_in, col_b_ref[c, inner, :].astype(F32))
            acc[c, b] += jnp.where(core == 0, got_a, got_b)
        acc[c, b, pl.ds(row_a, HALO), :] += row_a_ref[c, b].astype(F32)
        acc[c, b, pl.ds(row_b, HALO), :] += live(row_in, row_b_ref[c, b].astype(F32))
        copies[i].start()
    for copy in copies:
        copy.wait()


def finish_object(part, col_a, col_b, row_a, row_b):
    nblk, tile = part.shape[1:3]
    return pl.pallas_call(
        object_kernel,
        out_shape=pltpu.HBM((2, tile, nblk * LANES), F32),
        in_specs=[pl.BlockSpec(memory_space=pltpu.HBM)] + [VM] * 4,
        out_specs=pl.BlockSpec(memory_space=pltpu.HBM),
        scratch_shapes=[
            pltpu.VMEM((2, nblk, tile, LANES), F32),
            pltpu.SemaphoreType.DMA((2 * nblk,)),
            pltpu.SemaphoreType.DMA((2 * nblk,)),
        ],
        compiler_params=pltpu.CompilerParams(vmem_limit_bytes=8 * 1024 * 1024),
        cost_estimate=pl.CostEstimate(flops=5000000000, transcendentals=0, bytes_accessed=0),
        name="finish_object",
    )(pltpu.with_memory_space_constraint(part, pltpu.HBM), col_a, col_b, row_a, row_b)


def put_half(part_ref, half):
    modes, side = half.shape[0], half.shape[1]
    for m in range(modes):
        for i in range(side // CHUNK):
            for j in range(side // LANES):
                k = (m * (side // CHUNK) + i) * (side // LANES) + j
                half[m, i * CHUNK : (i + 1) * CHUNK, j * LANES : (j + 1) * LANES] = part_ref[k].astype(F32)


def mine_kernel(part_ref, out_hbm, half, sem):
    put_half(part_ref, half)
    copy = pltpu.make_async_copy(half, out_hbm.at[lax.axis_index("core")], sem)
    copy.start()
    copy.wait()


def theirs_kernel(part_ref, so_far_hbm, out_hbm, half, sem):
    del so_far_hbm
    put_half(part_ref, half)
    copy = pltpu.make_async_copy(half, out_hbm.at[1 - lax.axis_index("core")], sem)
    copy.start()
    copy.wait()


def finish_mine(mine, shape):
    hbm = pl.BlockSpec(memory_space=pltpu.HBM)
    return pl.pallas_call(
        mine_kernel,
        out_shape=pltpu.HBM(shape, F32),
        in_specs=[VM],
        out_specs=hbm,
        scratch_shapes=[pltpu.VMEM(shape[1:], F32), pltpu.SemaphoreType.DMA(())],
        compiler_params=pltpu.CompilerParams(vmem_limit_bytes=8 * 1024 * 1024),
        cost_estimate=pl.CostEstimate(flops=5000000000, transcendentals=0, bytes_accessed=0),
        name="finish_mine",
    )(mine)


def finish_theirs(theirs, so_far):
    hbm = pl.BlockSpec(memory_space=pltpu.HBM)
    return pl.pallas_call(
        theirs_kernel,
        out_shape=pltpu.HBM(so_far.shape, F32),
        in_specs=[VM, hbm],
        out_specs=hbm,
        input_output_aliases={1: 0},
        scratch_shapes=[pltpu.VMEM(so_far.shape[1:], F32), pltpu.SemaphoreType.DMA(())],
        compiler_params=pltpu.CompilerParams(vmem_limit_bytes=8 * 1024 * 1024),
        name="finish_theirs",
    )(theirs, so_far)


def trade(value, axis, phase):
    n_row, n_col = lax.axis_size("row"), lax.axis_size(COL)
    pairs = []
    for r in range(n_row):
        for c in range(n_col):
            if axis == "row":
                at = ((r + phase) ^ 1) - phase
                to = (at, c) if 0 <= at < n_row else (r, c ^ 1)
            else:
                at = ((c + phase) ^ 1) - phase
                to = (r, at) if 0 <= at < n_col else (r ^ 1, c)
            pairs.append((r * n_col + c, to[0] * n_col + to[1]))
    return lax.ppermute(value, ("row",) + COL, pairs)


def shards(object_field, probe_modes, measured_amp, scan_positions, frame_counts):
    slots = measured_amp.shape[2]
    to_edge_b, to_row_a, to_col_b, to_col_a, to_row_b = margins(object_field)
    edge_b = trade(to_edge_b, "row", 1)
    row_a = trade(to_row_a, "row", 0)
    col_b = trade(to_col_b, COL, 1)
    col_a = trade(to_col_a, COL, 0)
    to_row_b, col_a = lax.optimization_barrier((to_row_b, col_a))
    row_b = trade(to_row_b, "row", 1)
    to_cor_a, to_cor_b = corners(row_a, edge_b)
    cor_b = trade(to_cor_b, COL, 1)
    cor_a = trade(to_cor_a, COL, 0)
    prepared = prepare(object_field, probe_modes, measured_amp[0, 0], fourier_tables(probe_modes.shape[-1]))
    _, _, _, part, strip_a, strip_b, out_a, out_b, keep, send = run_frames(
        frame_counts, scan_positions, (edge_b, row_a, col_b, col_a, row_b, cor_b, cor_a), prepared
    )
    scale = 1.0 / math.sqrt(lax.axis_size("row") * lax.axis_size(COL) * slots)
    pair = (keep + trade(send, COL, 0).astype(F32)).astype(BF16)
    got_a = trade(out_a, COL, 0)
    got_b = trade(out_b, COL, 1)
    peers = lax.all_to_all(pair, PEERS, 0, 0, tiled=True)
    rows_a, rows_b = row_margins(strip_a, strip_b, got_a, got_b)
    back_a = trade(rows_a, "row", 0)
    back_b = trade(rows_b, "row", 1)
    peers, rows_a, rows_b = lax.optimization_barrier((peers, rows_a, rows_b))
    mine = lax.all_to_all(peer_sum(peers, scale), PEERS, 0, 0, tiled=True)
    obj = finish_object(part, got_a, got_b, back_a, back_b)
    mine, obj = lax.optimization_barrier((mine, obj))
    theirs = trade(mine, COL, 0)
    return obj, finish_theirs(theirs, finish_mine(mine, probe_modes.shape))


def solution(mesh):
    n_col = mesh.shape["col"]
    fine = Mesh(mesh.devices.reshape(mesh.shape["row"], n_col // 2, 2), ("row",) + COL)
    in_specs = (
        P(None, "row", COL),
        P(),
        P("row", COL, None, None, None),
        P("row", COL, None, None),
        P("row", COL),
    )
    out_specs = (P(None, "row", COL), P())
    return jax.shard_map(shards, mesh=fine, in_specs=in_specs, out_specs=out_specs, check_vma=False)
```

```python
import functools
import math

import jax
import jax.numpy as jnp
import numpy as np
from jax import lax
from jax.experimental import pallas as pl
from jax.experimental.pallas import tpu as pltpu
from jax.sharding import Mesh
from jax.sharding import PartitionSpec as P

HALO = 128
LANES = 128
CHUNK = 16
BF16 = jnp.bfloat16
F32 = jnp.float32
COL = ("colc", "core")
PEERS = ("row", "colc")
VM = pl.BlockSpec(memory_space=pltpu.VMEM)
SM = pl.BlockSpec(memory_space=pltpu.SMEM)


def fourier_tables(side):
    indices = np.arange(side)
    angles = 2.0 * math.pi / side * (indices[:, None] * indices[None, :] % side)
    real = jnp.asarray((np.cos(angles) / math.sqrt(side)).astype(np.float32)).astype(BF16)
    imag = jnp.asarray((-np.sin(angles) / math.sqrt(side)).astype(np.float32)).astype(BF16)
    return jnp.stack([jnp.block([[real, -imag], [imag, real]]), jnp.block([[real, imag], [-imag, real]])])


def place():
    return lax.axis_index("row") % 2, lax.axis_index("core")


def joined():
    row, n_row = lax.axis_index("row"), lax.axis_size("row")
    col, n_col = lax.axis_index(COL), lax.axis_size(COL)
    return (row > 0) & (row < n_row - 1), (col > 0) & (col < n_col - 1)


def live(cond, value):
    return jnp.where(cond, value, jnp.zeros_like(value))


def matmul(a, b):
    return jnp.dot(a, b, preferred_element_type=F32)


def cut(pairs, sems):
    copies = [pltpu.make_async_copy(src, dst, sems.at[i]) for i, (src, dst) in enumerate(pairs)]
    for copy in copies:
        copy.start()
    for copy in copies:
        copy.wait()


def start_at(tile, odd):
    return pl.ds(pl.multiple_of(odd * (tile - HALO), HALO), HALO)


def row_margins_kernel(obj, row_a, edge_b, row_b, sems):
    tile = obj.shape[1]
    row_odd = lax.axis_index("row") % 2
    rows = start_at(tile, row_odd)
    cut(
        (
            (obj.at[:, rows, 0:HALO], edge_b.at[0:2]),
            (obj.at[:, rows, tile - HALO :], edge_b.at[2:4]),
            (obj.at[:, rows, HALO : tile - HALO], row_b),
            (obj.at[:, start_at(tile, 1 - row_odd), :], row_a),
        ),
        sems,
    )


def col_margins_kernel(obj, col_a, col_b, sems):
    tile = obj.shape[1]
    core = lax.axis_index("core")
    cut(
        (
            (obj.at[:, :, start_at(tile, core)], col_b),
            (obj.at[:, :, start_at(tile, 1 - core)], col_a),
        ),
        sems,
    )


def margins(kernel, name, obj, *shapes):
    return pl.pallas_call(
        kernel,
        out_shape=tuple(jax.ShapeDtypeStruct(shape, BF16) for shape in shapes),
        in_specs=[pl.BlockSpec(memory_space=pltpu.HBM)],
        out_specs=(VM,) * len(shapes),
        scratch_shapes=[pltpu.SemaphoreType.DMA((4,))],
        compiler_params=pltpu.CompilerParams(vmem_limit_bytes=8 * 1024 * 1024),
        name=name,
    )(pltpu.with_memory_space_constraint(obj, pltpu.HBM))


def corners_kernel(row_a, edge_b, cor_a, cor_b):
    tile = row_a.shape[2]
    core = lax.axis_index("core")

    def emit(cor, side):
        cor[0:2] = row_a[:, :, side * (tile - HALO) : side * (tile - HALO) + HALO]
        cor[2:4] = edge_b[2 * side : 2 * side + 2]

    low, high = 0, 1

    @pl.when(core == 0)
    def _():
        emit(cor_a, high)
        emit(cor_b, low)

    @pl.when(core == 1)
    def _():
        emit(cor_a, low)
        emit(cor_b, high)


def corners(row_a, edge_b):
    shape = jax.ShapeDtypeStruct(edge_b.shape, BF16)
    return pl.pallas_call(
        corners_kernel,
        out_shape=(shape, shape),
        in_specs=[VM, VM],
        out_specs=(VM, VM),
        compiler_params=pltpu.CompilerParams(vmem_limit_bytes=8 * 1024 * 1024),
        name="corners",
    )(row_a, edge_b)


def frames_kernel(
    count_ref, pos_ref, row_a_ref, edge_b_ref, row_b_ref, col_a_ref, col_b_ref, cor_a_ref, cor_b_ref,
    ext_ref, grad_ref, pgrad_ref, probe_ref, amp_ref, tables_ref,
    ext, grad, pgrad, obj_hbm, strip_a_hbm, strip_b_hbm, out_a_hbm, out_b_hbm, keep_out, send,
    patch, waves, chi, firsts, backs, out_a, out_b, sems,
):
    side = probe_ref.shape[-1]
    modes = probe_ref.shape[1]
    tile = col_a_ref.shape[1]
    nblk = tile // LANES
    count = count_ref[0, 0]
    row_odd, core = place()
    row_in, col_in = joined()
    row_a = pl.multiple_of((1 - row_odd) * (HALO + tile), HALO)
    row_b = pl.multiple_of(row_odd * (HALO + tile), HALO)
    col_a = (1 - core) * (nblk + 1)
    col_b = core * (nblk + 1)
    lt_ref, rt_ref = tables_ref.at[0], tables_ref.at[1]
    for c in range(2):
        for b in range(nblk):
            cols = slice(b * LANES, (b + 1) * LANES)
            ext[c, b + 1, pl.ds(row_a, HALO), :] = row_a_ref[c, :, cols].astype(F32)
            if b in (0, nblk - 1):
                part = edge_b_ref[c + 2 * min(b, 1)]
            else:
                part = row_b_ref[c, :, (b - 1) * LANES : b * LANES]
            ext[c, b + 1, pl.ds(row_b, HALO), :] = live(row_in, part.astype(F32))
        ext[c, col_a, pl.ds(row_a, HALO), :] = cor_a_ref[c].astype(F32)
        ext[c, col_a, HALO : HALO + tile, :] = col_a_ref[c].astype(F32)
        ext[c, col_a, pl.ds(row_b, HALO), :] = live(row_in, cor_a_ref[2 + c].astype(F32))
        ext[c, col_b, pl.ds(row_a, HALO), :] = live(col_in, cor_b_ref[c].astype(F32))
        ext[c, col_b, HALO : HALO + tile, :] = live(col_in, col_b_ref[c].astype(F32))
        ext[c, col_b, pl.ds(row_b, HALO), :] = live(row_in & col_in, cor_b_ref[2 + c].astype(F32))
    lane = lax.broadcasted_iota(jnp.int32, (side, LANES), 1)

    def gather(s, slot):
        row = pos_ref[0, 0, 0, s]
        col = pos_ref[0, 0, 1, s]
        cq = col // LANES
        cr = col % LANES
        back_shift = (LANES - cr) % LANES
        keep = lane < LANES - cr
        for c in range(2):
            rolled = [
                pltpu.roll(ext[c, jnp.minimum(cq + j, nblk + 1), pl.ds(row, side), :], back_shift, 1)
                for j in range(side // LANES + 1)
            ]
            for j in range(side // LANES):
                patch[slot, c, :, j * LANES : (j + 1) * LANES] = jnp.where(keep, rolled[j], rolled[j + 1])

    def exits(slot):
        patch_r = patch[slot, 0]
        patch_i = patch[slot, 1]
        for m in range(modes):
            pr = probe_ref[0, m]
            pi = probe_ref[1, m]
            waves[m, 0:side, :] = (pr * patch_r - pi * patch_i).astype(BF16)
            waves[m, side:, :] = (pr * patch_i + pi * patch_r).astype(BF16)

    def left(table, src, dst):
        for m in range(modes):
            f = matmul(table, src[m]).astype(BF16)
            dst[m * side : (m + 1) * side, 0:side] = f[:side]
            dst[m * side : (m + 1) * side, side:] = f[side:]

    def make_chi(s):
        psi = matmul(firsts[...], rt_ref[...])
        psi_r = [psi[m * side : (m + 1) * side, :side] for m in range(modes)]
        psi_i = [psi[m * side : (m + 1) * side, side:] for m in range(modes)]
        power = sum(psi_r[m] * psi_r[m] + psi_i[m] * psi_i[m] for m in range(modes))
        factor = 1.0 - amp_ref[s].astype(F32) * lax.rsqrt(jnp.maximum(power, 0.25))
        for m in range(modes):
            chi[m, 0:side, :] = (psi_r[m] * factor).astype(BF16)
            chi[m, side:, :] = (psi_i[m] * factor).astype(BF16)

    def finish(s, slot, back):
        row = pos_ref[0, 0, 0, s]
        col = pos_ref[0, 0, 1, s]
        cq = col // LANES
        cr = col % LANES
        patch_r = patch[slot, 0]
        patch_i = patch[slot, 1]
        sum_r = jnp.zeros((side, side), F32)
        sum_i = jnp.zeros((side, side), F32)
        for m in range(modes):
            pr = probe_ref[0, m]
            pi = probe_ref[1, m]
            g_r = back[m * side : (m + 1) * side, :side]
            g_i = back[m * side : (m + 1) * side, side:]
            sum_r = sum_r + (pr * g_r + pi * g_i)
            sum_i = sum_i + (pr * g_i - pi * g_r)
            pgrad[0, m] += patch_r * g_r + patch_i * g_i
            pgrad[1, m] += patch_r * g_i - patch_i * g_r
        for c, v in enumerate((sum_r, sum_i)):
            parts = [pltpu.roll(v[:, j * LANES : (j + 1) * LANES], cr, 1) for j in range(side // LANES)]
            for j in range(side // LANES + 1):
                low = parts[j - 1] if j > 0 else jnp.zeros((side, LANES), F32)
                high = parts[j] if j < side // LANES else jnp.zeros((side, LANES), F32)
                grad[c, jnp.minimum(cq + j, nblk + 1), pl.ds(row, side), :] += jnp.where(lane >= cr, high, low)

    gather(0, 0)
    exits(0)
    left(lt_ref[...], waves, firsts)
    make_chi(0)

    def step(s, carry):
        slot = s % 2
        gather(s + 1, 1 - slot)
        left(rt_ref[...], chi, backs)
        exits(1 - slot)
        back = matmul(backs[...], lt_ref[...])
        left(lt_ref[...], waves, firsts)
        finish(s, slot, back)
        make_chi(s + 1)
        return carry

    lax.fori_loop(0, count - 1, step, 0)
    last = count - 1
    left(rt_ref[...], chi, backs)
    finish(last, last % 2, matmul(backs[...], lt_ref[...]))
    copies = []

    def put(src, dst):
        copies.append(pltpu.make_async_copy(src, dst, sems.at[len(copies)]))
        copies[-1].start()

    for c in range(2):
        for b in range(nblk):
            put(grad.at[c, b + 1, HALO : HALO + tile, :], obj_hbm.at[c, b])
        put(grad.at[c, 1 : nblk + 1, pl.ds(row_a, HALO), :], strip_a_hbm.at[c])
        put(grad.at[c, 1 : nblk + 1, pl.ds(row_b, HALO), :], strip_b_hbm.at[c])
    for c in range(2):
        out_a[c] = grad[c, col_a].astype(BF16)
        out_b[c] = grad[c, col_b].astype(BF16)
    put(out_a, out_a_hbm)
    put(out_b, out_b_hbm)
    for m in range(modes):
        for i in range(side // CHUNK):
            for j in range(side // LANES):
                k = (m * (side // CHUNK) + i) * (side // LANES) + j
                at = (m, slice(i * CHUNK, (i + 1) * CHUNK), slice(j * LANES, (j + 1) * LANES))
                send[k] = pgrad[(1 - core,) + at].astype(BF16)
                keep_out[k] = pgrad[(core,) + at]
    for copy in copies:
        copy.wait()


def prepare_kernel(mid_hbm, probe_hbm, amp_hbm, tables_hbm, ext, grad, pgrad, probe, amp, tables, mid, sems):
    tile = mid.shape[1]
    copies = [
        pltpu.make_async_copy(src, dst, sems.at[i])
        for i, (src, dst) in enumerate(((mid_hbm, mid), (probe_hbm, probe), (amp_hbm, amp), (tables_hbm, tables)))
    ]
    for copy in copies:
        copy.start()
    grad[...] = jnp.zeros_like(grad)
    pgrad[...] = jnp.zeros_like(pgrad)
    copies[0].wait()
    for c in range(2):
        for b in range(tile // LANES):
            ext[c, b + 1, HALO : HALO + tile, :] = mid[c, :, b * LANES : (b + 1) * LANES].astype(F32)
    for copy in copies[1:]:
        copy.wait()


def prepare(mid, probe, amp, tables):
    tile = mid.shape[1]
    big = pltpu.VMEM((2, tile // LANES + 2, tile + 2 * HALO, LANES), F32)
    hbm = pl.BlockSpec(memory_space=pltpu.HBM)
    return pl.pallas_call(
        prepare_kernel,
        out_shape=(big, big, pltpu.VMEM(probe.shape, F32), pltpu.VMEM(probe.shape, F32), pltpu.VMEM(amp.shape, BF16),
                   pltpu.VMEM(tables.shape, BF16)),
        in_specs=[hbm] * 4,
        out_specs=(VM,) * 6,
        scratch_shapes=[pltpu.VMEM(mid.shape, BF16), pltpu.SemaphoreType.DMA((4,))],
        compiler_params=pltpu.CompilerParams(vmem_limit_bytes=16 * 1024 * 1024),
        cost_estimate=pl.CostEstimate(flops=5000000000, transcendentals=0, bytes_accessed=0),
        name="prepare",
    )(*[pltpu.with_memory_space_constraint(x, pltpu.HBM) for x in (mid, probe, amp, tables)])


def run_frames(count, pos, halo, prepared):
    ext, grad, pgrad, probe, amp, tables = prepared
    side = probe.shape[-1]
    modes = probe.shape[1]
    nblk = ext.shape[1] - 2
    rows = ext.shape[2]
    tile = rows - 2 * HALO
    chunks = modes * side * side // (CHUNK * LANES)
    first = 2 + len(halo)
    return pl.pallas_call(
        frames_kernel,
        out_shape=(
            pltpu.VMEM(ext.shape, F32),
            pltpu.VMEM(grad.shape, F32),
            pltpu.VMEM(pgrad.shape, F32),
            pltpu.HBM((2, nblk, tile, LANES), F32),
            pltpu.HBM((2, nblk, HALO, LANES), F32),
            pltpu.HBM((2, nblk, HALO, LANES), F32),
            pltpu.HBM((2, rows, LANES), BF16),
            pltpu.HBM((2, rows, LANES), BF16),
            pltpu.VMEM((chunks, CHUNK, LANES), F32),
            pltpu.VMEM((chunks, CHUNK, LANES), BF16),
        ),
        in_specs=[SM, SM] + [VM] * (len(halo) + 6),
        out_specs=(VM,) * 3 + (pl.BlockSpec(memory_space=pltpu.HBM),) * 5 + (VM,) * 2,
        input_output_aliases={first: 0, first + 1: 1, first + 2: 2},
        scratch_shapes=[
            pltpu.VMEM((2, 2, side, side), F32),
            pltpu.VMEM((modes, 2 * side, side), BF16),
            pltpu.VMEM((modes, 2 * side, side), BF16),
            pltpu.VMEM((modes * side, 2 * side), BF16),
            pltpu.VMEM((modes * side, 2 * side), BF16),
            pltpu.VMEM((2, rows, LANES), BF16),
            pltpu.VMEM((2, rows, LANES), BF16),
            pltpu.SemaphoreType.DMA((2 * nblk + 6,)),
        ],
        compiler_params=pltpu.CompilerParams(vmem_limit_bytes=8 * 1024 * 1024),
        name="frames",
    )(count, pos, *halo, *prepared)


def row_margin_kernel(
    strip_a_hbm, strip_b_hbm, got_a_ref, got_b_ref, out_a_ref, out_b_ref, strip_a_ref, strip_b_ref, sem_a, sem_b
):
    nblk, rows = strip_a_ref.shape[1], got_a_ref.shape[1]
    row_odd, core = place()
    _, col_in = joined()
    copy_a = pltpu.make_async_copy(strip_a_hbm, strip_a_ref, sem_a)
    copy_b = pltpu.make_async_copy(strip_b_hbm, strip_b_ref, sem_b)
    copy_a.start()
    copy_b.start()
    copy_a.wait()
    copy_b.wait()

    def emit(own_ref, out_ref, start):
        for c in range(2):
            for b in range(nblk):
                out_ref[c, b] = own_ref[c, b].astype(BF16)
            at = slice(start, start + HALO)
            blk_a, blk_b = (1 - core) * (nblk - 1), core * (nblk - 1)
            out_ref[c, blk_a] = (own_ref[c, blk_a] + got_a_ref[c, at, :].astype(F32)).astype(BF16)
            out_ref[c, blk_b] = (own_ref[c, blk_b] + live(col_in, got_b_ref[c, at, :].astype(F32))).astype(BF16)

    @pl.when(row_odd == 0)
    def _():
        emit(strip_a_ref, out_a_ref, rows - HALO)
        emit(strip_b_ref, out_b_ref, 0)

    @pl.when(row_odd == 1)
    def _():
        emit(strip_a_ref, out_a_ref, 0)
        emit(strip_b_ref, out_b_ref, rows - HALO)


def row_margins(strip_a, strip_b, got_a, got_b):
    shape = jax.ShapeDtypeStruct(strip_a.shape, BF16)
    return pl.pallas_call(
        row_margin_kernel,
        out_shape=(shape, shape),
        in_specs=[pl.BlockSpec(memory_space=pltpu.HBM)] * 2 + [VM] * 2,
        out_specs=(VM, VM),
        scratch_shapes=[
            pltpu.VMEM(strip_a.shape, F32),
            pltpu.VMEM(strip_b.shape, F32),
            pltpu.SemaphoreType.DMA(()),
            pltpu.SemaphoreType.DMA(()),
        ],
        compiler_params=pltpu.CompilerParams(vmem_limit_bytes=16 * 1024 * 1024),
        cost_estimate=pl.CostEstimate(flops=5000000000, transcendentals=0, bytes_accessed=0),
        name="row_margins",
    )(*[pltpu.with_memory_space_constraint(x, pltpu.HBM) for x in (strip_a, strip_b)], got_a, got_b)


def peer_sum_kernel(scale, got_ref, out_ref):
    total = jnp.sum(got_ref[...].astype(F32), axis=0) * scale
    out_ref[...] = jnp.broadcast_to(total.astype(BF16)[None], out_ref.shape)


def peer_sum(got, scale):
    return pl.pallas_call(
        functools.partial(peer_sum_kernel, scale),
        out_shape=jax.ShapeDtypeStruct(got.shape, BF16),
        in_specs=[VM],
        out_specs=VM,
        compiler_params=pltpu.CompilerParams(vmem_limit_bytes=8 * 1024 * 1024),
        cost_estimate=pl.CostEstimate(flops=5000000000, transcendentals=0, bytes_accessed=0),
        name="peer_sum",
    )(got)


def object_kernel(part_hbm, col_a_ref, col_b_ref, row_a_ref, row_b_ref, obj_hbm, acc, in_sems, out_sems):
    nblk, tile = acc.shape[1], acc.shape[2]
    row_odd, core = place()
    row_in, col_in = joined()
    inner = slice(HALO, HALO + tile)
    row_a = pl.multiple_of((1 - row_odd) * (tile - HALO), HALO)
    row_b = pl.multiple_of(row_odd * (tile - HALO), HALO)
    blocks = [(c, b) for c in range(2) for b in range(nblk)]
    fetches, copies = [], []
    for i, (c, b) in enumerate(blocks):
        cols = slice(b * LANES, (b + 1) * LANES)
        fetches.append(pltpu.make_async_copy(part_hbm.at[c, b], acc.at[c, b], in_sems.at[i]))
        copies.append(pltpu.make_async_copy(acc.at[c, b], obj_hbm.at[c, :, cols], out_sems.at[i]))
        fetches[i].start()
    for i, (c, b) in enumerate(blocks):
        fetches[i].wait()
        if b == 0:
            got_a, got_b = col_a_ref[c, inner, :].astype(F32), live(col_in, col_b_ref[c, inner, :].astype(F32))
            acc[c, b] += jnp.where(core == 0, got_b, got_a)
        if b == nblk - 1:
            got_a, got_b = col_a_ref[c, inner, :].astype(F32), live(col_in, col_b_ref[c, inner, :].astype(F32))
            acc[c, b] += jnp.where(core == 0, got_a, got_b)
        acc[c, b, pl.ds(row_a, HALO), :] += row_a_ref[c, b].astype(F32)
        acc[c, b, pl.ds(row_b, HALO), :] += live(row_in, row_b_ref[c, b].astype(F32))
        copies[i].start()
    for copy in copies:
        copy.wait()


def finish_object(part, col_a, col_b, row_a, row_b):
    nblk, tile = part.shape[1:3]
    return pl.pallas_call(
        object_kernel,
        out_shape=pltpu.HBM((2, tile, nblk * LANES), F32),
        in_specs=[pl.BlockSpec(memory_space=pltpu.HBM)] + [VM] * 4,
        out_specs=pl.BlockSpec(memory_space=pltpu.HBM),
        scratch_shapes=[
            pltpu.VMEM((2, nblk, tile, LANES), F32),
            pltpu.SemaphoreType.DMA((2 * nblk,)),
            pltpu.SemaphoreType.DMA((2 * nblk,)),
        ],
        compiler_params=pltpu.CompilerParams(vmem_limit_bytes=8 * 1024 * 1024),
        cost_estimate=pl.CostEstimate(flops=5000000000, transcendentals=0, bytes_accessed=0),
        name="finish_object",
    )(pltpu.with_memory_space_constraint(part, pltpu.HBM), col_a, col_b, row_a, row_b)


def put_half(part_ref, half):
    modes, side = half.shape[0], half.shape[1]
    for m in range(modes):
        for i in range(side // CHUNK):
            for j in range(side // LANES):
                k = (m * (side // CHUNK) + i) * (side // LANES) + j
                half[m, i * CHUNK : (i + 1) * CHUNK, j * LANES : (j + 1) * LANES] = part_ref[k].astype(F32)


def mine_kernel(part_ref, out_hbm, half, sem):
    put_half(part_ref, half)
    copy = pltpu.make_async_copy(half, out_hbm.at[lax.axis_index("core")], sem)
    copy.start()
    copy.wait()


def theirs_kernel(part_ref, so_far_hbm, out_hbm, half, sem):
    del so_far_hbm
    put_half(part_ref, half)
    copy = pltpu.make_async_copy(half, out_hbm.at[1 - lax.axis_index("core")], sem)
    copy.start()
    copy.wait()


def finish_mine(mine, shape):
    hbm = pl.BlockSpec(memory_space=pltpu.HBM)
    return pl.pallas_call(
        mine_kernel,
        out_shape=pltpu.HBM(shape, F32),
        in_specs=[VM],
        out_specs=hbm,
        scratch_shapes=[pltpu.VMEM(shape[1:], F32), pltpu.SemaphoreType.DMA(())],
        compiler_params=pltpu.CompilerParams(vmem_limit_bytes=8 * 1024 * 1024),
        cost_estimate=pl.CostEstimate(flops=5000000000, transcendentals=0, bytes_accessed=0),
        name="finish_mine",
    )(mine)


def finish_theirs(theirs, so_far):
    hbm = pl.BlockSpec(memory_space=pltpu.HBM)
    return pl.pallas_call(
        theirs_kernel,
        out_shape=pltpu.HBM(so_far.shape, F32),
        in_specs=[VM, hbm],
        out_specs=hbm,
        input_output_aliases={1: 0},
        scratch_shapes=[pltpu.VMEM(so_far.shape[1:], F32), pltpu.SemaphoreType.DMA(())],
        compiler_params=pltpu.CompilerParams(vmem_limit_bytes=8 * 1024 * 1024),
        name="finish_theirs",
    )(theirs, so_far)


def trade(value, axis, phase):
    n_row, n_col = lax.axis_size("row"), lax.axis_size(COL)
    pairs = []
    for r in range(n_row):
        for c in range(n_col):
            if axis == "row":
                at = ((r + phase) ^ 1) - phase
                to = (at, c) if 0 <= at < n_row else (r, c ^ 1)
            else:
                at = ((c + phase) ^ 1) - phase
                to = (r, at) if 0 <= at < n_col else (r ^ 1, c)
            pairs.append((r * n_col + c, to[0] * n_col + to[1]))
    return lax.ppermute(value, ("row",) + COL, pairs)


def shards(object_field, probe_modes, measured_amp, scan_positions, frame_counts):
    slots = measured_amp.shape[2]
    tile = object_field.shape[1]
    to_row_a, to_edge_b, to_row_b = margins(
        row_margins_kernel, "halo_rows", object_field, (2, HALO, tile), (4, HALO, HALO), (2, HALO, tile - 2 * HALO)
    )
    rest, to_row_a, to_edge_b, to_row_b = lax.optimization_barrier((object_field, to_row_a, to_edge_b, to_row_b))
    to_col_a, to_col_b = margins(col_margins_kernel, "halo_cols", rest, (2, tile, HALO), (2, tile, HALO))
    edge_b = trade(to_edge_b, "row", 1)
    row_a = trade(to_row_a, "row", 0)
    row_b = trade(to_row_b, "row", 1)
    col_b = trade(to_col_b, COL, 1)
    col_a = trade(to_col_a, COL, 0)
    to_cor_a, to_cor_b = corners(row_a, edge_b)
    cor_b = trade(to_cor_b, COL, 1)
    cor_a = trade(to_cor_a, COL, 0)
    prepared = prepare(object_field, probe_modes, measured_amp[0, 0], fourier_tables(probe_modes.shape[-1]))
    _, _, _, part, strip_a, strip_b, out_a, out_b, keep, send = run_frames(
        frame_counts, scan_positions, (row_a, edge_b, row_b, col_a, col_b, cor_a, cor_b), prepared
    )
    scale = 1.0 / math.sqrt(lax.axis_size("row") * lax.axis_size(COL) * slots)
    pair = (keep + trade(send, COL, 0).astype(F32)).astype(BF16)
    got_a = trade(out_a, COL, 0)
    got_b = trade(out_b, COL, 1)
    peers = lax.all_to_all(pair, PEERS, 0, 0, tiled=True)
    rows_a, rows_b = row_margins(strip_a, strip_b, got_a, got_b)
    back_a = trade(rows_a, "row", 0)
    back_b = trade(rows_b, "row", 1)
    peers, rows_a, rows_b = lax.optimization_barrier((peers, rows_a, rows_b))
    mine = lax.all_to_all(peer_sum(peers, scale), PEERS, 0, 0, tiled=True)
    obj = finish_object(part, got_a, got_b, back_a, back_b)
    mine, obj = lax.optimization_barrier((mine, obj))
    theirs = trade(mine, COL, 0)
    return obj, finish_theirs(theirs, finish_mine(mine, probe_modes.shape))


def solution(mesh):
    n_col = mesh.shape["col"]
    fine = Mesh(mesh.devices.reshape(mesh.shape["row"], n_col // 2, 2), ("row",) + COL)
    in_specs = (
        P(None, "row", COL),
        P(),
        P("row", COL, None, None, None),
        P("row", COL, None, None),
        P("row", COL),
    )
    out_specs = (P(None, "row", COL), P())
    return jax.shard_map(shards, mesh=fine, in_specs=in_specs, out_specs=out_specs, check_vma=False)
```
